32 devices in a mesh: seq: 4 (over z), fsdp: 8 (over y, x, core).
Axes of the slice: x: 2, y: 2, z: 4, core: 2. Of those that a mesh axis runs over, the one named last changes fastest.
Arguments:
- tokens: bfloat16 [8, 1024, 768], P('fsdp', 'seq'), may hold values from -12 to 12
- cotangent: bfloat16 [8, 1024, 768], P('fsdp', 'seq'), may hold values from -6 to 6
- lengths: int32 [8], P('fsdp'), may hold values from 128 to 1024, as said below
- w_attn: float32 [4, 768, 768], P(None, 'fsdp', 'seq'), may hold values from -0.8660254 to 0.8660254
- attn_first: float32 [4, 768, 768], P(None, 'fsdp', 'seq'), may hold values from -0.3 to 0.3
- attn_second: float32 [4, 768, 768], P(None, 'fsdp', 'seq'), may hold values from 1e-06 to 0.0001
- w_ffn: float32 [2, 768, 3072], P(None, 'fsdp', 'seq'), may hold values from -0.21650635 to 0.21650635
- ffn_first: float32 [2, 768, 3072], P(None, 'fsdp', 'seq'), may hold values from -0.3 to 0.3
- ffn_second: float32 [2, 768, 3072], P(None, 'fsdp', 'seq'), may hold values from 1e-06 to 0.0001
- vectors: float32 [12, 768], P(None, ('seq', 'fsdp')), may hold values from -1 to 1.5
- vec_first: float32 [12, 768], P(None, ('seq', 'fsdp')), may hold values from -0.3 to 0.3
- vec_second: float32 [12, 768], P(None, ('seq', 'fsdp')), may hold values from 1e-06 to 0.0001
Outputs:
- block_out: bfloat16 [8, 1024, 768], P('fsdp', 'seq')
- input_grad: float32 [8, 1024, 768], P('fsdp', 'seq')
- grad_attn: float32 [4, 768, 768], P(None, 'fsdp', 'seq')
- grad_ffn: float32 [2, 768, 3072], P(None, 'fsdp', 'seq')
- grad_vec: float32 [12, 768], P(None, ('seq', 'fsdp'))
- attn_new: float32 [4, 768, 768], P(None, 'fsdp', 'seq')
- attn_first_new: float32 [4, 768, 768], P(None, 'fsdp', 'seq')
- attn_second_new: float32 [4, 768, 768], P(None, 'fsdp', 'seq')
- ffn_new: float32 [2, 768, 3072], P(None, 'fsdp', 'seq')
- ffn_first_new: float32 [2, 768, 3072], P(None, 'fsdp', 'seq')
- ffn_second_new: float32 [2, 768, 3072], P(None, 'fsdp', 'seq')
- vec_new: float32 [12, 768], P(None, ('seq', 'fsdp'))
- vec_first_new: float32 [12, 768], P(None, ('seq', 'fsdp'))
- vec_second_new: float32 [12, 768], P(None, ('seq', 'fsdp'))
The draws below stay inside these ranges and needn't reach their ends.
Inputs may be any that keep to these rules, and one draw needn't show every extreme that they name: `lengths`: in every draw one sequence has all 1024 tokens valid and one has 128.
All inputs are finite; a program needn't handle non-finite values.
Results may differ from the reference program's by a relative error of at most 0.011.
The reference program's roundings to bfloat16 on the way count: a program that leaves them out, or rounds other values in their place, can miss the bound.
Values may be sent and summed in bfloat16 or wider, within the bound.
No kernel may reach another device: no remote copies, remote signals or barrier semaphores. Data moves between devices by JAX's collectives and lax.ppermute only.
A program may use at most 128 MiB of HBM per device.

```python
import math
import jax
import jax.numpy as jnp
from jax import lax

D = 768
HEAD = 64
FF = 3072
LENGTH = 1024
STEP = 3
SEQS = 8
TOKENS = 8192


def draw_tokens(key, part):
    base_key = jax.random.fold_in(jax.random.fold_in(key, 11), 0)
    normal_part = jnp.clip(jax.random.normal(base_key, (SEQS, LENGTH, D), jnp.float32), -6.0, 6.0)
    return normal_part.astype(jnp.bfloat16)


def draw_lengths(key, part):
    draw_key, order_key = jax.random.split(jax.random.fold_in(key, 23))
    drawn = jax.random.randint(draw_key, (SEQS,), LENGTH // 8, LENGTH + 1, dtype=jnp.int32)
    order = jax.random.permutation(order_key, SEQS)
    drawn = drawn.at[order[0]].set(LENGTH)
    drawn = drawn.at[order[1]].set(LENGTH // 8)
    return drawn.astype(jnp.int32)


def draw_w_attn(key, part):
    normal_part = jnp.clip(jax.random.normal(jax.random.fold_in(key, 31), (4, D, D), jnp.float32), -6.0, 6.0)
    block = jnp.arange(4, dtype=jnp.int32)[:, None, None]
    factor = jnp.where(block < 3, 1.0, 4.0) / math.sqrt(D)
    return (normal_part * factor).astype(jnp.float32)


def draw_w_ffn(key, part):
    normal_part = jnp.clip(jax.random.normal(jax.random.fold_in(key, 37), (2, D, FF), jnp.float32), -6.0, 6.0)
    slab = jnp.arange(2, dtype=jnp.int32)[:, None, None]
    factor = jnp.where(slab == 0, 1.0 / math.sqrt(D), 1.0 / math.sqrt(FF))
    return (normal_part * factor).astype(jnp.float32)


def draw_vectors(key, part):
    uniform_part = jax.random.uniform(jax.random.fold_in(key, 41), (12, D), jnp.float32, -1.0, 1.0)
    row_index = jnp.arange(12, dtype=jnp.int32)[:, None]
    is_gain = (row_index == 4) | (row_index == 6)
    return jnp.where(is_gain, 1.0 + 0.5 * uniform_part, uniform_part).astype(jnp.float32)


def shard_levels(stream_key, extent, shards, low, top_value):
    level = 1.0
    for dim, shards_of in shards:
        steps = jax.random.uniform(jax.random.fold_in(jax.random.fold_in(stream_key, 6), dim), (shards_of,), jnp.float32, low / len(shards), top_value / len(shards))
        level = level * jnp.repeat(jnp.exp(steps), extent[dim] // shards_of).reshape((-1,) + (1,) * (len(extent) - 1 - dim))
    return level


def gaussian(own_key, extent, scale, limit, cuts=(), kind=jnp.bfloat16):
    entries = jax.random.normal(own_key, extent, jnp.float32) * scale
    if len(cuts) > 0:
        entries = shard_levels(own_key, extent, cuts, -0.22, 0.18) * entries
    return jnp.clip(entries, min=-limit, max=limit).astype(kind)


def setup_inputs(seed: int = 0) -> dict:
    keys = jax.random.split(jax.random.key(seed), 13)
    return {
        "tokens": draw_tokens(jax.random.fold_in(keys[12], 71), 0),
        "cotangent": gaussian(keys[1], (SEQS, LENGTH, D), 1.0, 6.0, ((0, 8), (1, 4))),
        "lengths": draw_lengths(jax.random.fold_in(keys[12], 71), 0),
        "w_attn": draw_w_attn(jax.random.fold_in(keys[12], 71), 0),
        "attn_first": gaussian(keys[4], (4, D, D), 0.05, 0.3, ((1, 8), (2, 4)), jnp.float32),
        "attn_second": jnp.clip(jnp.exp(math.log(0.0001) - 4.6051702 * jax.random.uniform(keys[5], (4, D, D), jnp.float32) ** shard_levels(keys[5], (4, D, D), ((1, 8), (2, 4)), -0.2, 0.2)), 9.999999974752427e-07, 0.0001),
        "w_ffn": draw_w_ffn(jax.random.fold_in(keys[12], 71), 0),
        "ffn_first": gaussian(keys[7], (2, D, FF), 0.05, 0.3, ((1, 8), (2, 4)), jnp.float32),
        "ffn_second": jnp.clip(jnp.exp(math.log(0.0001) - 4.6051702 * jax.random.uniform(keys[8], (2, D, FF), jnp.float32) ** shard_levels(keys[8], (2, D, FF), ((1, 8), (2, 4)), -0.2, 0.2)), 9.999999974752427e-07, 0.0001),
        "vectors": draw_vectors(jax.random.fold_in(keys[12], 71), 0),
        "vec_first": gaussian(keys[10], (12, D), 0.05, 0.3, ((1, 32),), jnp.float32),
        "vec_second": jnp.clip(jnp.exp(math.log(0.0001) - 4.6051702 * jax.random.uniform(keys[11], (12, D), jnp.float32) ** shard_levels(keys[11], (12, D), ((1, 32),), -0.2, 0.2)), 9.999999974752427e-07, 0.0001),
    }


EPS_NORM = 1e-12
ADAM_RATE = 0.005
BETA_ONE = 0.9
BETA_TWO = 0.999
ADAM_EPS = 1e-08
WEIGHT_DECAY = 0.01

def widen(values):
    return lax.optimization_barrier(values).astype(jnp.float32)

def layer_norm(values):
    center = values - lax.optimization_barrier(jnp.mean(values, axis=-1, keepdims=True))
    inv_scale = lax.rsqrt(lax.optimization_barrier(jnp.mean(center * center, axis=-1, keepdims=True)) + EPS_NORM)
    return (center * inv_scale, inv_scale)

def norm_back(grad_normed, normed, inv_scale):
    return inv_scale * (grad_normed - lax.optimization_barrier(jnp.mean(grad_normed, axis=-1, keepdims=True)) - normed * lax.optimization_barrier(jnp.mean(grad_normed * normed, axis=-1, keepdims=True)))

def gelu_pair(preact):
    normal_cdf = 0.5 * (1.0 + jax.scipy.special.erf(preact * (1.0 / math.sqrt(2.0))))
    density = jnp.exp(-0.5 * preact * preact) * (1.0 / math.sqrt(2.0 * math.pi))
    return (preact * normal_cdf, normal_cdf + preact * density)

def head_scores(queries, keys_all, valid_len, head_size):
    row_count = queries.shape[0]
    query_heads = widen(queries.reshape(row_count, -1, head_size))
    key_heads = widen(keys_all.reshape(row_count, -1, head_size))
    scores = jnp.einsum('qhd,khd->hqk', query_heads, key_heads, precision=lax.Precision.HIGHEST)
    scores = scores * (1.0 / math.sqrt(head_size))
    position = jnp.arange(row_count, dtype=jnp.int32)
    return jnp.where(position[None, None, :] < valid_len, scores, -jnp.inf)

def attention_forward(queries, keys_all, values_all, valid_len, head_size):
    row_count = queries.shape[0]
    scores = head_scores(queries, keys_all, valid_len, head_size)
    log_total = jax.nn.logsumexp(scores, axis=-1)
    attn_probs = jnp.exp(scores - log_total[:, :, None]).astype(jnp.bfloat16)
    value_heads = widen(values_all.reshape(row_count, -1, head_size))
    attn_mixed = jnp.einsum('hqk,khd->qhd', widen(attn_probs), value_heads, precision=lax.Precision.HIGHEST)
    return (attn_mixed.reshape(row_count, -1).astype(jnp.bfloat16), log_total)

def attention_backward(queries, keys_all, values_all, attn_mixed, grad_mixed, log_total, valid_len, head_size):
    row_count = queries.shape[0]
    scale_attn = 1.0 / math.sqrt(head_size)
    scores = head_scores(queries, keys_all, valid_len, head_size)
    probs_full = jnp.exp(scores - log_total[:, :, None])
    attn_probs = probs_full.astype(jnp.bfloat16)
    query_heads = widen(queries.reshape(row_count, -1, head_size))
    key_heads = widen(keys_all.reshape(row_count, -1, head_size))
    value_heads = widen(values_all.reshape(row_count, -1, head_size))
    grad_heads = widen(grad_mixed.reshape(row_count, -1, head_size))
    mixed_heads = widen(attn_mixed.reshape(row_count, -1, head_size))
    row_delta = lax.optimization_barrier(jnp.sum(grad_heads * mixed_heads, axis=-1)).T
    grad_probs = jnp.einsum('qhd,khd->hqk', grad_heads, value_heads, precision=lax.Precision.HIGHEST)
    grad_scores = (probs_full * (grad_probs - row_delta[:, :, None])).astype(jnp.bfloat16)
    grad_wide = widen(grad_scores)
    grad_query = (jnp.einsum('hqk,khd->qhd', grad_wide, key_heads, precision=lax.Precision.HIGHEST) * scale_attn).astype(jnp.bfloat16)
    grad_key = (jnp.einsum('hqk,qhd->khd', grad_wide, query_heads, precision=lax.Precision.HIGHEST) * scale_attn).astype(jnp.bfloat16)
    grad_value = jnp.einsum('hqk,qhd->khd', widen(attn_probs), grad_heads, precision=lax.Precision.HIGHEST).astype(jnp.bfloat16)
    return (grad_query.reshape(row_count, -1), grad_key.reshape(row_count, -1), grad_value.reshape(row_count, -1))

def adam_step(parameter, gradient, moment_one, moment_two, decay_rate):
    one_new = BETA_ONE * moment_one + (1.0 - BETA_ONE) * gradient
    two_new = BETA_TWO * moment_two + (1.0 - BETA_TWO) * gradient * gradient
    one_hat = one_new / (1.0 - BETA_ONE ** STEP)
    two_hat = two_new / (1.0 - BETA_TWO ** STEP)
    update = one_hat / (jnp.sqrt(two_hat) + ADAM_EPS)
    return (parameter - ADAM_RATE * (update + decay_rate * parameter), one_new, two_new)

def reference(tokens, cotangent, lengths, w_attn, attn_first, attn_second, w_ffn, ffn_first, ffn_second, vectors, vec_first, vec_second):
    attn_w = w_attn.astype(jnp.bfloat16)
    ffn_w = w_ffn.astype(jnp.bfloat16)
    vec_wide = widen(vectors.astype(jnp.bfloat16))
    model_width = D
    w_qkv = jnp.concatenate([attn_w[0], attn_w[1], attn_w[2]], axis=1)
    out_t = attn_w[3]
    zero_bias = jnp.zeros((model_width,), jnp.float32)
    bias_qkv = jnp.concatenate([vec_wide[0], zero_bias, vec_wide[1]])
    up_bias = vec_wide[8:12].reshape(-1)

    def one_sequence(totals, packed):
        token_rows, cot_seq, valid_len = packed
        qkv_rows = (jnp.dot(token_rows, w_qkv, preferred_element_type=jnp.float32) + bias_qkv).astype(jnp.bfloat16)
        queries = qkv_rows[:, :model_width]
        keys_all = qkv_rows[:, model_width:2 * model_width]
        values_all = qkv_rows[:, 2 * model_width:]
        attn_mixed, log_total = attention_forward(queries, keys_all, values_all, valid_len, HEAD)
        hidden_one = token_rows.astype(jnp.float32) + jnp.dot(attn_mixed, out_t.T, preferred_element_type=jnp.float32) + vec_wide[2]
        normed_one, inv_one = layer_norm(hidden_one)
        resid_one = normed_one * vec_wide[4] + vec_wide[5]
        resid_half = resid_one.astype(jnp.bfloat16)
        preact = jnp.dot(resid_half, ffn_w[0], preferred_element_type=jnp.float32) + up_bias
        activation, gelu_slope = gelu_pair(preact)
        act_half = activation.astype(jnp.bfloat16)
        hidden_two = resid_one + jnp.dot(act_half, ffn_w[1].T, preferred_element_type=jnp.float32) + vec_wide[3]
        normed_two, inv_two = layer_norm(hidden_two)
        block_seq = (normed_two * vec_wide[6] + vec_wide[7]).astype(jnp.bfloat16)
        cot_rows = cot_seq.astype(jnp.float32)
        grad_two = norm_back(cot_rows * vec_wide[6], normed_two, inv_two)
        grad_two_half = grad_two.astype(jnp.bfloat16)
        grad_pre = jnp.dot(grad_two_half, ffn_w[1], preferred_element_type=jnp.float32) * gelu_slope
        grad_pre_half = grad_pre.astype(jnp.bfloat16)
        grad_resid = grad_two + jnp.dot(grad_pre_half, ffn_w[0].T, preferred_element_type=jnp.float32)
        grad_one = norm_back(grad_resid * vec_wide[4], normed_one, inv_one)
        grad_one_half = grad_one.astype(jnp.bfloat16)
        grad_mixed = jnp.dot(grad_one_half, out_t, preferred_element_type=jnp.float32).astype(jnp.bfloat16)
        grad_query, grad_key, grad_value = attention_backward(queries, keys_all, values_all, attn_mixed, grad_mixed, log_total, valid_len, HEAD)
        grad_qkv = jnp.concatenate([grad_query, grad_key, grad_value], axis=1)
        grad_input = grad_one + jnp.dot(grad_qkv, w_qkv.T, preferred_element_type=jnp.float32)
        qkv_part = jnp.dot(token_rows.T, grad_qkv, preferred_element_type=jnp.float32)
        attn_part = jnp.stack([qkv_part[:, :model_width], qkv_part[:, model_width:2 * model_width], qkv_part[:, 2 * model_width:], jnp.dot(grad_one_half.T, attn_mixed, preferred_element_type=jnp.float32)])
        ffn_part = jnp.stack([jnp.dot(resid_half.T, grad_pre_half, preferred_element_type=jnp.float32), jnp.dot(grad_two_half.T, act_half, preferred_element_type=jnp.float32)])
        qkv_sums = lax.optimization_barrier(jnp.sum(grad_qkv.astype(jnp.float32), axis=0))
        vec_part = jnp.concatenate([jnp.stack([qkv_sums[:model_width], qkv_sums[2 * model_width:], lax.optimization_barrier(jnp.sum(grad_one, axis=0)), lax.optimization_barrier(jnp.sum(grad_two, axis=0)), lax.optimization_barrier(jnp.sum(grad_resid * normed_one, axis=0)), lax.optimization_barrier(jnp.sum(grad_resid, axis=0)), lax.optimization_barrier(jnp.sum(cot_rows * normed_two, axis=0)), lax.optimization_barrier(jnp.sum(cot_rows, axis=0))]), lax.optimization_barrier(jnp.sum(grad_pre, axis=0)).reshape(4, model_width)], axis=0)
        return ((totals[0] + attn_part, totals[1] + ffn_part, totals[2] + vec_part), (block_seq, grad_input))
    start = (jnp.zeros((4, D, D), jnp.float32), jnp.zeros((2, D, FF), jnp.float32), jnp.zeros((12, D), jnp.float32))
    sums, outputs = lax.scan(one_sequence, start, (tokens, cotangent, lengths.astype(jnp.int32)))
    block_all, input_all = outputs
    grad_scale = float(TOKENS) ** (-0.5)
    attn_grad = sums[0] * grad_scale
    ffn_grad = sums[1] * grad_scale
    vec_grad = sums[2] * grad_scale
    attn_new, attn_one, attn_two = adam_step(w_attn, attn_grad, attn_first, attn_second, WEIGHT_DECAY)
    ffn_new, ffn_one, ffn_two = adam_step(w_ffn, ffn_grad, ffn_first, ffn_second, WEIGHT_DECAY)
    vec_new, vec_one, vec_two = adam_step(vectors, vec_grad, vec_first, vec_second, 0.0)
    return (block_all, input_all, attn_grad, ffn_grad, vec_grad, attn_new, attn_one, attn_two, ffn_new, ffn_one, ffn_two, vec_new, vec_one, vec_two)
```

```python
import math

import jax
import jax.numpy as jnp
from jax import lax
from jax.sharding import PartitionSpec as P

HEAD = 64
STEP = 3


EPS_NORM = 1e-12
ADAM_RATE = 0.005
BETA_ONE = 0.9
BETA_TWO = 0.999
ADAM_EPS = 1e-08
WEIGHT_DECAY = 0.01


def layer_norm(values):
    center = values - jnp.mean(values, axis=-1, keepdims=True)
    inv_scale = lax.rsqrt(jnp.mean(center * center, axis=-1, keepdims=True) + EPS_NORM)
    return (center * inv_scale, inv_scale)


def norm_back(grad_normed, normed, inv_scale):
    return inv_scale * (
        grad_normed
        - jnp.mean(grad_normed, axis=-1, keepdims=True)
        - normed * jnp.mean(grad_normed * normed, axis=-1, keepdims=True)
    )


def gelu_pair(preact):
    normal_cdf = 0.5 * (1.0 + jax.scipy.special.erf(preact * (1.0 / math.sqrt(2.0))))
    density = jnp.exp(-0.5 * preact * preact) * (1.0 / math.sqrt(2.0 * math.pi))
    return (preact * normal_cdf, normal_cdf + preact * density)


def dot_right_t(left, right):
    return lax.dot_general(
        left, right, (((1,), (1,)), ((), ())), preferred_element_type=jnp.float32
    )


def head_scores(query_heads, key_heads, key_position, valid_len):
    scores = jnp.einsum("qhd,khd->hqk", query_heads, key_heads, preferred_element_type=jnp.float32)
    scores = scores * (1.0 / math.sqrt(HEAD))
    return jnp.where(key_position[None, None, :] < valid_len, scores, -jnp.inf)


def split_heads(rows):
    return rows.reshape(rows.shape[0], -1, HEAD)


def attention_forward(queries, keys_all, values_all, key_position, valid_len):
    scores = head_scores(split_heads(queries), split_heads(keys_all), key_position, valid_len)
    log_total = jax.nn.logsumexp(scores, axis=-1)
    attn_probs = jnp.exp(scores - log_total[:, :, None]).astype(jnp.bfloat16)
    attn_mixed = jnp.einsum(
        "hqk,khd->qhd", attn_probs, split_heads(values_all), preferred_element_type=jnp.float32
    )
    return (attn_mixed.reshape(queries.shape).astype(jnp.bfloat16), log_total)


def attention_backward(
    queries, keys_all, values_all, attn_mixed, grad_mixed, log_total, key_position, valid_len
):
    scale_attn = 1.0 / math.sqrt(HEAD)
    query_heads, key_heads = split_heads(queries), split_heads(keys_all)
    grad_heads, mixed_heads = split_heads(grad_mixed), split_heads(attn_mixed)
    scores = head_scores(query_heads, key_heads, key_position, valid_len)
    probs_full = jnp.exp(scores - log_total[:, :, None])
    attn_probs = probs_full.astype(jnp.bfloat16)
    row_delta = jnp.sum(grad_heads.astype(jnp.float32) * mixed_heads.astype(jnp.float32), axis=-1).T
    grad_probs = jnp.einsum(
        "qhd,khd->hqk", grad_heads, split_heads(values_all), preferred_element_type=jnp.float32
    )
    grad_scores = (probs_full * (grad_probs - row_delta[:, :, None])).astype(jnp.bfloat16)
    grad_query = (
        jnp.einsum("hqk,khd->qhd", grad_scores, key_heads, preferred_element_type=jnp.float32)
        * scale_attn
    ).astype(jnp.bfloat16)
    grad_key = (
        jnp.einsum("hqk,qhd->khd", grad_scores, query_heads, preferred_element_type=jnp.float32)
        * scale_attn
    ).astype(jnp.bfloat16)
    grad_value = jnp.einsum(
        "hqk,qhd->khd", attn_probs, grad_heads, preferred_element_type=jnp.float32
    ).astype(jnp.bfloat16)
    return tuple(part.reshape(queries.shape) for part in (grad_query, grad_key, grad_value))


def from_behind(piece, distance):
    count = lax.axis_size("seq")
    if distance % count == 0:
        return piece
    return lax.ppermute(piece, "seq", [(i, (i + distance) % count) for i in range(count)])


def gather_behind(piece):
    return [from_behind(piece, r) for r in range(lax.axis_size("seq"))]


def swap_behind(pieces):
    count = len(pieces)
    return [from_behind(pieces[(-r) % count], r) for r in range(count)]


def turn_blocks(blocks):
    count = blocks.shape[0]
    place = lax.axis_index("seq")
    order = (place - jnp.arange(count, dtype=jnp.int32)) % count
    mask = order[:, None] == jnp.arange(count, dtype=jnp.int32)[None, :]
    mask = mask.reshape((count, count) + (1,) * (blocks.ndim - 1))
    return jnp.sum(jnp.where(mask, blocks[None], jnp.zeros((), blocks.dtype)), axis=1)


def adam_step(parameter, gradient, moment_one, moment_two, decay_rate):
    one_new = BETA_ONE * moment_one + (1.0 - BETA_ONE) * gradient
    two_new = BETA_TWO * moment_two + (1.0 - BETA_TWO) * gradient * gradient
    one_hat = one_new / (1.0 - BETA_ONE**STEP)
    two_hat = two_new / (1.0 - BETA_TWO**STEP)
    update = one_hat / (jnp.sqrt(two_hat) + ADAM_EPS)
    return (parameter - ADAM_RATE * (update + decay_rate * parameter), one_new, two_new)


def on_device(
    tokens,
    cotangent,
    lengths,
    w_attn,
    attn_first,
    attn_second,
    w_ffn,
    ffn_first,
    ffn_second,
    vectors,
    vec_first,
    vec_second,
):
    bf16, f32 = jnp.bfloat16, jnp.float32
    _, shard_len, model_width = tokens.shape
    seq_count, fsdp_count = lax.axis_size("seq"), lax.axis_size("fsdp")
    place = lax.axis_index("seq")
    _, row_shard, head_width = w_attn.shape
    hidden_shard = w_ffn.shape[2]
    vec_rows, vec_shard = vectors.shape
    token_rows = tokens.reshape(shard_len, model_width)
    cot_rows = cotangent.reshape(shard_len, model_width).astype(f32)

    early_shard = jnp.concatenate([w_attn[3], w_ffn[0]], axis=1).astype(bf16)
    late_shard = w_ffn[1].astype(bf16)
    vec_line = -(-vec_rows * vec_shard // (16 * head_width)) * 16
    vec_pad = vec_line * head_width - vec_rows * vec_shard
    vec_packed = jnp.pad(vectors.astype(bf16).reshape(-1), (0, vec_pad)).reshape(vec_line, head_width)
    qkv_shard = jnp.concatenate(
        [w_attn[:3].astype(bf16).reshape(3 * row_shard, head_width), vec_packed], axis=0
    )
    qkv_all = lax.all_gather(qkv_shard, "fsdp", axis=0, tiled=False)
    early_pieces = gather_behind(early_shard)
    token_pieces = gather_behind(token_rows)
    late_pieces = gather_behind(late_shard)
    early_all = lax.all_gather(
        jnp.concatenate(
            [piece[:, :head_width] for piece in early_pieces]
            + [piece[:, head_width:] for piece in early_pieces],
            axis=1,
        ),
        "fsdp",
        axis=0,
        tiled=True,
    )
    down_t = lax.all_gather(jnp.concatenate(late_pieces, axis=1), "fsdp", axis=0, tiled=True)
    out_t = early_all[:, : head_width * seq_count]
    up_w = early_all[:, head_width * seq_count :]
    w_qkv = [
        qkv_all[:, i * row_shard : (i + 1) * row_shard].reshape(model_width, head_width)
        for i in range(3)
    ]
    vec_own = (
        qkv_all[:, 3 * row_shard :]
        .reshape(fsdp_count, vec_line * head_width)[:, : vec_rows * vec_shard]
        .reshape(fsdp_count, vec_rows, vec_shard)
        .transpose(1, 0, 2)
        .reshape(vec_rows, head_width)
    )
    vec_wide = (
        turn_blocks(jnp.stack(gather_behind(vec_own)))
        .transpose(1, 0, 2)
        .reshape(vec_rows, model_width)
        .astype(f32)
    )
    up_bias = turn_blocks(vec_wide[8:12].reshape(seq_count, hidden_shard)).reshape(-1)
    vec_near = vec_own.astype(f32)

    token_all = jnp.concatenate(token_pieces, axis=0)
    queries, keys_all, values_all = (
        (jnp.dot(token_all, w_qkv[0], preferred_element_type=f32) + vec_near[0]).astype(bf16),
        jnp.dot(token_all, w_qkv[1], preferred_element_type=f32).astype(bf16),
        (jnp.dot(token_all, w_qkv[2], preferred_element_type=f32) + vec_near[1]).astype(bf16),
    )
    shard_order = (place - jnp.arange(seq_count, dtype=jnp.int32)) % seq_count
    key_position = (
        shard_order[:, None] * shard_len + jnp.arange(shard_len, dtype=jnp.int32)[None, :]
    ).reshape(-1)
    valid_len = lengths[0]
    mixed_heads, log_total = attention_forward(
        queries, keys_all, values_all, key_position, valid_len
    )
    mixed_rows = jnp.concatenate(
        swap_behind([mixed_heads[r * shard_len : (r + 1) * shard_len] for r in range(seq_count)]),
        axis=1,
    )

    hidden_one = token_rows.astype(f32) + dot_right_t(mixed_rows, out_t) + vec_wide[2]
    normed_one, inv_one = layer_norm(hidden_one)
    resid_one = normed_one * vec_wide[4] + vec_wide[5]
    resid_half = resid_one.astype(bf16)
    preact = jnp.dot(resid_half, up_w, preferred_element_type=f32) + up_bias
    activation, gelu_slope = gelu_pair(preact)
    act_half = activation.astype(bf16)
    hidden_two = resid_one + dot_right_t(act_half, down_t) + vec_wide[3]
    normed_two, inv_two = layer_norm(hidden_two)
    block_out = (normed_two * vec_wide[6] + vec_wide[7]).astype(bf16)
    grad_two = norm_back(cot_rows * vec_wide[6], normed_two, inv_two)
    grad_two_half = grad_two.astype(bf16)

    def own_sum(pieces):
        moved = swap_behind([piece.astype(bf16) for piece in pieces])
        total = pieces[0].astype(f32)
        for piece in moved[1:]:
            total = total + piece.astype(f32)
        return total

    def reduce_rows(left, right):
        product = lax.dot_general(
            left, right, (((0,), (0,)), ((), ())), preferred_element_type=f32
        ).astype(bf16)
        return lax.psum_scatter(product, "fsdp", scatter_dimension=0, tiled=True)

    def reduce_seq(part):
        return own_sum(jnp.split(part, seq_count, axis=1))

    down_part = reduce_rows(grad_two_half, act_half)
    grad_pre = jnp.dot(grad_two_half, down_t, preferred_element_type=f32) * gelu_slope
    grad_pre_half = grad_pre.astype(bf16)
    up_part = reduce_rows(resid_half, grad_pre_half)
    grad_resid = grad_two + dot_right_t(grad_pre_half, up_w)
    grad_one = norm_back(grad_resid * vec_wide[4], normed_one, inv_one)
    grad_one_half = grad_one.astype(bf16)
    grad_mixed = jnp.dot(grad_one_half, out_t, preferred_element_type=f32).astype(bf16)
    out_part = reduce_rows(grad_one_half, mixed_rows)
    grad_heads = jnp.concatenate(swap_behind(jnp.split(grad_mixed, seq_count, axis=1)), axis=0)
    grads = attention_backward(
        queries, keys_all, values_all, mixed_heads, grad_heads, log_total, key_position, valid_len
    )
    input_part = sum(dot_right_t(grad, weight) for grad, weight in zip(grads, w_qkv, strict=True))
    input_grad = grad_one + own_sum(
        [input_part[r * shard_len : (r + 1) * shard_len] for r in range(seq_count)]
    )

    bias_sums = turn_blocks(jnp.sum(grad_pre, axis=0).reshape(seq_count, hidden_shard))
    vec_local = jnp.concatenate(
        [
            jnp.stack(
                [
                    jnp.sum(grad_one, axis=0),
                    jnp.sum(grad_two, axis=0),
                    jnp.sum(grad_resid * normed_one, axis=0),
                    jnp.sum(grad_resid, axis=0),
                    jnp.sum(cot_rows * normed_two, axis=0),
                    jnp.sum(cot_rows, axis=0),
                ]
            ),
            bias_sums.reshape(-1, model_width),
        ],
        axis=0,
    )
    vec_blocks = turn_blocks(vec_local.reshape(-1, seq_count, head_width).transpose(1, 0, 2))
    vec_lower = sum(swap_behind([vec_blocks[r] for r in range(seq_count)]))
    vec_sums = jnp.concatenate(
        [
            jnp.sum(grads[0].astype(f32), axis=0)[None],
            jnp.sum(grads[2].astype(f32), axis=0)[None],
            vec_lower,
        ],
        axis=0,
    )
    vec_send = (
        vec_sums.reshape(vec_rows, fsdp_count, vec_shard)
        .transpose(1, 0, 2)
        .reshape(fsdp_count, vec_rows * vec_shard)
    )
    vec_send = jnp.pad(vec_send, ((0, 0), (0, vec_pad))).reshape(fsdp_count, vec_line, head_width)
    qkv_send = jnp.concatenate(
        [
            lax.dot_general(
                token_all, grad, (((0,), (0,)), ((), ())), preferred_element_type=f32
            ).reshape(fsdp_count, row_shard, head_width)
            for grad in grads
        ]
        + [vec_send],
        axis=1,
    )
    qkv_sum = lax.psum_scatter(qkv_send, "fsdp", scatter_dimension=0, tiled=False)

    token_total = shard_len * seq_count * fsdp_count
    grad_scale = float(token_total) ** (-0.5)
    attn_grad = grad_scale * jnp.concatenate(
        [
            qkv_sum[: 3 * row_shard].reshape(3, row_shard, head_width),
            reduce_seq(out_part)[None],
        ],
        axis=0,
    )
    ffn_grad = grad_scale * jnp.stack([reduce_seq(up_part), reduce_seq(down_part)])
    vec_grad = grad_scale * qkv_sum[3 * row_shard :].reshape(-1)[: vec_rows * vec_shard].reshape(
        vec_rows, vec_shard
    )
    attn_new, attn_one, attn_two = adam_step(
        w_attn, attn_grad, attn_first, attn_second, WEIGHT_DECAY
    )
    ffn_new, ffn_one, ffn_two = adam_step(w_ffn, ffn_grad, ffn_first, ffn_second, WEIGHT_DECAY)
    vec_new, vec_one, vec_two = adam_step(vectors, vec_grad, vec_first, vec_second, 0.0)
    return (
        block_out.reshape(tokens.shape),
        input_grad.reshape(tokens.shape),
        attn_grad,
        ffn_grad,
        vec_grad,
        attn_new,
        attn_one,
        attn_two,
        ffn_new,
        ffn_one,
        ffn_two,
        vec_new,
        vec_one,
        vec_two,
    )


def solution(mesh):
    placed = (
        P("fsdp", "seq", None),
        P("fsdp", "seq", None),
        P("fsdp"),
        P(None, "fsdp", "seq"),
        P(None, "fsdp", "seq"),
        P(None, "fsdp", "seq"),
        P(None, "fsdp", "seq"),
        P(None, "fsdp", "seq"),
        P(None, "fsdp", "seq"),
        P(None, ("seq", "fsdp")),
        P(None, ("seq", "fsdp")),
        P(None, ("seq", "fsdp")),
    )
    return jax.shard_map(
        on_device,
        mesh=mesh,
        in_specs=placed,
        out_specs=(
            P("fsdp", "seq", None),
            P("fsdp", "seq", None),
            P(None, "fsdp", "seq"),
            P(None, "fsdp", "seq"),
            P(None, ("seq", "fsdp")),
            P(None, "fsdp", "seq"),
            P(None, "fsdp", "seq"),
            P(None, "fsdp", "seq"),
            P(None, "fsdp", "seq"),
            P(None, "fsdp", "seq"),
            P(None, "fsdp", "seq"),
            P(None, ("seq", "fsdp")),
            P(None, ("seq", "fsdp")),
            P(None, ("seq", "fsdp")),
        ),
        check_vma=False,
    )
```

```python
import math

import jax
import jax.numpy as jnp
from jax import lax
from jax.experimental import pallas as pl
from jax.experimental.pallas import tpu as pltpu
from jax.sharding import PartitionSpec as P

HEAD = 64
STEP = 3


EPS_NORM = 1e-12
ADAM_RATE = 0.005
BETA_ONE = 0.9
BETA_TWO = 0.999
ADAM_EPS = 1e-08
WEIGHT_DECAY = 0.01


def layer_norm(values):
    center = values - jnp.mean(values, axis=-1, keepdims=True)
    inv_scale = lax.rsqrt(jnp.mean(center * center, axis=-1, keepdims=True) + EPS_NORM)
    return (center * inv_scale, inv_scale)


def norm_back(grad_normed, normed, inv_scale):
    return inv_scale * (
        grad_normed
        - jnp.mean(grad_normed, axis=-1, keepdims=True)
        - normed * jnp.mean(grad_normed * normed, axis=-1, keepdims=True)
    )


def gelu_pair(preact):
    normal_cdf = 0.5 * (1.0 + jax.scipy.special.erf(preact * (1.0 / math.sqrt(2.0))))
    density = jnp.exp(-0.5 * preact * preact) * (1.0 / math.sqrt(2.0 * math.pi))
    return (preact * normal_cdf, normal_cdf + preact * density)


def dot_right_t(left, right):
    return lax.dot_general(
        left, right, (((1,), (1,)), ((), ())), preferred_element_type=jnp.float32
    )


def head_scores(query_heads, key_heads, key_position, valid_len):
    scores = jnp.einsum("qhd,khd->hqk", query_heads, key_heads, preferred_element_type=jnp.float32)
    scores = scores * (1.0 / math.sqrt(HEAD))
    return jnp.where(key_position[None, None, :] < valid_len, scores, -jnp.inf)


def split_heads(rows):
    return rows.reshape(rows.shape[0], -1, HEAD)


def attention_forward(queries, keys_all, values_all, key_position, valid_len):
    scores = head_scores(split_heads(queries), split_heads(keys_all), key_position, valid_len)
    log_total = jax.nn.logsumexp(scores, axis=-1)
    attn_probs = jnp.exp(scores - log_total[:, :, None]).astype(jnp.bfloat16)
    attn_mixed = jnp.einsum(
        "hqk,khd->qhd", attn_probs, split_heads(values_all), preferred_element_type=jnp.float32
    )
    return (attn_mixed.reshape(queries.shape).astype(jnp.bfloat16), log_total)


def attention_backward(
    queries, keys_all, values_all, attn_mixed, grad_mixed, log_total, key_position, valid_len
):
    scale_attn = 1.0 / math.sqrt(HEAD)
    query_heads, key_heads = split_heads(queries), split_heads(keys_all)
    grad_heads, mixed_heads = split_heads(grad_mixed), split_heads(attn_mixed)
    scores = head_scores(query_heads, key_heads, key_position, valid_len)
    probs_full = jnp.exp(scores - log_total[:, :, None])
    attn_probs = probs_full.astype(jnp.bfloat16)
    row_delta = jnp.sum(grad_heads.astype(jnp.float32) * mixed_heads.astype(jnp.float32), axis=-1).T
    grad_probs = jnp.einsum(
        "qhd,khd->hqk", grad_heads, split_heads(values_all), preferred_element_type=jnp.float32
    )
    grad_scores = (probs_full * (grad_probs - row_delta[:, :, None])).astype(jnp.bfloat16)
    grad_query = (
        jnp.einsum("hqk,khd->qhd", grad_scores, key_heads, preferred_element_type=jnp.float32)
        * scale_attn
    ).astype(jnp.bfloat16)
    grad_key = (
        jnp.einsum("hqk,qhd->khd", grad_scores, query_heads, preferred_element_type=jnp.float32)
        * scale_attn
    ).astype(jnp.bfloat16)
    grad_value = jnp.einsum(
        "hqk,qhd->khd", attn_probs, grad_heads, preferred_element_type=jnp.float32
    ).astype(jnp.bfloat16)
    return tuple(part.reshape(queries.shape) for part in (grad_query, grad_key, grad_value))


def from_behind(piece, distance):
    count = lax.axis_size("seq")
    if distance % count == 0:
        return piece
    return lax.ppermute(piece, "seq", [(i, (i + distance) % count) for i in range(count)])


def gather_behind(piece):
    return [from_behind(piece, r) for r in range(lax.axis_size("seq"))]


def swap_behind(pieces):
    count = len(pieces)
    return [from_behind(pieces[(-r) % count], r) for r in range(count)]


def turn_blocks(blocks):
    count = blocks.shape[0]
    place = lax.axis_index("seq")
    order = (place - jnp.arange(count, dtype=jnp.int32)) % count
    mask = order[:, None] == jnp.arange(count, dtype=jnp.int32)[None, :]
    mask = mask.reshape((count, count) + (1,) * (blocks.ndim - 1))
    return jnp.sum(jnp.where(mask, blocks[None], jnp.zeros((), blocks.dtype)), axis=1)


def adam_step(parameter, gradient, moment_one, moment_two, decay_rate):
    one_new = BETA_ONE * moment_one + (1.0 - BETA_ONE) * gradient
    two_new = BETA_TWO * moment_two + (1.0 - BETA_TWO) * gradient * gradient
    one_hat = one_new / (1.0 - BETA_ONE**STEP)
    two_hat = two_new / (1.0 - BETA_TWO**STEP)
    update = one_hat / (jnp.sqrt(two_hat) + ADAM_EPS)
    return (parameter - ADAM_RATE * (update + decay_rate * parameter), one_new, two_new)


def halve(blocks, bit, from_low):
    count = blocks.shape[0]
    rest = blocks.shape[1:]
    own = (lax.axis_index("fsdp") >> bit) & 1
    split = (count // 2, 2) if from_low else (2, count // 2)
    axis = 1 if from_low else 0
    view = blocks.reshape(split + rest)
    kept = lax.dynamic_index_in_dim(view, own, axis, keepdims=False)
    sent = lax.dynamic_index_in_dim(view, 1 - own, axis, keepdims=False)
    pairs = [(i, i ^ (1 << bit)) for i in range(lax.axis_size("fsdp"))]
    received = lax.ppermute(sent.astype(jnp.bfloat16), "fsdp", pairs)
    return kept.astype(jnp.float32) + received.astype(jnp.float32)


def fold_up(blocks, bits):
    for bit in bits:
        blocks = halve(blocks, bit, True)
    return blocks[0]


def fold_down(blocks, bits):
    for bit in reversed(bits):
        blocks = halve(blocks, bit, False)
    return blocks[0]


def fsdp_bits():
    return list(range(lax.axis_size("fsdp").bit_length() - 1))


def vector_kernel(
    place_ref, one_ref, two_ref, resid_ref, normed_one_ref, normed_two_ref, cot_ref, pre_ref, out_ref
):
    seq_count, _, head_width = out_ref.shape
    model_width = one_ref.shape[1]
    resid = resid_ref[...]
    cot = cot_ref[...].astype(jnp.float32)
    rows = [
        one_ref[...],
        two_ref[...],
        resid * normed_one_ref[...],
        resid,
        cot * normed_two_ref[...],
        cot,
    ]
    out_ref[...] = jnp.zeros_like(out_ref)
    for k, values in enumerate(rows):
        total = jnp.sum(values, axis=0, keepdims=True)
        for j in range(seq_count):
            out_ref[j, 2 + k : 3 + k, :] = total[:, j * head_width : (j + 1) * head_width]
    pre = pre_ref[...].astype(jnp.float32)
    per_place = pre.shape[1] // seq_count // model_width
    totals = [
        jnp.sum(pre[:, k * model_width : (k + 1) * model_width], axis=0, keepdims=True)
        for k in range(seq_count * per_place)
    ]
    for k in range(seq_count):
        owner = (place_ref[0] + seq_count - k) % seq_count
        for i in range(per_place):
            row = 8 + owner * per_place + i
            total = totals[k * per_place + i]
            for j in range(seq_count):
                out_ref[j, pl.ds(row, 1), :] = total[:, j * head_width : (j + 1) * head_width]


def vector_sums(place, seq_count, head_width, *arrays):
    return pl.pallas_call(
        vector_kernel,
        out_shape=jax.ShapeDtypeStruct((seq_count, 16, head_width), jnp.float32),
        in_specs=[pl.BlockSpec(memory_space=pltpu.SMEM)]
        + [pl.BlockSpec(memory_space=pltpu.VMEM)] * len(arrays),
        out_specs=pl.BlockSpec(memory_space=pltpu.VMEM),
        compiler_params=pltpu.CompilerParams(vmem_limit_bytes=32 << 20),
        name="vector_sums",
    )(place.reshape(1), *arrays)


def on_device(
    tokens,
    cotangent,
    lengths,
    w_attn,
    attn_first,
    attn_second,
    w_ffn,
    ffn_first,
    ffn_second,
    vectors,
    vec_first,
    vec_second,
):
    bf16, f32 = jnp.bfloat16, jnp.float32
    _, shard_len, model_width = tokens.shape
    seq_count, fsdp_count = lax.axis_size("seq"), lax.axis_size("fsdp")
    place, member = lax.axis_index("seq"), lax.axis_index("fsdp")
    _, row_shard, head_width = w_attn.shape
    hidden_shard = w_ffn.shape[2]
    vec_rows, vec_shard = vectors.shape
    token_rows = tokens.reshape(shard_len, model_width)
    cot_half = cotangent.reshape(shard_len, model_width)
    cot_rows = cot_half.astype(f32)
    bits = fsdp_bits()

    own_shard = jnp.concatenate([w_ffn[0], w_ffn[1], w_attn[3]], axis=1).astype(bf16)
    early_shard = jnp.concatenate([w_ffn[0], w_attn[3]], axis=1).astype(bf16)
    late_shard = w_ffn[1].astype(bf16)
    vec_placed = lax.dynamic_update_slice(
        jnp.zeros((16, head_width), bf16), vectors.astype(bf16), (0, member * vec_shard)
    )
    qkv_shard = jnp.concatenate(
        [w_attn[:3].astype(bf16).reshape(3 * row_shard, head_width), vec_placed], axis=0
    )
    own_all = lax.all_gather(own_shard, "fsdp", axis=0, tiled=True)
    token_pieces = gather_behind(token_rows)
    early_pieces = gather_behind(early_shard)
    qkv_all = lax.all_gather(qkv_shard, "fsdp", axis=0, tiled=False)
    early_all = lax.all_gather(
        jnp.concatenate(
            [piece[:, :hidden_shard] for piece in early_pieces[1:]]
            + [piece[:, hidden_shard:] for piece in early_pieces[1:]],
            axis=1,
        ),
        "fsdp",
        axis=0,
        tiled=True,
    )
    late_shard, _ = lax.optimization_barrier((late_shard, early_pieces[1]))
    late_pieces = gather_behind(late_shard)
    late_all = lax.all_gather(jnp.concatenate(late_pieces[1:], axis=1), "fsdp", axis=0, tiled=True)
    up_parts = [own_all[:, :hidden_shard], early_all[:, : hidden_shard * (seq_count - 1)]]
    down_parts = [own_all[:, hidden_shard : 2 * hidden_shard], late_all]
    out_parts = [own_all[:, 2 * hidden_shard :], early_all[:, hidden_shard * (seq_count - 1) :]]

    def times(left, parts):
        return jnp.concatenate(
            [jnp.dot(left, part, preferred_element_type=f32) for part in parts], axis=1
        )

    def times_t(left, parts):
        width = parts[0].shape[1]
        return dot_right_t(left[:, :width], parts[0]) + dot_right_t(left[:, width:], parts[1])

    w_qkv = [
        qkv_all[:, i * row_shard : (i + 1) * row_shard].reshape(model_width, head_width)
        for i in range(3)
    ]
    vec_own = jnp.sum(qkv_all[:, 3 * row_shard :].astype(f32), axis=0)[:vec_rows]
    vec_near = [piece.astype(f32) for piece in gather_behind(vec_own.astype(bf16))]

    def near(order):
        return sum(jnp.where(order == r, piece, 0.0) for r, piece in enumerate(vec_near))

    vec_wide = jnp.concatenate(
        [near((place - j) % seq_count) for j in range(seq_count)], axis=1
    )
    up_bias = turn_blocks(vec_wide[8:12].reshape(seq_count, hidden_shard)).reshape(-1)

    token_all = jnp.concatenate(token_pieces, axis=0)
    queries, keys_all, values_all = (
        (jnp.dot(token_all, w_qkv[0], preferred_element_type=f32) + vec_own[0]).astype(bf16),
        jnp.dot(token_all, w_qkv[1], preferred_element_type=f32).astype(bf16),
        (jnp.dot(token_all, w_qkv[2], preferred_element_type=f32) + vec_own[1]).astype(bf16),
    )
    shard_order = (place - jnp.arange(seq_count, dtype=jnp.int32)) % seq_count
    key_position = (
        shard_order[:, None] * shard_len + jnp.arange(shard_len, dtype=jnp.int32)[None, :]
    ).reshape(-1)
    valid_len = lengths[0]
    mixed_heads, log_total = attention_forward(
        queries, keys_all, values_all, key_position, valid_len
    )
    mixed_rows = jnp.concatenate(
        swap_behind([mixed_heads[r * shard_len : (r + 1) * shard_len] for r in range(seq_count)]),
        axis=1,
    )

    hidden_one = token_rows.astype(f32) + times_t(mixed_rows, out_parts) + vec_wide[2]
    normed_one, inv_one = layer_norm(hidden_one)
    resid_one = normed_one * vec_wide[4] + vec_wide[5]
    resid_half = resid_one.astype(bf16)
    preact = times(resid_half, up_parts) + up_bias
    activation, gelu_slope = gelu_pair(preact)
    act_half = activation.astype(bf16)
    hidden_two = resid_one + times_t(act_half, down_parts) + vec_wide[3]
    normed_two, inv_two = layer_norm(hidden_two)
    block_out = (normed_two * vec_wide[6] + vec_wide[7]).astype(bf16)
    grad_two = norm_back(cot_rows * vec_wide[6], normed_two, inv_two)
    grad_two_half = grad_two.astype(bf16)

    def outer(left, right):
        return lax.dot_general(
            left, right, (((0,), (0,)), ((), ())), preferred_element_type=f32
        ).astype(bf16)

    def own_sum(pieces):
        moved = swap_behind([piece.astype(bf16) for piece in pieces])
        total = pieces[0].astype(f32)
        for piece in moved[1:]:
            total = total + piece.astype(f32)
        return total

    down_local, grad_two_half = lax.optimization_barrier(
        (outer(grad_two_half, act_half), grad_two_half)
    )
    down_part = lax.psum_scatter(down_local, "fsdp", scatter_dimension=0, tiled=True)
    grad_pre_half = (times(grad_two_half, down_parts) * gelu_slope).astype(bf16)
    up_local, grad_pre_half = lax.optimization_barrier(
        (outer(resid_half, grad_pre_half), grad_pre_half)
    )
    grad_resid = grad_two + times_t(grad_pre_half, up_parts)
    grad_one = norm_back(grad_resid * vec_wide[4], normed_one, inv_one)
    grad_one_half = grad_one.astype(bf16)
    grad_mixed = times(grad_one_half, out_parts).astype(bf16)
    out_local = outer(grad_one_half, mixed_rows)
    grad_heads = jnp.concatenate(swap_behind(jnp.split(grad_mixed, seq_count, axis=1)), axis=0)

    vec_blocks = vector_sums(
        place,
        seq_count,
        head_width,
        grad_one,
        grad_two,
        grad_resid,
        normed_one,
        normed_two,
        cot_half,
        grad_pre_half,
    )
    vec_part = lax.psum_scatter(vec_blocks, "seq", scatter_dimension=0, tiled=True)[0]

    near_places = seq_count // 2
    wide_blocks = jnp.concatenate(
        [
            up_local.reshape(fsdp_count, row_shard, -1),
            out_local.reshape(fsdp_count, row_shard, -1),
        ],
        axis=2,
    )
    wide_blocks = halve(wide_blocks, 0, True)
    up_half, out_half = near_places * hidden_shard, near_places * head_width
    up_wide = seq_count * hidden_shard
    first_half = fold_up(
        jnp.concatenate(
            [wide_blocks[..., :up_half], wide_blocks[..., up_wide : up_wide + out_half]], axis=-1
        ),
        bits[1:],
    )
    second_half = fold_down(
        jnp.concatenate(
            [wide_blocks[..., up_half:up_wide], wide_blocks[..., up_wide + out_half :]], axis=-1
        ),
        bits[1:],
    )

    def place_pieces(half, count):
        ups, outs = half[:, : count * hidden_shard], half[:, count * hidden_shard :]
        return [
            jnp.concatenate(
                [
                    ups[:, r * hidden_shard : (r + 1) * hidden_shard],
                    outs[:, r * head_width : (r + 1) * head_width],
                ],
                axis=1,
            )
            for r in range(count)
        ]

    up_out_sum = own_sum(
        place_pieces(first_half, near_places) + place_pieces(second_half, seq_count - near_places)
    )
    down_sum = own_sum(jnp.split(down_part, seq_count, axis=1))

    grads = attention_backward(
        queries, keys_all, values_all, mixed_heads, grad_heads, log_total, key_position, valid_len
    )
    input_part = sum(dot_right_t(grad, weight) for grad, weight in zip(grads, w_qkv, strict=True))
    input_grad = grad_one + own_sum(
        [input_part[r * shard_len : (r + 1) * shard_len] for r in range(seq_count)]
    )
    bias_rows = jnp.arange(16, dtype=jnp.int32)[:, None]
    vec_lines = jnp.where(
        bias_rows == 0,
        jnp.sum(grads[0].astype(f32), axis=0)[None],
        jnp.where(bias_rows == 1, jnp.sum(grads[2].astype(f32), axis=0)[None], vec_part),
    )
    qkv_send = jnp.concatenate(
        [
            lax.dot_general(
                token_all, grad, (((0,), (0,)), ((), ())), preferred_element_type=f32
            ).reshape(fsdp_count, row_shard, head_width)
            for grad in grads
        ]
        + [jnp.broadcast_to(vec_lines[None], (fsdp_count, 16, head_width))],
        axis=1,
    )
    qkv_sum = fold_up(qkv_send, bits)

    token_total = shard_len * seq_count * fsdp_count
    grad_scale = float(token_total) ** (-0.5)
    attn_grad = grad_scale * jnp.concatenate(
        [
            qkv_sum[: 3 * row_shard].reshape(3, row_shard, head_width),
            up_out_sum[None, :, hidden_shard:],
        ],
        axis=0,
    )
    ffn_grad = grad_scale * jnp.stack([up_out_sum[:, :hidden_shard], down_sum])
    vec_grad = grad_scale * lax.dynamic_slice(
        qkv_sum[3 * row_shard :], (0, member * vec_shard), (vec_rows, vec_shard)
    )
    attn_new, attn_one, attn_two = adam_step(
        w_attn, attn_grad, attn_first, attn_second, WEIGHT_DECAY
    )
    ffn_new, ffn_one, ffn_two = adam_step(w_ffn, ffn_grad, ffn_first, ffn_second, WEIGHT_DECAY)
    vec_new, vec_one, vec_two = adam_step(vectors, vec_grad, vec_first, vec_second, 0.0)
    return (
        block_out.reshape(tokens.shape),
        input_grad.reshape(tokens.shape),
        attn_grad,
        ffn_grad,
        vec_grad,
        attn_new,
        attn_one,
        attn_two,
        ffn_new,
        ffn_one,
        ffn_two,
        vec_new,
        vec_one,
        vec_two,
    )


def solution(mesh):
    placed = (
        P("fsdp", "seq", None),
        P("fsdp", "seq", None),
        P("fsdp"),
        P(None, "fsdp", "seq"),
        P(None, "fsdp", "seq"),
        P(None, "fsdp", "seq"),
        P(None, "fsdp", "seq"),
        P(None, "fsdp", "seq"),
        P(None, "fsdp", "seq"),
        P(None, ("seq", "fsdp")),
        P(None, ("seq", "fsdp")),
        P(None, ("seq", "fsdp")),
    )
    return jax.shard_map(
        on_device,
        mesh=mesh,
        in_specs=placed,
        out_specs=(
            P("fsdp", "seq", None),
            P("fsdp", "seq", None),
            P(None, "fsdp", "seq"),
            P(None, "fsdp", "seq"),
            P(None, ("seq", "fsdp")),
            P(None, "fsdp", "seq"),
            P(None, "fsdp", "seq"),
            P(None, "fsdp", "seq"),
            P(None, "fsdp", "seq"),
            P(None, "fsdp", "seq"),
            P(None, "fsdp", "seq"),
            P(None, ("seq", "fsdp")),
            P(None, ("seq", "fsdp")),
            P(None, ("seq", "fsdp")),
        ),
        check_vma=False,
    )
```

```python
import math

import jax
import jax.numpy as jnp
from jax import lax
from jax.experimental import pallas as pl
from jax.experimental.pallas import tpu as pltpu
from jax.sharding import PartitionSpec as P

HEAD = 64
STEP = 3
SCORE_SCALE = 1.0 / math.sqrt(HEAD)


EPS_NORM = 1e-12
ADAM_RATE = 0.005
BETA_ONE = 0.9
BETA_TWO = 0.999
ADAM_EPS = 1e-08
WEIGHT_DECAY = 0.01


def layer_norm(values):
    center = values - jnp.mean(values, axis=-1, keepdims=True)
    inv_scale = lax.rsqrt(jnp.mean(center * center, axis=-1, keepdims=True) + EPS_NORM)
    return (center * inv_scale, inv_scale)


def norm_back(grad_normed, normed, inv_scale):
    return inv_scale * (
        grad_normed
        - jnp.mean(grad_normed, axis=-1, keepdims=True)
        - normed * jnp.mean(grad_normed * normed, axis=-1, keepdims=True)
    )


def gelu_pair(preact):
    normal_cdf = 0.5 * (1.0 + jax.scipy.special.erf(preact * (1.0 / math.sqrt(2.0))))
    density = jnp.exp(-0.5 * preact * preact) * (1.0 / math.sqrt(2.0 * math.pi))
    return (preact * normal_cdf, normal_cdf + preact * density)


def dot_right_t(left, right):
    return lax.dot_general(
        left, right, (((1,), (1,)), ((), ())), preferred_element_type=jnp.float32
    )


def from_behind(piece, distance):
    count = lax.axis_size("seq")
    if distance % count == 0:
        return piece
    return lax.ppermute(piece, "seq", [(i, (i + distance) % count) for i in range(count)])


def gather_behind(piece):
    return [from_behind(piece, r) for r in range(lax.axis_size("seq"))]


def swap_behind(pieces):
    count = len(pieces)
    return [from_behind(pieces[(-r) % count], r) for r in range(count)]


def turn_blocks(blocks):
    count = blocks.shape[0]
    place = lax.axis_index("seq")
    order = (place - jnp.arange(count, dtype=jnp.int32)) % count
    mask = order[:, None] == jnp.arange(count, dtype=jnp.int32)[None, :]
    mask = mask.reshape((count, count) + (1,) * (blocks.ndim - 1))
    return jnp.sum(jnp.where(mask, blocks[None], jnp.zeros((), blocks.dtype)), axis=1)


def adam_step(parameter, gradient, moment_one, moment_two, decay_rate):
    one_new = BETA_ONE * moment_one + (1.0 - BETA_ONE) * gradient
    two_new = BETA_TWO * moment_two + (1.0 - BETA_TWO) * gradient * gradient
    one_hat = one_new / (1.0 - BETA_ONE**STEP)
    two_hat = two_new / (1.0 - BETA_TWO**STEP)
    update = one_hat / (jnp.sqrt(two_hat) + ADAM_EPS)
    return (parameter - ADAM_RATE * (update + decay_rate * parameter), one_new, two_new)


def after(values, *earlier):
    return lax.optimization_barrier((values, earlier))[0]


def halving(blocks, bit, from_low):
    count = blocks.shape[0]
    own = (lax.axis_index("fsdp") >> bit) & 1
    split = (count // 2, 2) if from_low else (2, count // 2)
    axis = 1 if from_low else 0
    view = blocks.reshape(split + blocks.shape[1:])
    kept = lax.dynamic_index_in_dim(view, own, axis, keepdims=False)
    sent = lax.dynamic_index_in_dim(view, 1 - own, axis, keepdims=False)
    return kept, sent.astype(jnp.bfloat16)


def swapped(sent, bit):
    return lax.ppermute(sent, "fsdp", [(i, i ^ (1 << bit)) for i in range(lax.axis_size("fsdp"))])


def joined(kept, received):
    return kept.astype(jnp.float32) + received.astype(jnp.float32)


def attend_kernel(
    place_ref, length_ref, bias_ref, *refs
):
    count = (len(refs) - 3 - 4) // 2
    token_refs, weight_refs = refs[:count], refs[count : count + 3]
    q_ref, k_ref, v_ref, lse_ref = refs[count + 3 : count + 7]
    mixed_refs = refs[count + 7 :]
    shard_len = token_refs[0].shape[0]
    rows, width = q_ref.shape
    for r, token_ref in enumerate(token_refs):
        piece = token_ref[...]
        for k, (weight_ref, out_ref) in enumerate(
            zip(weight_refs, (q_ref, k_ref, v_ref), strict=True)
        ):
            out = jnp.dot(piece, weight_ref[...], preferred_element_type=jnp.float32)
            if k != 1:
                out = out + bias_ref[k // 2 : k // 2 + 1, :]
            out_ref[r * shard_len : (r + 1) * shard_len, :] = out.astype(jnp.bfloat16)
    masked = key_mask(place_ref[0], length_ref[0], count, shard_len)

    for i, mixed_ref in enumerate(mixed_refs):
        at = slice(i * shard_len, (i + 1) * shard_len)
        queries = q_ref[at, :]
        mixed = []
        for h in range(width // HEAD):
            cols = slice(h * HEAD, (h + 1) * HEAD)
            scores = dot_right_t(queries[:, cols] * SCORE_SCALE, k_ref[:, cols]) + masked
            top = jnp.max(scores, axis=1, keepdims=True)
            raised = jnp.exp(scores - top)
            total = jnp.sum(raised, axis=1, keepdims=True)
            probs = (raised * (1.0 / total)).astype(jnp.bfloat16)
            mixed.append(jnp.dot(probs, v_ref[:, cols], preferred_element_type=jnp.float32))
            lse_ref[at, h : h + 1] = top + jnp.log(total)
        mixed_ref[...] = jnp.concatenate(mixed, axis=1).astype(jnp.bfloat16)


def key_mask(place, length, count, shard_len):
    column = lax.broadcasted_iota(jnp.int32, (1, shard_len), 1)
    pieces = []
    for r in range(count):
        start = lax.rem(place + count - r, count) * shard_len
        pieces.append(jnp.where(column + start < length, 0.0, -jnp.inf))
    return jnp.concatenate(pieces, axis=1)


def attend(place, length, bias, token_pieces, weights):
    shard_len = token_pieces[0].shape[0]
    rows, width = shard_len * len(token_pieces), weights[0].shape[1]
    half = jax.ShapeDtypeStruct((rows, width), jnp.bfloat16)
    smem, vmem = pl.BlockSpec(memory_space=pltpu.SMEM), pl.BlockSpec(memory_space=pltpu.VMEM)
    arrays = (bias, *token_pieces, *weights)
    return pl.pallas_call(
        attend_kernel,
        out_shape=(half, half, half, jax.ShapeDtypeStruct((rows, 8), jnp.float32))
        + (jax.ShapeDtypeStruct((shard_len, width), jnp.bfloat16),) * len(token_pieces),
        in_specs=[smem, smem] + [vmem] * len(arrays),
        out_specs=(vmem,) * (4 + len(token_pieces)),
        compiler_params=pltpu.CompilerParams(vmem_limit_bytes=40 << 20),
        cost_estimate=pl.CostEstimate(
            flops=2 * rows * width * (3 * weights[0].shape[0] + 8 * rows),
            bytes_accessed=8 << 20,
            transcendentals=rows * rows * (width // HEAD),
        ),
        name="attend",
    )(place.reshape(1), length.reshape(1), *arrays)


def attend_back_kernel(
    place_ref,
    length_ref,
    q_ref,
    k_ref,
    v_ref,
    lse_ref,
    *refs,
):
    count = (len(refs) - 3 - 3 - 2) // 3
    mixed_refs, grad_refs = refs[:count], refs[count : 2 * count]
    weight_refs, refs = refs[2 * count : 2 * count + 3], refs[2 * count + 3 :]
    dq_ref, dk_ref, dv_ref = refs[:3]
    part_refs = refs[3 : 3 + count]
    dk_sum, dv_sum = refs[3 + count :]
    shard_len = grad_refs[0].shape[0]
    rows, width = q_ref.shape
    masked = key_mask(place_ref[0], length_ref[0], count, shard_len)
    for i, (grad_ref, mixed_ref) in enumerate(zip(grad_refs, mixed_refs, strict=True)):
        at = slice(i * shard_len, (i + 1) * shard_len)
        queries, grad = q_ref[at, :], grad_ref[...]
        product = grad.astype(jnp.float32) * mixed_ref[...].astype(jnp.float32)
        parts = []
        for h in range(width // HEAD):
            cols = slice(h * HEAD, (h + 1) * HEAD)
            head_q, head_grad = queries[:, cols], grad[:, cols]
            scores = dot_right_t(head_q * SCORE_SCALE, k_ref[:, cols]) + masked
            probs = jnp.exp(scores - lse_ref[at, h : h + 1])
            delta = jnp.sum(product[:, cols], axis=1, keepdims=True)
            grad_probs = dot_right_t(head_grad, v_ref[:, cols])
            grad_scores = (probs * (grad_probs - delta)).astype(jnp.bfloat16)
            parts.append(
                jnp.dot(grad_scores, k_ref[:, cols], preferred_element_type=jnp.float32)
                * SCORE_SCALE
            )
            dk = jnp.dot(head_q.T, grad_scores, preferred_element_type=jnp.float32)
            dv = jnp.dot(head_grad.T, probs.astype(jnp.bfloat16), preferred_element_type=jnp.float32)
            if i == 0:
                dk_sum[cols, :] = dk
                dv_sum[cols, :] = dv
            else:
                dk_sum[cols, :] += dk
                dv_sum[cols, :] += dv
        dq_ref[at, :] = jnp.concatenate(parts, axis=1).astype(jnp.bfloat16)
    dk_ref[...] = (dk_sum[...].T * SCORE_SCALE).astype(jnp.bfloat16)
    dv_ref[...] = dv_sum[...].T.astype(jnp.bfloat16)
    for i, part_ref in enumerate(part_refs):
        at = slice(i * shard_len, (i + 1) * shard_len)
        part = dot_right_t(dq_ref[at, :], weight_refs[0][...])
        part = part + dot_right_t(dk_ref[at, :], weight_refs[1][...])
        part = part + dot_right_t(dv_ref[at, :], weight_refs[2][...])
        part_ref[...] = part.astype(part_ref.dtype)


def attend_back(
    place, length, queries, keys_all, values_all, lse, mixed_pieces, grad_pieces, weights
):
    rows, width = queries.shape
    shard_len, model_width = mixed_pieces[0].shape[0], weights[0].shape[0]
    half = jax.ShapeDtypeStruct((rows, width), jnp.bfloat16)
    smem, vmem = pl.BlockSpec(memory_space=pltpu.SMEM), pl.BlockSpec(memory_space=pltpu.VMEM)
    arrays = (queries, keys_all, values_all, lse, *mixed_pieces, *grad_pieces, *weights)
    parts = [jax.ShapeDtypeStruct((shard_len, model_width), jnp.float32)] + [
        jax.ShapeDtypeStruct((shard_len, model_width), jnp.bfloat16)
    ] * (len(mixed_pieces) - 1)
    return pl.pallas_call(
        attend_back_kernel,
        out_shape=(half, half, half, *parts),
        in_specs=[smem, smem] + [vmem] * len(arrays),
        out_specs=(vmem,) * (3 + len(parts)),
        scratch_shapes=[pltpu.VMEM((width, rows), jnp.float32)] * 2,
        compiler_params=pltpu.CompilerParams(vmem_limit_bytes=48 << 20),
        cost_estimate=pl.CostEstimate(
            flops=20 * rows * width * rows,
            bytes_accessed=8 << 20,
            transcendentals=rows * rows * (width // HEAD),
        ),
        name="attend_back",
    )(place.reshape(1), length.reshape(1), *arrays)


def vector_kernel(
    place_ref, one_ref, two_ref, resid_ref, normed_one_ref, normed_two_ref, cot_ref, pre_ref, out_ref
):
    seq_count, _, head_width = out_ref.shape
    model_width = one_ref.shape[1]
    resid = resid_ref[...]
    cot = cot_ref[...].astype(jnp.float32)
    rows = [
        one_ref[...],
        two_ref[...],
        resid * normed_one_ref[...],
        resid,
        cot * normed_two_ref[...],
        cot,
    ]
    out_ref[...] = jnp.zeros_like(out_ref)
    for k, values in enumerate(rows):
        total = jnp.sum(values, axis=0, keepdims=True)
        for j in range(seq_count):
            out_ref[j, 2 + k : 3 + k, :] = total[:, j * head_width : (j + 1) * head_width]
    pre = pre_ref[...].astype(jnp.float32)
    per_place = pre.shape[1] // seq_count // model_width
    totals = [
        jnp.sum(pre[:, k * model_width : (k + 1) * model_width], axis=0, keepdims=True)
        for k in range(seq_count * per_place)
    ]
    for k in range(seq_count):
        owner = (place_ref[0] + seq_count - k) % seq_count
        for i in range(per_place):
            row = 8 + owner * per_place + i
            total = totals[k * per_place + i]
            for j in range(seq_count):
                out_ref[j, pl.ds(row, 1), :] = total[:, j * head_width : (j + 1) * head_width]


def vector_sums(place, seq_count, head_width, *arrays):
    return pl.pallas_call(
        vector_kernel,
        out_shape=jax.ShapeDtypeStruct((seq_count, 16, head_width), jnp.float32),
        in_specs=[pl.BlockSpec(memory_space=pltpu.SMEM)]
        + [pl.BlockSpec(memory_space=pltpu.VMEM)] * len(arrays),
        out_specs=pl.BlockSpec(memory_space=pltpu.VMEM),
        compiler_params=pltpu.CompilerParams(vmem_limit_bytes=32 << 20),
        name="vector_sums",
    )(place.reshape(1), *arrays)


def on_device(
    tokens,
    cotangent,
    lengths,
    w_attn,
    attn_first,
    attn_second,
    w_ffn,
    ffn_first,
    ffn_second,
    vectors,
    vec_first,
    vec_second,
):
    bf16, f32 = jnp.bfloat16, jnp.float32
    _, shard_len, model_width = tokens.shape
    seq_count, fsdp_count = lax.axis_size("seq"), lax.axis_size("fsdp")
    place, member = lax.axis_index("seq"), lax.axis_index("fsdp")
    _, row_shard, head_width = w_attn.shape
    hidden_shard = w_ffn.shape[2]
    vec_rows, vec_shard = vectors.shape
    token_rows = tokens.reshape(shard_len, model_width)
    cot_half = cotangent.reshape(shard_len, model_width)
    cot_rows = cot_half.astype(f32)
    bits = list(range(fsdp_count.bit_length() - 1))

    own_shard = jnp.concatenate([w_ffn[0], w_ffn[1], w_attn[3]], axis=1).astype(bf16)
    early_shard = jnp.concatenate([w_ffn[0], w_attn[3]], axis=1).astype(bf16)
    late_shard = w_ffn[1].astype(bf16)
    vec_placed = lax.dynamic_update_slice(
        jnp.zeros((16, head_width), bf16), vectors.astype(bf16), (0, member * vec_shard)
    )
    qkv_shard = jnp.concatenate(
        [w_attn[:3].astype(bf16).reshape(3 * row_shard, head_width), vec_placed], axis=0
    )
    own_all = lax.all_gather(own_shard, "fsdp", axis=0, tiled=True)
    token_pieces = gather_behind(token_rows)
    early_pieces = gather_behind(after(early_shard, token_pieces[1]))
    qkv_all = lax.all_gather(qkv_shard, "fsdp", axis=0, tiled=False)
    early_all = lax.all_gather(
        jnp.concatenate(
            [piece[:, :hidden_shard] for piece in early_pieces[1:]]
            + [piece[:, hidden_shard:] for piece in early_pieces[1:]],
            axis=1,
        ),
        "fsdp",
        axis=0,
        tiled=True,
    )
    late_pieces = gather_behind(after(late_shard, early_pieces[1]))[1:]

    def times(left, parts):
        return jnp.concatenate(
            [jnp.dot(left, part, preferred_element_type=f32) for part in parts], axis=1
        )

    def times_t(left, parts):
        width = parts[0].shape[1]
        return dot_right_t(left[:, :width], parts[0]) + dot_right_t(left[:, width:], parts[1])

    w_qkv = [
        qkv_all[:, i * row_shard : (i + 1) * row_shard].reshape(model_width, head_width)
        for i in range(3)
    ]
    vec_own = jnp.sum(qkv_all[:, 3 * row_shard :].astype(f32), axis=0)[:vec_rows]
    vec_near = [piece.astype(f32) for piece in gather_behind(vec_own.astype(bf16))]

    def near(order):
        return sum(jnp.where(order == r, piece, 0.0) for r, piece in enumerate(vec_near))

    vec_wide = jnp.concatenate(
        [near((place - j) % seq_count) for j in range(seq_count)], axis=1
    )
    up_bias = turn_blocks(vec_wide[8:12].reshape(seq_count, hidden_shard)).reshape(-1)

    valid_len = lengths[0]
    queries, keys_all, values_all, lse, *mixed_pieces = attend(
        place, valid_len, vec_own[:2], token_pieces, w_qkv
    )
    late_pieces = after(late_pieces, mixed_pieces)
    late_all = lax.all_gather(jnp.concatenate(late_pieces, axis=1), "fsdp", axis=0, tiled=True)
    up_parts = [own_all[:, :hidden_shard], early_all[:, : hidden_shard * (seq_count - 1)]]
    down_parts = [own_all[:, hidden_shard : 2 * hidden_shard], late_all]
    out_parts = [own_all[:, 2 * hidden_shard :], early_all[:, hidden_shard * (seq_count - 1) :]]
    mixed_rows = jnp.concatenate(swap_behind(mixed_pieces), axis=1)

    hidden_one = token_rows.astype(f32) + times_t(mixed_rows, out_parts) + vec_wide[2]
    normed_one, inv_one = layer_norm(hidden_one)
    resid_one = normed_one * vec_wide[4] + vec_wide[5]
    resid_half = resid_one.astype(bf16)
    preact = times(resid_half, up_parts) + up_bias
    activation, gelu_slope = gelu_pair(preact)
    act_half = activation.astype(bf16)
    hidden_two = resid_one + times_t(act_half, down_parts) + vec_wide[3]
    normed_two, inv_two = layer_norm(hidden_two)
    block_out = (normed_two * vec_wide[6] + vec_wide[7]).astype(bf16)
    grad_two = norm_back(cot_rows * vec_wide[6], normed_two, inv_two)
    grad_two_half = grad_two.astype(bf16)

    def outer(left, right):
        return lax.dot_general(
            left, right, (((0,), (0,)), ((), ())), preferred_element_type=f32
        ).astype(bf16)

    def total_of(pieces):
        total = pieces[0].astype(f32)
        for piece in pieces[1:]:
            total = total + piece.astype(f32)
        return total

    def halves_of(pieces):
        return [piece.astype(bf16) for piece in pieces]

    down_local, grad_two_half = lax.optimization_barrier(
        (outer(grad_two_half, act_half), grad_two_half)
    )
    down_part = lax.psum_scatter(down_local, "fsdp", scatter_dimension=0, tiled=True)
    grad_pre_half = (times(grad_two_half, down_parts) * gelu_slope).astype(bf16)
    up_kept, up_sent = halving(
        outer(resid_half, grad_pre_half).reshape(fsdp_count, row_shard, -1), bits[0], True
    )
    up_sent, up_kept, grad_pre_half = lax.optimization_barrier((up_sent, up_kept, grad_pre_half))
    up_received = swapped(up_sent, bits[0])
    grad_resid = grad_two + times_t(grad_pre_half, up_parts)
    grad_one = norm_back(grad_resid * vec_wide[4], normed_one, inv_one)
    grad_one_half = grad_one.astype(bf16)
    grad_mixed = times(grad_one_half, out_parts).astype(bf16)
    grad_pieces = swap_behind(jnp.split(grad_mixed, seq_count, axis=1))

    out_kept, out_sent = halving(
        outer(after(grad_one_half, grad_mixed), mixed_rows).reshape(fsdp_count, row_shard, -1),
        bits[0],
        True,
    )
    out_received = swapped(out_sent, bits[0])
    vec_blocks = vector_sums(
        place,
        seq_count,
        head_width,
        grad_one,
        grad_two,
        grad_resid,
        normed_one,
        normed_two,
        cot_half,
        grad_pre_half,
    )
    vec_order = turn_blocks(vec_blocks)
    vec_moved = swap_behind([vec_order[r] for r in range(seq_count)])
    up_wide = joined(up_kept, up_received)
    out_wide = joined(out_kept, out_received)
    near_places = seq_count // 2
    up_cut, out_cut = near_places * hidden_shard, near_places * head_width
    wide = [
        jnp.concatenate([up_wide[..., :up_cut], out_wide[..., :out_cut]], axis=-1),
        jnp.concatenate([up_wide[..., up_cut:], out_wide[..., out_cut:]], axis=-1),
    ]
    routes = [list(bits[1:]), list(reversed(bits[1:]))]
    wide_moving = []
    for half, route, low in zip(wide, routes, (True, False), strict=True):
        kept, sent = halving(half, route[0], low)
        wide_moving.append((kept, swapped(sent, route[0])))
        grad_pieces = after(grad_pieces, sent)

    *grads, input_own, input_parts = (
        lambda out: (*out[:3], out[3], list(out[4:]))
    )(
        attend_back(
            place,
            valid_len,
            queries,
            keys_all,
            values_all,
            lse,
            mixed_pieces,
            grad_pieces,
            w_qkv,
        )
    )
    input_moved = swap_behind([input_own] + input_parts)
    vec_part = sum(vec_moved)
    vec_line = jnp.arange(16, dtype=jnp.int32)[:, None]
    vec_lines = jnp.where(
        vec_line == 0,
        jnp.sum(grads[0].astype(f32), axis=0)[None],
        jnp.where(vec_line == 1, jnp.sum(grads[2].astype(f32), axis=0)[None], vec_part),
    )
    token_all = jnp.concatenate(token_pieces, axis=0)
    qkv_blocks = jnp.concatenate(
        [
            lax.dot_general(
                token_all, grad, (((0,), (0,)), ((), ())), preferred_element_type=f32
            ).reshape(fsdp_count, row_shard, head_width)
            for grad in after(grads, input_parts)
        ]
        + [jnp.broadcast_to(vec_lines[None], (fsdp_count, 16, head_width))],
        axis=1,
    )

    qkv_kept, qkv_sent = halving(qkv_blocks, bits[0], True)
    qkv_received = swapped(qkv_sent, bits[0])
    step = qkv_sent
    for at in range(1, len(bits)):
        moving = []
        for (kept, received), route, low in zip(wide_moving, routes, (True, False), strict=True):
            received = after(received, step)
            half = joined(kept, received)
            if at < len(bits) - 1:
                kept, sent = halving(half, route[at], low)
                moving.append((kept, swapped(sent, route[at])))
                step = sent
            else:
                moving.append(half[0])
        wide_moving = moving
        if at < len(bits) - 1:
            qkv_half = joined(qkv_kept, after(qkv_received, step))
            qkv_kept, qkv_sent = halving(qkv_half, bits[at], True)
            qkv_received = swapped(qkv_sent, bits[at])
            step = qkv_sent

    def place_pieces(half, count):
        ups, outs = half[:, : count * hidden_shard], half[:, count * hidden_shard :]
        return [
            jnp.concatenate(
                [
                    ups[:, r * hidden_shard : (r + 1) * hidden_shard],
                    outs[:, r * head_width : (r + 1) * head_width],
                ],
                axis=1,
            )
            for r in range(count)
        ]

    wide_pieces = place_pieces(wide_moving[0], near_places) + place_pieces(
        wide_moving[1], seq_count - near_places
    )
    wide_sent = halves_of(wide_pieces[1:])
    wide_moved = swap_behind([wide_pieces[0]] + wide_sent)
    down_pieces = jnp.split(after(down_part, wide_sent), seq_count, axis=1)
    down_moved = swap_behind(down_pieces)
    step = down_pieces
    qkv_half = joined(qkv_kept, after(qkv_received, step))
    qkv_kept, qkv_sent = halving(qkv_half, bits[-1], True)
    qkv_sum = joined(qkv_kept, swapped(qkv_sent, bits[-1]))[0]
    up_out_sum = total_of([wide_moved[0]] + after(wide_moved[1:], qkv_sum))
    down_sum = total_of([down_moved[0]] + after(down_moved[1:], up_out_sum))
    input_grad = grad_one + total_of([input_moved[0]] + after(input_moved[1:], down_sum))

    token_total = shard_len * seq_count * fsdp_count
    grad_scale = float(token_total) ** (-0.5)
    attn_grad = grad_scale * jnp.concatenate(
        [
            qkv_sum[: 3 * row_shard].reshape(3, row_shard, head_width),
            up_out_sum[None, :, hidden_shard:],
        ],
        axis=0,
    )
    ffn_grad = grad_scale * jnp.stack([up_out_sum[:, :hidden_shard], down_sum])
    vec_grad = grad_scale * lax.dynamic_slice(
        qkv_sum[3 * row_shard :], (0, member * vec_shard), (vec_rows, vec_shard)
    )
    attn_new, attn_one, attn_two = adam_step(
        w_attn, attn_grad, attn_first, attn_second, WEIGHT_DECAY
    )
    ffn_new, ffn_one, ffn_two = adam_step(w_ffn, ffn_grad, ffn_first, ffn_second, WEIGHT_DECAY)
    vec_new, vec_one, vec_two = adam_step(vectors, vec_grad, vec_first, vec_second, 0.0)
    return (
        block_out.reshape(tokens.shape),
        input_grad.reshape(tokens.shape),
        attn_grad,
        ffn_grad,
        vec_grad,
        attn_new,
        attn_one,
        attn_two,
        ffn_new,
        ffn_one,
        ffn_two,
        vec_new,
        vec_one,
        vec_two,
    )


def solution(mesh):
    placed = (
        P("fsdp", "seq", None),
        P("fsdp", "seq", None),
        P("fsdp"),
        P(None, "fsdp", "seq"),
        P(None, "fsdp", "seq"),
        P(None, "fsdp", "seq"),
        P(None, "fsdp", "seq"),
        P(None, "fsdp", "seq"),
        P(None, "fsdp", "seq"),
        P(None, ("seq", "fsdp")),
        P(None, ("seq", "fsdp")),
        P(None, ("seq", "fsdp")),
    )
    return jax.shard_map(
        on_device,
        mesh=mesh,
        in_specs=placed,
        out_specs=(
            P("fsdp", "seq", None),
            P("fsdp", "seq", None),
            P(None, "fsdp", "seq"),
            P(None, "fsdp", "seq"),
            P(None, ("seq", "fsdp")),
            P(None, "fsdp", "seq"),
            P(None, "fsdp", "seq"),
            P(None, "fsdp", "seq"),
            P(None, "fsdp", "seq"),
            P(None, "fsdp", "seq"),
            P(None, "fsdp", "seq"),
            P(None, ("seq", "fsdp")),
            P(None, ("seq", "fsdp")),
            P(None, ("seq", "fsdp")),
        ),
        check_vma=False,
    )
```

```python
import math

import jax
import jax.numpy as jnp
from jax import lax
from jax.experimental import pallas as pl
from jax.experimental.pallas import tpu as pltpu
from jax.sharding import PartitionSpec as P


HEAD = 64
STEP = 3
SCORE_SCALE = 1.0 / math.sqrt(HEAD)


EPS_NORM = 1e-12
ADAM_RATE = 0.005
BETA_ONE = 0.9
BETA_TWO = 0.999
ADAM_EPS = 1e-08
WEIGHT_DECAY = 0.01


def layer_norm(values):
    center = values - jnp.mean(values, axis=-1, keepdims=True)
    inv_scale = lax.rsqrt(jnp.mean(center * center, axis=-1, keepdims=True) + EPS_NORM)
    return (center * inv_scale, inv_scale)


def norm_back(grad_normed, normed, inv_scale):
    return inv_scale * (
        grad_normed
        - jnp.mean(grad_normed, axis=-1, keepdims=True)
        - normed * jnp.mean(grad_normed * normed, axis=-1, keepdims=True)
    )


def gelu_pair(preact):
    normal_cdf = 0.5 * (1.0 + jax.scipy.special.erf(preact * (1.0 / math.sqrt(2.0))))
    density = jnp.exp(-0.5 * preact * preact) * (1.0 / math.sqrt(2.0 * math.pi))
    return (preact * normal_cdf, normal_cdf + preact * density)


def dot_right_t(left, right):
    return lax.dot_general(
        left, right, (((1,), (1,)), ((), ())), preferred_element_type=jnp.float32
    )


def from_behind(piece, distance):
    count = lax.axis_size("seq")
    if distance % count == 0:
        return piece
    return lax.ppermute(piece, "seq", [(i, (i + distance) % count) for i in range(count)])


def gather_behind(piece):
    return [from_behind(piece, r) for r in range(lax.axis_size("seq"))]


def swap_behind(pieces):
    count = len(pieces)
    return [from_behind(pieces[(-r) % count], r) for r in range(count)]


def turn_blocks(blocks):
    count = blocks.shape[0]
    place = lax.axis_index("seq")
    order = (place - jnp.arange(count, dtype=jnp.int32)) % count
    mask = order[:, None] == jnp.arange(count, dtype=jnp.int32)[None, :]
    mask = mask.reshape((count, count) + (1,) * (blocks.ndim - 1))
    return jnp.sum(jnp.where(mask, blocks[None], jnp.zeros((), blocks.dtype)), axis=1)


def adam_step(parameter, gradient, moment_one, moment_two, decay_rate):
    one_new = BETA_ONE * moment_one + (1.0 - BETA_ONE) * gradient
    two_new = BETA_TWO * moment_two + (1.0 - BETA_TWO) * gradient * gradient
    one_hat = one_new / (1.0 - BETA_ONE**STEP)
    two_hat = two_new / (1.0 - BETA_TWO**STEP)
    update = one_hat / (jnp.sqrt(two_hat) + ADAM_EPS)
    return (parameter - ADAM_RATE * (update + decay_rate * parameter), one_new, two_new)


def after(values, *earlier):
    return lax.optimization_barrier((values, earlier))[0]


def halving(blocks, bit, from_low):
    count = blocks.shape[0]
    own = (lax.axis_index("fsdp") >> bit) & 1
    split = (count // 2, 2) if from_low else (2, count // 2)
    axis = 1 if from_low else 0
    view = blocks.reshape(split + blocks.shape[1:])
    kept = lax.dynamic_index_in_dim(view, own, axis, keepdims=False)
    sent = lax.dynamic_index_in_dim(view, 1 - own, axis, keepdims=False)
    return kept, sent.astype(jnp.bfloat16)


def swapped(sent, bit):
    pairs = [(i, i ^ (1 << bit)) for i in range(lax.axis_size("fsdp"))]
    return lax.ppermute(sent, "fsdp", pairs)


def joined(kept, received):
    return kept.astype(jnp.float32) + received.astype(jnp.float32)


def attend_kernel(
    place_ref, length_ref, bias_ref, *refs
):
    count = (len(refs) - 3 - 4) // 2
    token_refs, weight_refs = refs[:count], refs[count : count + 3]
    q_ref, k_ref, v_ref, lse_ref = refs[count + 3 : count + 7]
    mixed_refs = refs[count + 7 :]
    shard_len = token_refs[0].shape[0]
    _, width = q_ref.shape
    for r, token_ref in enumerate(token_refs):
        piece = token_ref[...]
        for k, (weight_ref, out_ref) in enumerate(
            zip(weight_refs, (q_ref, k_ref, v_ref), strict=True)
        ):
            out = jnp.dot(piece, weight_ref[...], preferred_element_type=jnp.float32)
            if k != 1:
                out = out + bias_ref[k // 2 : k // 2 + 1, :]
            out_ref[r * shard_len : (r + 1) * shard_len, :] = out.astype(jnp.bfloat16)
    masked = key_mask(place_ref[0], length_ref[0], count, shard_len)

    for i, mixed_ref in enumerate(mixed_refs):
        at = slice(i * shard_len, (i + 1) * shard_len)
        queries = q_ref[at, :]
        mixed = []
        for h in range(width // HEAD):
            cols = slice(h * HEAD, (h + 1) * HEAD)
            scores = dot_right_t(queries[:, cols] * SCORE_SCALE, k_ref[:, cols]) + masked
            top = jnp.max(scores, axis=1, keepdims=True)
            raised = jnp.exp(scores - top)
            total = jnp.sum(raised, axis=1, keepdims=True)
            probs = (raised * (1.0 / total)).astype(jnp.bfloat16)
            mixed.append(jnp.dot(probs, v_ref[:, cols], preferred_element_type=jnp.float32))
            lse_ref[at, h : h + 1] = top + jnp.log(total)
        mixed_ref[...] = jnp.concatenate(mixed, axis=1).astype(jnp.bfloat16)


def key_mask(place, length, count, shard_len):
    column = lax.broadcasted_iota(jnp.int32, (1, shard_len), 1)
    pieces = []
    for r in range(count):
        start = lax.rem(place + count - r, count) * shard_len
        pieces.append(jnp.where(column + start < length, 0.0, -jnp.inf))
    return jnp.concatenate(pieces, axis=1)


def attend(place, length, bias, token_pieces, weights):
    shard_len = token_pieces[0].shape[0]
    rows, width = shard_len * len(token_pieces), weights[0].shape[1]
    half = jax.ShapeDtypeStruct((rows, width), jnp.bfloat16)
    smem, vmem = pl.BlockSpec(memory_space=pltpu.SMEM), pl.BlockSpec(memory_space=pltpu.VMEM)
    arrays = (bias, *token_pieces, *weights)
    return pl.pallas_call(
        attend_kernel,
        out_shape=(half, half, half, jax.ShapeDtypeStruct((rows, 8), jnp.float32))
        + (jax.ShapeDtypeStruct((shard_len, width), jnp.bfloat16),) * len(token_pieces),
        in_specs=[smem, smem] + [vmem] * len(arrays),
        out_specs=(vmem,) * (4 + len(token_pieces)),
        compiler_params=pltpu.CompilerParams(vmem_limit_bytes=40 << 20),
        cost_estimate=pl.CostEstimate(
            flops=2 * rows * width * (3 * weights[0].shape[0] + 8 * rows),
            bytes_accessed=8 << 20,
            transcendentals=rows * rows * (width // HEAD),
        ),
        name="attend",
    )(place.reshape(1), length.reshape(1), *arrays)


def attend_back_kernel(
    place_ref,
    length_ref,
    q_ref,
    k_ref,
    v_ref,
    lse_ref,
    *refs,
):
    count = (len(refs) - 3 - 2 - 2) // 3
    mixed_refs, grad_refs = refs[:count], refs[count : 2 * count]
    weight_refs, refs = refs[2 * count : 2 * count + 3], refs[2 * count + 3 :]
    all_ref, sums_ref = refs[:2]
    part_refs = refs[2 : 2 + count]
    dk_sum, dv_sum = refs[2 + count :]
    shard_len = grad_refs[0].shape[0]
    _, width = q_ref.shape
    masked = key_mask(place_ref[0], length_ref[0], count, shard_len)
    for i, (grad_ref, mixed_ref) in enumerate(zip(grad_refs, mixed_refs, strict=True)):
        at = slice(i * shard_len, (i + 1) * shard_len)
        queries, grad = q_ref[at, :], grad_ref[...]
        product = grad.astype(jnp.float32) * mixed_ref[...].astype(jnp.float32)
        parts = []
        for h in range(width // HEAD):
            cols = slice(h * HEAD, (h + 1) * HEAD)
            head_q, head_grad = queries[:, cols], grad[:, cols]
            scores = dot_right_t(head_q * SCORE_SCALE, k_ref[:, cols]) + masked
            probs = jnp.exp(scores - lse_ref[at, h : h + 1])
            delta = jnp.sum(product[:, cols], axis=1, keepdims=True)
            grad_probs = dot_right_t(head_grad, v_ref[:, cols])
            grad_scores = (probs * (grad_probs - delta)).astype(jnp.bfloat16)
            parts.append(
                jnp.dot(grad_scores, k_ref[:, cols], preferred_element_type=jnp.float32)
                * SCORE_SCALE
            )
            dk = jnp.dot(head_q.T, grad_scores, preferred_element_type=jnp.float32)
            dv = jnp.dot(head_grad.T, probs.astype(jnp.bfloat16), preferred_element_type=jnp.float32)
            if i == 0:
                dk_sum[cols, :] = dk
                dv_sum[cols, :] = dv
            else:
                dk_sum[cols, :] += dk
                dv_sum[cols, :] += dv
        all_ref[at, :width] = jnp.concatenate(parts, axis=1).astype(jnp.bfloat16)
    all_ref[:, width : 2 * width] = (dk_sum[...].T * SCORE_SCALE).astype(jnp.bfloat16)
    all_ref[:, 2 * width :] = dv_sum[...].T.astype(jnp.bfloat16)
    sums_ref[...] = jnp.zeros_like(sums_ref)
    sums_ref[:1, :] = jnp.sum(all_ref[...].astype(jnp.float32), axis=0, keepdims=True)
    for i, part_ref in enumerate(part_refs):
        at = slice(i * shard_len, (i + 1) * shard_len)
        part = dot_right_t(all_ref[at, :width], weight_refs[0][...])
        part = part + dot_right_t(all_ref[at, width : 2 * width], weight_refs[1][...])
        part = part + dot_right_t(all_ref[at, 2 * width :], weight_refs[2][...])
        part_ref[...] = part.astype(part_ref.dtype)


def attend_back(
    place, length, queries, keys_all, values_all, lse, mixed_pieces, grad_pieces, weights
):
    rows, width = queries.shape
    shard_len, model_width = mixed_pieces[0].shape[0], weights[0].shape[0]
    smem, vmem = pl.BlockSpec(memory_space=pltpu.SMEM), pl.BlockSpec(memory_space=pltpu.VMEM)
    arrays = (queries, keys_all, values_all, lse, *mixed_pieces, *grad_pieces, *weights)
    parts = [jax.ShapeDtypeStruct((shard_len, model_width), jnp.float32)] + [
        jax.ShapeDtypeStruct((shard_len, model_width), jnp.bfloat16)
    ] * (len(mixed_pieces) - 1)
    return pl.pallas_call(
        attend_back_kernel,
        out_shape=(
            jax.ShapeDtypeStruct((rows, 3 * width), jnp.bfloat16),
            jax.ShapeDtypeStruct((16, 3 * width), jnp.float32),
            *parts,
        ),
        in_specs=[smem, smem] + [vmem] * len(arrays),
        out_specs=(vmem,) * (2 + len(parts)),
        scratch_shapes=[pltpu.VMEM((width, rows), jnp.float32)] * 2,
        compiler_params=pltpu.CompilerParams(vmem_limit_bytes=48 << 20),
        cost_estimate=pl.CostEstimate(
            flops=20 * rows * width * rows,
            bytes_accessed=8 << 20,
            transcendentals=rows * rows * (width // HEAD),
        ),
        name="attend_back",
    )(place.reshape(1), length.reshape(1), *arrays)


def vector_kernel(
    place_ref, one_ref, two_ref, resid_ref, normed_one_ref, normed_two_ref, cot_ref, pre_ref, out_ref
):
    seq_count, _, head_width = out_ref.shape
    model_width = one_ref.shape[1]
    resid = resid_ref[...]
    cot = cot_ref[...].astype(jnp.float32)
    rows = [
        one_ref[...],
        two_ref[...],
        resid * normed_one_ref[...],
        resid,
        cot * normed_two_ref[...],
        cot,
    ]
    out_ref[...] = jnp.zeros_like(out_ref)
    for k, values in enumerate(rows):
        total = jnp.sum(values, axis=0, keepdims=True)
        for j in range(seq_count):
            out_ref[j, 2 + k : 3 + k, :] = total[:, j * head_width : (j + 1) * head_width]
    pre = pre_ref[...].astype(jnp.float32)
    per_place = pre.shape[1] // seq_count // model_width
    totals = [
        jnp.sum(pre[:, k * model_width : (k + 1) * model_width], axis=0, keepdims=True)
        for k in range(seq_count * per_place)
    ]
    for k in range(seq_count):
        owner = (place_ref[0] + seq_count - k) % seq_count
        for i in range(per_place):
            row = 8 + owner * per_place + i
            total = totals[k * per_place + i]
            for j in range(seq_count):
                out_ref[j, pl.ds(row, 1), :] = total[:, j * head_width : (j + 1) * head_width]


def vector_sums(place, seq_count, head_width, *arrays):
    return pl.pallas_call(
        vector_kernel,
        out_shape=jax.ShapeDtypeStruct((seq_count, 16, head_width), jnp.float32),
        in_specs=[pl.BlockSpec(memory_space=pltpu.SMEM)]
        + [pl.BlockSpec(memory_space=pltpu.VMEM)] * len(arrays),
        out_specs=pl.BlockSpec(memory_space=pltpu.VMEM),
        compiler_params=pltpu.CompilerParams(vmem_limit_bytes=32 << 20),
        name="vector_sums",
    )(place.reshape(1), *arrays)


def layer(
    tokens,
    cotangent,
    lengths,
    w_attn,
    attn_first,
    attn_second,
    w_ffn,
    ffn_first,
    ffn_second,
    vectors,
    vec_first,
    vec_second,
):
    bf16, f32 = jnp.bfloat16, jnp.float32
    _, shard_len, model_width = tokens.shape
    seq_count, fsdp_count = lax.axis_size("seq"), lax.axis_size("fsdp")
    place, member = lax.axis_index("seq"), lax.axis_index("fsdp")
    _, row_shard, head_width = w_attn.shape
    hidden_shard = w_ffn.shape[2]
    vec_rows, vec_shard = vectors.shape
    token_rows = tokens.reshape(shard_len, model_width)
    cot_half = cotangent.reshape(shard_len, model_width)
    cot_rows = cot_half.astype(f32)
    bits = list(range(fsdp_count.bit_length() - 1))

    own_shard = jnp.concatenate([w_ffn[0], w_ffn[1], w_attn[3]], axis=1).astype(bf16)
    early_shard = jnp.concatenate([w_ffn[0], w_attn[3]], axis=1).astype(bf16)
    late_shard = w_ffn[1].astype(bf16)
    vec_placed = lax.dynamic_update_slice(
        jnp.zeros((16, head_width), bf16), vectors.astype(bf16), (0, member * vec_shard)
    )
    qkv_shard = jnp.concatenate(
        [w_attn[:3].astype(bf16).reshape(3 * row_shard, head_width), vec_placed], axis=0
    )
    own_all = lax.all_gather(own_shard, "fsdp", axis=0, tiled=True)
    token_pieces = gather_behind(token_rows)
    early_pieces = gather_behind(early_shard)
    qkv_all = lax.all_gather(qkv_shard, "fsdp", axis=0, tiled=False)
    early_pieces = after(early_pieces, qkv_all)
    early_cat = jnp.concatenate(
        [piece[:, :hidden_shard] for piece in early_pieces[1:]]
        + [piece[:, hidden_shard:] for piece in early_pieces[1:]],
        axis=1,
    )
    early_all = lax.all_gather(early_cat, "fsdp", axis=0, tiled=True)
    late_pieces = gather_behind(after(late_shard, early_pieces[1]))[1:]

    def times(left, parts):
        return jnp.concatenate(
            [jnp.dot(left, part, preferred_element_type=f32) for part in parts], axis=1
        )

    def times_t(left, parts):
        width = parts[0].shape[1]
        return dot_right_t(left[:, :width], parts[0]) + dot_right_t(left[:, width:], parts[1])

    w_qkv = [
        qkv_all[:, i * row_shard : (i + 1) * row_shard].reshape(model_width, head_width)
        for i in range(3)
    ]
    vec_own = jnp.sum(qkv_all[:, 3 * row_shard :].astype(f32), axis=0)[:vec_rows]
    vec_near = [piece.astype(f32) for piece in gather_behind(vec_own.astype(bf16))]

    def near(order):
        return sum(jnp.where(order == r, piece, 0.0) for r, piece in enumerate(vec_near))

    vec_wide = jnp.concatenate(
        [near((place - j) % seq_count) for j in range(seq_count)], axis=1
    )
    up_bias = turn_blocks(vec_wide[8:12].reshape(seq_count, hidden_shard)).reshape(-1)

    valid_len = lengths[0]
    queries, keys_all, values_all, lse, *mixed_pieces = attend(
        place, valid_len, vec_own[:2], token_pieces, w_qkv
    )
    late_pieces = after(late_pieces, mixed_pieces)
    late_all = lax.all_gather(jnp.concatenate(late_pieces, axis=1), "fsdp", axis=0, tiled=True)
    up_parts = [own_all[:, :hidden_shard], early_all[:, : hidden_shard * (seq_count - 1)]]
    down_parts = [own_all[:, hidden_shard : 2 * hidden_shard], late_all]
    out_parts = [own_all[:, 2 * hidden_shard :], early_all[:, hidden_shard * (seq_count - 1) :]]
    mixed_rows = jnp.concatenate(swap_behind(mixed_pieces), axis=1)

    hidden_one = token_rows.astype(f32) + times_t(mixed_rows, out_parts) + vec_wide[2]
    normed_one, inv_one = layer_norm(hidden_one)
    resid_one = normed_one * vec_wide[4] + vec_wide[5]
    resid_half = resid_one.astype(bf16)
    preact = times(resid_half, up_parts) + up_bias
    activation, gelu_slope = gelu_pair(preact)
    act_half = activation.astype(bf16)
    hidden_two = resid_one + times_t(act_half, down_parts) + vec_wide[3]
    normed_two, inv_two = layer_norm(hidden_two)
    block_out = (normed_two * vec_wide[6] + vec_wide[7]).astype(bf16)
    grad_two = norm_back(cot_rows * vec_wide[6], normed_two, inv_two)
    grad_two_half = grad_two.astype(bf16)

    def outer(left, right):
        return lax.dot_general(
            left, right, (((0,), (0,)), ((), ())), preferred_element_type=f32
        ).astype(bf16)

    def total_of(pieces):
        total = pieces[0].astype(f32)
        for piece in pieces[1:]:
            total = total + piece.astype(f32)
        return total

    def halves_of(pieces):
        return [piece.astype(bf16) for piece in pieces]

    down_local, grad_two_half = lax.optimization_barrier(
        (outer(grad_two_half, act_half), grad_two_half)
    )
    down_part = lax.psum_scatter(down_local, "fsdp", scatter_dimension=0, tiled=True)
    grad_pre_half = (times(grad_two_half, down_parts) * gelu_slope).astype(bf16)
    up_kept, up_sent = halving(
        outer(resid_half, grad_pre_half).reshape(fsdp_count, row_shard, -1), bits[0], True
    )
    up_sent, up_kept, grad_pre_half = lax.optimization_barrier((up_sent, up_kept, grad_pre_half))
    up_received = swapped(up_sent, bits[0])
    grad_resid = grad_two + times_t(grad_pre_half, up_parts)
    grad_one = norm_back(grad_resid * vec_wide[4], normed_one, inv_one)
    grad_one_half = grad_one.astype(bf16)
    grad_mixed = times(grad_one_half, out_parts).astype(bf16)
    grad_pieces = swap_behind(jnp.split(grad_mixed, seq_count, axis=1))

    out_kept, out_sent = halving(
        outer(after(grad_one_half, grad_mixed), mixed_rows).reshape(fsdp_count, row_shard, -1),
        bits[0],
        True,
    )
    out_received = swapped(out_sent, bits[0])
    vec_blocks = vector_sums(
        place,
        seq_count,
        head_width,
        grad_one,
        grad_two,
        grad_resid,
        normed_one,
        normed_two,
        cot_half,
        grad_pre_half,
    )
    vec_order = turn_blocks(vec_blocks)
    vec_moved = swap_behind([vec_order[r] for r in range(seq_count)])
    up_wide = joined(up_kept, up_received)
    out_wide = joined(out_kept, out_received)
    near_places = seq_count // 2
    up_cut, out_cut = near_places * hidden_shard, near_places * head_width
    wide = [
        jnp.concatenate([up_wide[..., :up_cut], out_wide[..., :out_cut]], axis=-1),
        jnp.concatenate([up_wide[..., up_cut:], out_wide[..., out_cut:]], axis=-1),
    ]
    routes = [list(bits[1:]), list(reversed(bits[1:]))]
    wide_moving = []
    for half, route, low in zip(wide, routes, (True, False), strict=True):
        kept, sent = halving(half, route[0], low)
        wide_moving.append((kept, swapped(sent, route[0])))
        grad_pieces = after(grad_pieces, sent)

    grad_qkv, head_sums, input_own, *input_parts = attend_back(
        place,
        valid_len,
        queries,
        keys_all,
        values_all,
        lse,
        mixed_pieces,
        grad_pieces,
        w_qkv,
    )
    input_moved = swap_behind([input_own, *input_parts])
    vec_part = sum(vec_moved)
    vec_lines = jnp.concatenate(
        [head_sums[:1, :head_width], head_sums[:1, 2 * head_width :], vec_part[2:]], axis=0
    )
    vec_lines = jnp.pad(vec_lines, ((0, 0), (0, 2 * head_width)))
    token_all = jnp.concatenate(token_pieces, axis=0)
    qkv_local = lax.dot_general(
        token_all, grad_qkv, (((0,), (0,)), ((), ())), preferred_element_type=f32
    ).astype(bf16)
    qkv_blocks = jnp.concatenate(
        [
            qkv_local.reshape(fsdp_count, row_shard, 3 * head_width),
            jnp.broadcast_to(
                vec_lines.astype(bf16)[None], (fsdp_count, 16, 3 * head_width)
            ),
        ],
        axis=1,
    )

    def place_pieces(half, count):
        ups, outs = half[:, : count * hidden_shard], half[:, count * hidden_shard :]
        return [
            jnp.concatenate(
                [
                    ups[:, r * hidden_shard : (r + 1) * hidden_shard],
                    outs[:, r * head_width : (r + 1) * head_width],
                ],
                axis=1,
            )
            for r in range(count)
        ]

    qkv_kept, qkv_sent = halving(qkv_blocks, bits[0], True)
    qkv_received = swapped(qkv_sent, bits[0])
    step = qkv_sent
    down_moved = None
    for at in range(1, len(bits)):
        moving = []
        for (kept, received), route, low in zip(wide_moving, routes, (True, False), strict=True):
            half = joined(kept, after(received, step))
            if at < len(bits) - 1:
                kept, sent = halving(half, route[at], low)
                moving.append((kept, swapped(sent, route[at])))
                step = sent
            else:
                moving.append(half[0])
        wide_moving = moving
        if down_moved is None:
            down_pieces = jnp.split(after(down_part, step), seq_count, axis=1)
            down_moved = swap_behind(down_pieces)
            step = down_pieces
        if at < len(bits) - 1:
            qkv_half = joined(qkv_kept, after(qkv_received, step))
            qkv_kept, qkv_sent = halving(qkv_half, bits[at], True)
            qkv_received = swapped(qkv_sent, bits[at])
            step = qkv_sent
    wide_pieces = place_pieces(wide_moving[0], near_places) + place_pieces(
        wide_moving[1], seq_count - near_places
    )
    wide_sent = halves_of(wide_pieces[1:])
    wide_moved = swap_behind([wide_pieces[0]] + wide_sent)
    qkv_half = joined(qkv_kept, after(qkv_received, wide_sent))
    qkv_kept, qkv_sent = halving(qkv_half, bits[-1], True)
    qkv_sum = joined(qkv_kept, swapped(qkv_sent, bits[-1]))[0]
    down_sum = total_of([down_moved[0]] + after(down_moved[1:], qkv_sum))
    input_grad = grad_one + total_of([input_moved[0]] + after(input_moved[1:], down_sum))
    up_out_sum = total_of([wide_moved[0]] + after(wide_moved[1:], input_grad))

    token_total = shard_len * seq_count * fsdp_count
    grad_scale = float(token_total) ** (-0.5)
    attn_grad = grad_scale * jnp.concatenate(
        [
            qkv_sum[:row_shard].reshape(row_shard, 3, head_width).transpose(1, 0, 2),
            up_out_sum[None, :, hidden_shard:],
        ],
        axis=0,
    )
    ffn_grad = grad_scale * jnp.stack([up_out_sum[:, :hidden_shard], down_sum])
    vec_grad = grad_scale * lax.dynamic_slice(
        qkv_sum[row_shard:], (0, member * vec_shard), (vec_rows, vec_shard)
    )
    attn_new, attn_one, attn_two = adam_step(
        w_attn, attn_grad, attn_first, attn_second, WEIGHT_DECAY
    )
    ffn_new, ffn_one, ffn_two = adam_step(w_ffn, ffn_grad, ffn_first, ffn_second, WEIGHT_DECAY)
    vec_new, vec_one, vec_two = adam_step(vectors, vec_grad, vec_first, vec_second, 0.0)
    return (
        block_out.reshape(tokens.shape),
        input_grad.reshape(tokens.shape),
        attn_grad,
        ffn_grad,
        vec_grad,
        attn_new,
        attn_one,
        attn_two,
        ffn_new,
        ffn_one,
        ffn_two,
        vec_new,
        vec_one,
        vec_two,
    )


def solution(mesh):
    placed = (
        P("fsdp", "seq", None),
        P("fsdp", "seq", None),
        P("fsdp"),
        P(None, "fsdp", "seq"),
        P(None, "fsdp", "seq"),
        P(None, "fsdp", "seq"),
        P(None, "fsdp", "seq"),
        P(None, "fsdp", "seq"),
        P(None, "fsdp", "seq"),
        P(None, ("seq", "fsdp")),
        P(None, ("seq", "fsdp")),
        P(None, ("seq", "fsdp")),
    )
    return jax.shard_map(
        layer,
        mesh=mesh,
        in_specs=placed,
        out_specs=(
            P("fsdp", "seq", None),
            P("fsdp", "seq", None),
            P(None, "fsdp", "seq"),
            P(None, "fsdp", "seq"),
            P(None, ("seq", "fsdp")),
            P(None, "fsdp", "seq"),
            P(None, "fsdp", "seq"),
            P(None, "fsdp", "seq"),
            P(None, "fsdp", "seq"),
            P(None, "fsdp", "seq"),
            P(None, "fsdp", "seq"),
            P(None, ("seq", "fsdp")),
            P(None, ("seq", "fsdp")),
            P(None, ("seq", "fsdp")),
        ),
        check_vma=False,
    )
```

```python
import math

import jax
import jax.numpy as jnp
from jax import lax
from jax.experimental import pallas as pl
from jax.experimental.layout import Layout, with_layout_constraint
from jax.experimental.pallas import tpu as pltpu
from jax.sharding import PartitionSpec as P


HEAD = 64
STEP = 3
SCORE_SCALE = 1.0 / math.sqrt(HEAD)


EPS_NORM = 1e-12
ADAM_RATE = 0.005
BETA_ONE = 0.9
BETA_TWO = 0.999
ADAM_EPS = 1e-08
WEIGHT_DECAY = 0.01


def layer_norm(values):
    center = values - jnp.mean(values, axis=-1, keepdims=True)
    inv_scale = lax.rsqrt(jnp.mean(center * center, axis=-1, keepdims=True) + EPS_NORM)
    return (center * inv_scale, inv_scale)


def norm_back(grad_normed, normed, inv_scale):
    return inv_scale * (
        grad_normed
        - jnp.mean(grad_normed, axis=-1, keepdims=True)
        - normed * jnp.mean(grad_normed * normed, axis=-1, keepdims=True)
    )


def gelu_pair(preact):
    normal_cdf = 0.5 * (1.0 + jax.scipy.special.erf(preact * (1.0 / math.sqrt(2.0))))
    density = jnp.exp(-0.5 * preact * preact) * (1.0 / math.sqrt(2.0 * math.pi))
    return (preact * normal_cdf, normal_cdf + preact * density)


def dot_right_t(left, right):
    return lax.dot_general(
        left, right, (((1,), (1,)), ((), ())), preferred_element_type=jnp.float32
    )


def from_behind(piece, distance):
    count = lax.axis_size("seq")
    if distance % count == 0:
        return piece
    return lax.ppermute(piece, "seq", [(i, (i + distance) % count) for i in range(count)])


def gather_behind(piece):
    return [from_behind(piece, r) for r in range(lax.axis_size("seq"))]


def swap_behind(pieces):
    count = len(pieces)
    return [from_behind(pieces[(-r) % count], r) for r in range(count)]


def turn_blocks(blocks):
    count = blocks.shape[0]
    place = lax.axis_index("seq")
    order = (place - jnp.arange(count, dtype=jnp.int32)) % count
    mask = order[:, None] == jnp.arange(count, dtype=jnp.int32)[None, :]
    mask = mask.reshape((count, count) + (1,) * (blocks.ndim - 1))
    return jnp.sum(jnp.where(mask, blocks[None], jnp.zeros((), blocks.dtype)), axis=1)


def adam_step(parameter, gradient, moment_one, moment_two, decay_rate):
    one_new = BETA_ONE * moment_one + (1.0 - BETA_ONE) * gradient
    two_new = BETA_TWO * moment_two + (1.0 - BETA_TWO) * gradient * gradient
    one_hat = one_new / (1.0 - BETA_ONE**STEP)
    two_hat = two_new / (1.0 - BETA_TWO**STEP)
    update = one_hat / (jnp.sqrt(two_hat) + ADAM_EPS)
    return (parameter - ADAM_RATE * (update + decay_rate * parameter), one_new, two_new)


def after(values, *earlier):
    return lax.optimization_barrier((values, earlier))[0]


def halving(blocks, bit, from_low):
    count = blocks.shape[0]
    own = (lax.axis_index("fsdp") >> bit) & 1
    split = (count // 2, 2) if from_low else (2, count // 2)
    axis = 1 if from_low else 0
    view = blocks.reshape(split + blocks.shape[1:])
    kept = lax.dynamic_index_in_dim(view, own, axis, keepdims=False)
    sent = lax.dynamic_index_in_dim(view, 1 - own, axis, keepdims=False)
    return kept, sent.astype(jnp.bfloat16)


def swapped(sent, bit):
    pairs = [(i, i ^ (1 << bit)) for i in range(lax.axis_size("fsdp"))]
    return lax.ppermute(sent, "fsdp", pairs)


def joined(kept, received):
    return kept.astype(jnp.float32) + received.astype(jnp.float32)


def attend_kernel(
    place_ref, length_ref, bias_ref, *refs
):
    count = (len(refs) - 3 - 4 - 2) // 2
    token_refs, weight_refs = refs[:count], refs[count : count + 3]
    q_ref, k_ref, v_ref, lse_ref = refs[count + 3 : count + 7]
    mixed_refs, (mixed_all, token_all) = refs[count + 7 : -2], refs[-2:]
    shard_len = token_refs[0].shape[0]
    _, width = q_ref.shape
    for r, token_ref in enumerate(token_refs):
        token_all[r * shard_len : (r + 1) * shard_len, :] = token_ref[...]

    def project(i, carry):
        at = pl.ds(pl.multiple_of(i * shard_len, shard_len), shard_len)
        piece = token_all[at, :]
        for k, (weight_ref, out_ref) in enumerate(
            zip(weight_refs, (q_ref, k_ref, v_ref), strict=True)
        ):
            out = jnp.dot(piece, weight_ref[...], preferred_element_type=jnp.float32)
            if k != 1:
                out = out + bias_ref[k // 2 : k // 2 + 1, :]
            out_ref[at, :] = out.astype(jnp.bfloat16)
        return carry

    lax.fori_loop(0, count, project, 0)
    masked = key_mask(place_ref[0], length_ref[0], count, shard_len)


    def block(i, carry):
        at = pl.ds(pl.multiple_of(i * shard_len, shard_len), shard_len)
        queries = q_ref[at, :]
        mixed = []
        for h in range(width // HEAD):
            cols = slice(h * HEAD, (h + 1) * HEAD)
            scores = dot_right_t(queries[:, cols] * SCORE_SCALE, k_ref[:, cols]) + masked
            top = jnp.max(scores, axis=1, keepdims=True)
            raised = jnp.exp(scores - top)
            total = jnp.sum(raised, axis=1, keepdims=True)
            probs = (raised * (1.0 / total)).astype(jnp.bfloat16)
            mixed.append(jnp.dot(probs, v_ref[:, cols], preferred_element_type=jnp.float32))
            lse_ref[at, h : h + 1] = top + jnp.log(total)
        mixed_all[at, :] = jnp.concatenate(mixed, axis=1).astype(jnp.bfloat16)
        return carry

    lax.fori_loop(0, count, block, 0)
    for i, mixed_ref in enumerate(mixed_refs):
        mixed_ref[...] = mixed_all[i * shard_len : (i + 1) * shard_len, :]


def key_mask(place, length, count, shard_len):
    column = lax.broadcasted_iota(jnp.int32, (1, shard_len), 1)
    pieces = []
    for r in range(count):
        start = lax.rem(place + count - r, count) * shard_len
        pieces.append(jnp.where(column + start < length, 0.0, -jnp.inf))
    return jnp.concatenate(pieces, axis=1)


def attend(place, length, bias, token_pieces, weights):
    shard_len = token_pieces[0].shape[0]
    rows, width = shard_len * len(token_pieces), weights[0].shape[1]
    half = jax.ShapeDtypeStruct((rows, width), jnp.bfloat16)
    smem, vmem = pl.BlockSpec(memory_space=pltpu.SMEM), pl.BlockSpec(memory_space=pltpu.VMEM)
    arrays = (bias, *token_pieces, *weights)
    return pl.pallas_call(
        attend_kernel,
        out_shape=(half, half, half, jax.ShapeDtypeStruct((rows, 8), jnp.float32))
        + (jax.ShapeDtypeStruct((shard_len, width), jnp.bfloat16),) * len(token_pieces),
        in_specs=[smem, smem] + [vmem] * len(arrays),
        out_specs=(vmem,) * (4 + len(token_pieces)),
        scratch_shapes=[
            pltpu.VMEM((rows, width), jnp.bfloat16),
            pltpu.VMEM((rows, weights[0].shape[0]), jnp.bfloat16),
        ],
        compiler_params=pltpu.CompilerParams(vmem_limit_bytes=40 << 20),
        cost_estimate=pl.CostEstimate(
            flops=2 * rows * width * (3 * weights[0].shape[0] + 8 * rows),
            bytes_accessed=8 << 20,
            transcendentals=rows * rows * (width // HEAD),
        ),
        name="attend",
    )(place.reshape(1), length.reshape(1), *arrays)


def attend_back_kernel(
    place_ref,
    length_ref,
    q_ref,
    k_ref,
    v_ref,
    lse_ref,
    *refs,
):
    count = (len(refs) - 3 - 2 - 5) // 3
    mixed_refs, grad_refs = refs[:count], refs[count : 2 * count]
    weight_refs, refs = refs[2 * count : 2 * count + 3], refs[2 * count + 3 :]
    all_ref, sums_ref = refs[:2]
    part_refs = refs[2 : 2 + count]
    dk_sum, dv_sum, mixed_all, grad_all, part_all = refs[2 + count :]
    shard_len = grad_refs[0].shape[0]
    _, width = q_ref.shape
    masked = key_mask(place_ref[0], length_ref[0], count, shard_len)
    for i in range(count):
        at = slice(i * shard_len, (i + 1) * shard_len)
        mixed_all[at, :] = mixed_refs[i][...]
        grad_all[at, :] = grad_refs[i][...]
    dk_sum[...] = jnp.zeros_like(dk_sum)
    dv_sum[...] = jnp.zeros_like(dv_sum)

    def block(i, carry):
        at = pl.ds(pl.multiple_of(i * shard_len, shard_len), shard_len)
        queries, grad = q_ref[at, :], grad_all[at, :]
        product = grad.astype(jnp.float32) * mixed_all[at, :].astype(jnp.float32)
        parts = []
        for h in range(width // HEAD):
            cols = slice(h * HEAD, (h + 1) * HEAD)
            head_q, head_grad = queries[:, cols], grad[:, cols]
            scores = dot_right_t(head_q * SCORE_SCALE, k_ref[:, cols]) + masked
            probs = jnp.exp(scores - lse_ref[at, h : h + 1])
            delta = jnp.sum(product[:, cols], axis=1, keepdims=True)
            grad_probs = dot_right_t(head_grad, v_ref[:, cols])
            grad_scores = (probs * (grad_probs - delta)).astype(jnp.bfloat16)
            parts.append(
                jnp.dot(grad_scores, k_ref[:, cols], preferred_element_type=jnp.float32)
                * SCORE_SCALE
            )
            dk_sum[cols, :] += jnp.dot(head_q.T, grad_scores, preferred_element_type=jnp.float32)
            dv_sum[cols, :] += jnp.dot(
                head_grad.T, probs.astype(jnp.bfloat16), preferred_element_type=jnp.float32
            )
        all_ref[at, :width] = jnp.concatenate(parts, axis=1).astype(jnp.bfloat16)
        return carry

    lax.fori_loop(0, count, block, 0)
    all_ref[:, width : 2 * width] = (dk_sum[...].T * SCORE_SCALE).astype(jnp.bfloat16)
    all_ref[:, 2 * width :] = dv_sum[...].T.astype(jnp.bfloat16)
    sums_ref[...] = jnp.zeros_like(sums_ref)
    sums_ref[:1, :] = jnp.sum(all_ref[...].astype(jnp.float32), axis=0, keepdims=True)

    def part_of(at):
        part = dot_right_t(all_ref[at, :width], weight_refs[0][...])
        part = part + dot_right_t(all_ref[at, width : 2 * width], weight_refs[1][...])
        return part + dot_right_t(all_ref[at, 2 * width :], weight_refs[2][...])

    def other(i, carry):
        at = pl.ds(pl.multiple_of(i * shard_len, shard_len), shard_len)
        part_all[at, :] = part_of(at).astype(jnp.bfloat16)
        return carry

    part_refs[0][...] = part_of(slice(0, shard_len))
    lax.fori_loop(1, count, other, 0)
    for i in range(1, count):
        part_refs[i][...] = part_all[i * shard_len : (i + 1) * shard_len, :]


def attend_back(
    place, length, queries, keys_all, values_all, lse, mixed_pieces, grad_pieces, weights
):
    rows, width = queries.shape
    shard_len, model_width = mixed_pieces[0].shape[0], weights[0].shape[0]
    smem, vmem = pl.BlockSpec(memory_space=pltpu.SMEM), pl.BlockSpec(memory_space=pltpu.VMEM)
    arrays = (queries, keys_all, values_all, lse, *mixed_pieces, *grad_pieces, *weights)
    parts = [jax.ShapeDtypeStruct((shard_len, model_width), jnp.float32)] + [
        jax.ShapeDtypeStruct((shard_len, model_width), jnp.bfloat16)
    ] * (len(mixed_pieces) - 1)
    return pl.pallas_call(
        attend_back_kernel,
        out_shape=(
            jax.ShapeDtypeStruct((rows, 3 * width), jnp.bfloat16),
            jax.ShapeDtypeStruct((16, 3 * width), jnp.float32),
            *parts,
        ),
        in_specs=[smem, smem] + [vmem] * len(arrays),
        out_specs=(vmem,) * (2 + len(parts)),
        scratch_shapes=[pltpu.VMEM((width, rows), jnp.float32)] * 2
        + [pltpu.VMEM((rows, width), jnp.bfloat16)] * 2
        + [pltpu.VMEM((rows, model_width), jnp.bfloat16)],
        compiler_params=pltpu.CompilerParams(vmem_limit_bytes=48 << 20),
        cost_estimate=pl.CostEstimate(
            flops=20 * rows * width * rows,
            bytes_accessed=8 << 20,
            transcendentals=rows * rows * (width // HEAD),
        ),
        name="attend_back",
    )(place.reshape(1), length.reshape(1), *arrays)


def vector_kernel(
    place_ref, one_ref, two_ref, resid_ref, normed_one_ref, normed_two_ref, cot_ref, pre_ref, out_ref
):
    seq_count, _, head_width = out_ref.shape
    model_width = one_ref.shape[1]
    resid = resid_ref[...]
    cot = cot_ref[...].astype(jnp.float32)
    rows = [
        one_ref[...],
        two_ref[...],
        resid * normed_one_ref[...],
        resid,
        cot * normed_two_ref[...],
        cot,
    ]
    out_ref[...] = jnp.zeros_like(out_ref)
    for k, values in enumerate(rows):
        total = jnp.sum(values, axis=0, keepdims=True)
        for j in range(seq_count):
            out_ref[j, 2 + k : 3 + k, :] = total[:, j * head_width : (j + 1) * head_width]
    pre = pre_ref[...].astype(jnp.float32)
    per_place = pre.shape[1] // seq_count // model_width
    totals = [
        jnp.sum(pre[:, k * model_width : (k + 1) * model_width], axis=0, keepdims=True)
        for k in range(seq_count * per_place)
    ]
    for k in range(seq_count):
        owner = (place_ref[0] + seq_count - k) % seq_count
        for i in range(per_place):
            row = 8 + owner * per_place + i
            total = totals[k * per_place + i]
            for j in range(seq_count):
                out_ref[j, pl.ds(row, 1), :] = total[:, j * head_width : (j + 1) * head_width]


def vector_sums(place, seq_count, head_width, *arrays):
    return pl.pallas_call(
        vector_kernel,
        out_shape=jax.ShapeDtypeStruct((seq_count, 16, head_width), jnp.float32),
        in_specs=[pl.BlockSpec(memory_space=pltpu.SMEM)]
        + [pl.BlockSpec(memory_space=pltpu.VMEM)] * len(arrays),
        out_specs=pl.BlockSpec(memory_space=pltpu.VMEM),
        compiler_params=pltpu.CompilerParams(vmem_limit_bytes=32 << 20),
        name="vector_sums",
    )(place.reshape(1), *arrays)


def layer(
    tokens,
    cotangent,
    lengths,
    w_attn,
    attn_first,
    attn_second,
    w_ffn,
    ffn_first,
    ffn_second,
    vectors,
    vec_first,
    vec_second,
):
    bf16, f32 = jnp.bfloat16, jnp.float32
    _, shard_len, model_width = tokens.shape
    seq_count, fsdp_count = lax.axis_size("seq"), lax.axis_size("fsdp")
    place, member = lax.axis_index("seq"), lax.axis_index("fsdp")
    _, row_shard, head_width = w_attn.shape
    hidden_shard = w_ffn.shape[2]
    vec_rows, vec_shard = vectors.shape
    token_rows = tokens.reshape(shard_len, model_width)
    cot_half = cotangent.reshape(shard_len, model_width)
    cot_rows = cot_half.astype(f32)
    bits = list(range(fsdp_count.bit_length() - 1))

    own_shard = jnp.concatenate([w_ffn[0], w_ffn[1], w_attn[3]], axis=1).astype(bf16)
    early_shard = jnp.concatenate([w_ffn[0], w_attn[3]], axis=1).astype(bf16)
    late_shard = w_ffn[1].astype(bf16)
    vec_placed = lax.dynamic_update_slice(
        jnp.zeros((16, head_width), bf16), vectors.astype(bf16), (0, member * vec_shard)
    )
    qkv_shard = jnp.concatenate(
        [w_attn[:3].astype(bf16).reshape(3 * row_shard, head_width), vec_placed], axis=0
    )
    own_all = lax.all_gather(own_shard, "fsdp", axis=0, tiled=True)
    token_pieces = gather_behind(token_rows)
    early_pieces = gather_behind(early_shard)
    qkv_all = lax.all_gather(qkv_shard, "fsdp", axis=0, tiled=False)
    w_qkv = [
        qkv_all[:, i * row_shard : (i + 1) * row_shard].reshape(model_width, head_width)
        for i in range(3)
    ]
    vec_own = jnp.sum(qkv_all[:, 3 * row_shard :].astype(f32), axis=0)[:vec_rows]
    vec_half = vec_own.astype(bf16)
    early_pieces = after(early_pieces, w_qkv, vec_half)
    early_cat = jnp.concatenate(
        [piece[:, :hidden_shard] for piece in early_pieces[1:]]
        + [piece[:, hidden_shard:] for piece in early_pieces[1:]],
        axis=1,
    )
    early_all = lax.all_gather(early_cat, "fsdp", axis=0, tiled=True)
    late_pieces = gather_behind(after(late_shard, early_pieces[1]))[1:]

    def times(left, parts):
        return jnp.concatenate(
            [jnp.dot(left, part, preferred_element_type=f32) for part in parts], axis=1
        )

    def times_t(left, parts):
        width = parts[0].shape[1]
        return dot_right_t(left[:, :width], parts[0]) + dot_right_t(left[:, width:], parts[1])

    vec_near = [piece.astype(f32) for piece in gather_behind(vec_half)]

    def near(order):
        return sum(jnp.where(order == r, piece, 0.0) for r, piece in enumerate(vec_near))

    vec_wide = jnp.concatenate(
        [near((place - j) % seq_count) for j in range(seq_count)], axis=1
    )
    up_bias = turn_blocks(vec_wide[8:12].reshape(seq_count, hidden_shard)).reshape(-1)

    valid_len = lengths[0]
    queries, keys_all, values_all, lse, *mixed_pieces = attend(
        place, valid_len, vec_own[:2], after(token_pieces, vec_wide, up_bias), w_qkv
    )
    late_pieces = after(late_pieces, mixed_pieces)
    late_cat = jnp.concatenate(late_pieces, axis=1)
    late_all = lax.all_gather(late_cat, "fsdp", axis=0, tiled=True)
    up_parts = [own_all[:, :hidden_shard], early_all[:, : hidden_shard * (seq_count - 1)]]
    down_parts = [own_all[:, hidden_shard : 2 * hidden_shard], late_all]
    out_parts = [own_all[:, 2 * hidden_shard :], early_all[:, hidden_shard * (seq_count - 1) :]]
    mixed_rows = jnp.concatenate(swap_behind(mixed_pieces), axis=1)

    hidden_one = token_rows.astype(f32) + times_t(mixed_rows, out_parts) + vec_wide[2]
    normed_one, inv_one = layer_norm(hidden_one)
    resid_one = normed_one * vec_wide[4] + vec_wide[5]
    resid_half = resid_one.astype(bf16)
    preact = times(resid_half, up_parts) + up_bias
    activation, gelu_slope = gelu_pair(preact)
    act_half = activation.astype(bf16)
    hidden_two = resid_one + times_t(act_half, down_parts) + vec_wide[3]
    normed_two, inv_two = layer_norm(hidden_two)
    block_out = (normed_two * vec_wide[6] + vec_wide[7]).astype(bf16)
    grad_two = norm_back(cot_rows * vec_wide[6], normed_two, inv_two)
    grad_two_half = grad_two.astype(bf16)

    def outer(left, right):
        return lax.dot_general(
            left, right, (((0,), (0,)), ((), ())), preferred_element_type=f32
        ).astype(bf16)

    def total_of(pieces):
        total = pieces[0].astype(f32)
        for piece in pieces[1:]:
            total = total + piece.astype(f32)
        return total

    def halves_of(pieces):
        return [piece.astype(bf16) for piece in pieces]

    down_local, grad_two_half = lax.optimization_barrier(
        (outer(grad_two_half, act_half), grad_two_half)
    )
    down_part = lax.psum_scatter(down_local, "fsdp", scatter_dimension=0, tiled=True)
    grad_pre_half = (times(grad_two_half, down_parts) * gelu_slope).astype(bf16)
    up_kept, up_sent = halving(
        outer(resid_half, grad_pre_half).reshape(fsdp_count, row_shard, -1), bits[0], True
    )
    up_sent, up_kept, grad_pre_half = lax.optimization_barrier((up_sent, up_kept, grad_pre_half))
    up_received = swapped(up_sent, bits[0])
    grad_resid = grad_two + times_t(grad_pre_half, up_parts)
    grad_one = norm_back(grad_resid * vec_wide[4], normed_one, inv_one)
    grad_one_half = grad_one.astype(bf16)
    grad_mixed = times(grad_one_half, out_parts).astype(bf16)
    grad_pieces = swap_behind(jnp.split(grad_mixed, seq_count, axis=1))

    out_kept, out_sent = halving(
        outer(after(grad_one_half, grad_mixed), mixed_rows).reshape(fsdp_count, row_shard, -1),
        bits[0],
        True,
    )
    out_received = swapped(out_sent, bits[0])
    vec_blocks = vector_sums(
        place,
        seq_count,
        head_width,
        grad_one,
        grad_two,
        grad_resid,
        normed_one,
        normed_two,
        cot_half,
        grad_pre_half,
    )
    vec_order = turn_blocks(vec_blocks)
    vec_moved = swap_behind([vec_order[r] for r in range(seq_count)])
    up_wide = joined(up_kept, up_received)
    out_wide = joined(out_kept, out_received)
    near_places = seq_count // 2
    up_cut, out_cut = near_places * hidden_shard, near_places * head_width
    wide = [
        jnp.concatenate([up_wide[..., :up_cut], out_wide[..., :out_cut]], axis=-1),
        jnp.concatenate([up_wide[..., up_cut:], out_wide[..., out_cut:]], axis=-1),
    ]
    routes = [list(bits[1:]), list(reversed(bits[1:]))]
    wide_moving = []
    for half, route, low in zip(wide, routes, (True, False), strict=True):
        kept, sent = halving(half, route[0], low)
        wide_moving.append((kept, swapped(sent, route[0])))
        grad_pieces = after(grad_pieces, sent)

    grad_qkv, head_sums, input_own, *input_parts = attend_back(
        place,
        valid_len,
        queries,
        keys_all,
        values_all,
        lse,
        mixed_pieces,
        grad_pieces,
        w_qkv,
    )
    input_moved = swap_behind([input_own, *input_parts])
    vec_part = sum(after(vec_moved, input_own))
    vec_lines = jnp.concatenate(
        [head_sums[:1, :head_width], head_sums[:1, 2 * head_width :], vec_part[2:]], axis=0
    )
    vec_lines = jnp.pad(vec_lines, ((0, 0), (0, 2 * head_width)))
    token_all = jnp.concatenate(token_pieces, axis=0)
    qkv_local = lax.dot_general(
        token_all, grad_qkv, (((0,), (0,)), ((), ())), preferred_element_type=f32
    ).astype(bf16)
    qkv_blocks = jnp.concatenate(
        [
            qkv_local.reshape(fsdp_count, row_shard, 3 * head_width),
            jnp.broadcast_to(
                vec_lines.astype(bf16)[None], (fsdp_count, 16, 3 * head_width)
            ),
        ],
        axis=1,
    )

    def place_pieces(half, count):
        ups, outs = half[:, : count * hidden_shard], half[:, count * hidden_shard :]
        return [
            jnp.concatenate(
                [
                    ups[:, r * hidden_shard : (r + 1) * hidden_shard],
                    outs[:, r * head_width : (r + 1) * head_width],
                ],
                axis=1,
            )
            for r in range(count)
        ]

    qkv_kept, qkv_sent = halving(qkv_blocks, bits[0], True)
    qkv_received = swapped(qkv_sent, bits[0])
    step = qkv_sent
    down_moved = None
    for at in range(1, len(bits)):
        moving = []
        for (kept, received), route, low in zip(wide_moving, routes, (True, False), strict=True):
            half = joined(kept, after(received, step))
            if at < len(bits) - 1:
                kept, sent = halving(half, route[at], low)
                moving.append((kept, swapped(sent, route[at])))
                step = sent
            else:
                moving.append(half[0])
        wide_moving = moving
        if down_moved is None:
            down_pieces = jnp.split(after(down_part, step), seq_count, axis=1)
            down_moved = swap_behind(down_pieces)
            step = down_pieces
        if at < len(bits) - 1:
            qkv_half = joined(qkv_kept, after(qkv_received, step))
            qkv_kept, qkv_sent = halving(qkv_half, bits[at], True)
            qkv_received = swapped(qkv_sent, bits[at])
            step = qkv_sent
    wide_pieces = place_pieces(wide_moving[0], near_places) + place_pieces(
        wide_moving[1], seq_count - near_places
    )
    wide_sent = halves_of(wide_pieces[1:])
    wide_moved = swap_behind([wide_pieces[0]] + wide_sent)
    qkv_half = joined(qkv_kept, after(qkv_received, wide_sent))
    qkv_kept, qkv_sent = halving(qkv_half, bits[-1], True)
    qkv_sum = joined(qkv_kept, swapped(qkv_sent, bits[-1]))[0]
    down_sum = total_of([down_moved[0]] + after(down_moved[1:], qkv_sum))
    input_grad = grad_one + total_of([input_moved[0]] + after(input_moved[1:], down_sum))
    up_out_sum = total_of([wide_moved[0]] + after(wide_moved[1:], input_grad))

    token_total = shard_len * seq_count * fsdp_count
    grad_scale = float(token_total) ** (-0.5)
    attn_grad = grad_scale * with_layout_constraint(
        jnp.stack(
            [
                qkv_sum[:row_shard, i * head_width : (i + 1) * head_width]
                for i in range(3)
            ]
            + [up_out_sum[:, hidden_shard:]]
        ),
        Layout(major_to_minor=(0, 1, 2)),
    )
    ffn_grad = grad_scale * jnp.stack([up_out_sum[:, :hidden_shard], down_sum])
    vec_grad = grad_scale * lax.dynamic_slice(
        qkv_sum[row_shard:], (0, member * vec_shard), (vec_rows, vec_shard)
    )
    attn_new, attn_one, attn_two = adam_step(
        w_attn, attn_grad, attn_first, attn_second, WEIGHT_DECAY
    )
    ffn_new, ffn_one, ffn_two = adam_step(w_ffn, ffn_grad, ffn_first, ffn_second, WEIGHT_DECAY)
    vec_new, vec_one, vec_two = adam_step(vectors, vec_grad, vec_first, vec_second, 0.0)
    return (
        block_out.reshape(tokens.shape),
        input_grad.reshape(tokens.shape),
        attn_grad,
        ffn_grad,
        vec_grad,
        attn_new,
        attn_one,
        attn_two,
        ffn_new,
        ffn_one,
        ffn_two,
        vec_new,
        vec_one,
        vec_two,
    )


def solution(mesh):
    placed = (
        P("fsdp", "seq", None),
        P("fsdp", "seq", None),
        P("fsdp"),
        P(None, "fsdp", "seq"),
        P(None, "fsdp", "seq"),
        P(None, "fsdp", "seq"),
        P(None, "fsdp", "seq"),
        P(None, "fsdp", "seq"),
        P(None, "fsdp", "seq"),
        P(None, ("seq", "fsdp")),
        P(None, ("seq", "fsdp")),
        P(None, ("seq", "fsdp")),
    )
    return jax.shard_map(
        layer,
        mesh=mesh,
        in_specs=placed,
        out_specs=(
            P("fsdp", "seq", None),
            P("fsdp", "seq", None),
            P(None, "fsdp", "seq"),
            P(None, "fsdp", "seq"),
            P(None, ("seq", "fsdp")),
            P(None, "fsdp", "seq"),
            P(None, "fsdp", "seq"),
            P(None, "fsdp", "seq"),
            P(None, "fsdp", "seq"),
            P(None, "fsdp", "seq"),
            P(None, "fsdp", "seq"),
            P(None, ("seq", "fsdp")),
            P(None, ("seq", "fsdp")),
            P(None, ("seq", "fsdp")),
        ),
        check_vma=False,
    )
```

```python
import math

import jax
import jax.numpy as jnp
from jax import lax
from jax.experimental import pallas as pl
from jax.experimental.layout import Layout, with_layout_constraint
from jax.experimental.pallas import tpu as pltpu
from jax.sharding import PartitionSpec as P


HEAD = 64
STEP = 3
SCORE_SCALE = 1.0 / math.sqrt(HEAD)


EPS_NORM = 1e-12
ADAM_RATE = 0.005
BETA_ONE = 0.9
BETA_TWO = 0.999
ADAM_EPS = 1e-08
WEIGHT_DECAY = 0.01


def layer_norm(values):
    center = values - jnp.mean(values, axis=-1, keepdims=True)
    inv_scale = lax.rsqrt(jnp.mean(center * center, axis=-1, keepdims=True) + EPS_NORM)
    return (center * inv_scale, inv_scale)


def norm_back(grad_normed, normed, inv_scale):
    return inv_scale * (
        grad_normed
        - jnp.mean(grad_normed, axis=-1, keepdims=True)
        - normed * jnp.mean(grad_normed * normed, axis=-1, keepdims=True)
    )


def gelu_pair(preact):
    normal_cdf = 0.5 * (1.0 + jax.scipy.special.erf(preact * (1.0 / math.sqrt(2.0))))
    density = jnp.exp(-0.5 * preact * preact) * (1.0 / math.sqrt(2.0 * math.pi))
    return (preact * normal_cdf, normal_cdf + preact * density)


def dot_right_t(left, right):
    return lax.dot_general(
        left, right, (((1,), (1,)), ((), ())), preferred_element_type=jnp.float32
    )


def from_behind(piece, distance):
    count = lax.axis_size("seq")
    if distance % count == 0:
        return piece
    return lax.ppermute(piece, "seq", [(i, (i + distance) % count) for i in range(count)])


def gather_behind(piece):
    return [from_behind(piece, r) for r in range(lax.axis_size("seq"))]


def swap_behind(pieces):
    count = len(pieces)
    return [from_behind(pieces[(-r) % count], r) for r in range(count)]


def turn_blocks(blocks):
    count = blocks.shape[0]
    place = lax.axis_index("seq")
    order = (place - jnp.arange(count, dtype=jnp.int32)) % count
    mask = order[:, None] == jnp.arange(count, dtype=jnp.int32)[None, :]
    mask = mask.reshape((count, count) + (1,) * (blocks.ndim - 1))
    return jnp.sum(jnp.where(mask, blocks[None], jnp.zeros((), blocks.dtype)), axis=1)


def adam_step(parameter, gradient, moment_one, moment_two, decay_rate):
    one_new = BETA_ONE * moment_one + (1.0 - BETA_ONE) * gradient
    two_new = BETA_TWO * moment_two + (1.0 - BETA_TWO) * gradient * gradient
    one_hat = one_new / (1.0 - BETA_ONE**STEP)
    two_hat = two_new / (1.0 - BETA_TWO**STEP)
    update = one_hat / (jnp.sqrt(two_hat) + ADAM_EPS)
    return (parameter - ADAM_RATE * (update + decay_rate * parameter), one_new, two_new)


def after(values, *earlier):
    return lax.optimization_barrier((values, earlier))[0]


def halving(blocks, bit, from_low):
    count = blocks.shape[0]
    own = (lax.axis_index("fsdp") >> bit) & 1
    split = (count // 2, 2) if from_low else (2, count // 2)
    axis = 1 if from_low else 0
    view = blocks.reshape(split + blocks.shape[1:])
    kept = lax.dynamic_index_in_dim(view, own, axis, keepdims=False)
    sent = lax.dynamic_index_in_dim(view, 1 - own, axis, keepdims=False)
    return kept, sent.astype(jnp.bfloat16)


def swapped(sent, bit):
    pairs = [(i, i ^ (1 << bit)) for i in range(lax.axis_size("fsdp"))]
    return lax.ppermute(sent, "fsdp", pairs)


def joined(kept, received):
    return kept.astype(jnp.float32) + received.astype(jnp.float32)


def attend_kernel(
    place_ref, length_ref, bias_ref, *refs
):
    count = (len(refs) - 3 - 4 - 2) // 2
    token_refs, weight_refs = refs[:count], refs[count : count + 3]
    q_ref, k_ref, v_ref, lse_ref = refs[count + 3 : count + 7]
    mixed_refs, (mixed_all, token_all) = refs[count + 7 : -2], refs[-2:]
    shard_len = token_refs[0].shape[0]
    _, width = q_ref.shape
    for r, token_ref in enumerate(token_refs):
        token_all[r * shard_len : (r + 1) * shard_len, :] = token_ref[...]

    def project(i, carry):
        at = pl.ds(pl.multiple_of(i * shard_len, shard_len), shard_len)
        piece = token_all[at, :]
        for k, (weight_ref, out_ref) in enumerate(
            zip(weight_refs, (q_ref, k_ref, v_ref), strict=True)
        ):
            out = jnp.dot(piece, weight_ref[...], preferred_element_type=jnp.float32)
            if k != 1:
                out = out + bias_ref[k // 2 : k // 2 + 1, :]
            out_ref[at, :] = out.astype(jnp.bfloat16)
        return carry

    lax.fori_loop(0, count, project, 0)
    masked = key_mask(place_ref[0], length_ref[0], count, shard_len)


    def block(i, carry):
        at = pl.ds(pl.multiple_of(i * shard_len, shard_len), shard_len)
        queries = q_ref[at, :]
        mixed = []
        for h in range(width // HEAD):
            cols = slice(h * HEAD, (h + 1) * HEAD)
            scores = dot_right_t(queries[:, cols] * SCORE_SCALE, k_ref[:, cols]) + masked
            top = jnp.max(scores, axis=1, keepdims=True)
            raised = jnp.exp(scores - top)
            total = jnp.sum(raised, axis=1, keepdims=True)
            probs = (raised * (1.0 / total)).astype(jnp.bfloat16)
            mixed.append(jnp.dot(probs, v_ref[:, cols], preferred_element_type=jnp.float32))
            lse_ref[at, h : h + 1] = top + jnp.log(total)
        mixed_all[at, :] = jnp.concatenate(mixed, axis=1).astype(jnp.bfloat16)
        return carry

    lax.fori_loop(0, count, block, 0)
    for i, mixed_ref in enumerate(mixed_refs):
        mixed_ref[...] = mixed_all[i * shard_len : (i + 1) * shard_len, :]


def key_mask(place, length, count, shard_len):
    column = lax.broadcasted_iota(jnp.int32, (1, shard_len), 1)
    pieces = []
    for r in range(count):
        start = lax.rem(place + count - r, count) * shard_len
        pieces.append(jnp.where(column + start < length, 0.0, -jnp.inf))
    return jnp.concatenate(pieces, axis=1)


def attend(place, length, bias, token_pieces, weights):
    shard_len = token_pieces[0].shape[0]
    rows, width = shard_len * len(token_pieces), weights[0].shape[1]
    half = jax.ShapeDtypeStruct((rows, width), jnp.bfloat16)
    smem, vmem = pl.BlockSpec(memory_space=pltpu.SMEM), pl.BlockSpec(memory_space=pltpu.VMEM)
    arrays = (bias, *token_pieces, *weights)
    return pl.pallas_call(
        attend_kernel,
        out_shape=(half, half, half, jax.ShapeDtypeStruct((rows, 8), jnp.float32))
        + (jax.ShapeDtypeStruct((shard_len, width), jnp.bfloat16),) * len(token_pieces),
        in_specs=[smem, smem] + [vmem] * len(arrays),
        out_specs=(vmem,) * (4 + len(token_pieces)),
        scratch_shapes=[
            pltpu.VMEM((rows, width), jnp.bfloat16),
            pltpu.VMEM((rows, weights[0].shape[0]), jnp.bfloat16),
        ],
        compiler_params=pltpu.CompilerParams(vmem_limit_bytes=40 << 20),
        cost_estimate=pl.CostEstimate(
            flops=2 * rows * width * (3 * weights[0].shape[0] + 8 * rows),
            bytes_accessed=8 << 20,
            transcendentals=rows * rows * (width // HEAD),
        ),
        name="attend",
    )(place.reshape(1), length.reshape(1), *arrays)


def attend_back_kernel(
    place_ref,
    length_ref,
    q_ref,
    k_ref,
    v_ref,
    lse_ref,
    *refs,
):
    count = (len(refs) - 3 - 2 - 5) // 3
    mixed_refs, grad_refs = refs[:count], refs[count : 2 * count]
    weight_refs, refs = refs[2 * count : 2 * count + 3], refs[2 * count + 3 :]
    all_ref, sums_ref = refs[:2]
    part_refs = refs[2 : 2 + count]
    dk_sum, dv_sum, mixed_all, grad_all, part_all = refs[2 + count :]
    shard_len = grad_refs[0].shape[0]
    _, width = q_ref.shape
    masked = key_mask(place_ref[0], length_ref[0], count, shard_len)
    for i in range(count):
        at = slice(i * shard_len, (i + 1) * shard_len)
        mixed_all[at, :] = mixed_refs[i][...]
        grad_all[at, :] = grad_refs[i][...]
    dk_sum[...] = jnp.zeros_like(dk_sum)
    dv_sum[...] = jnp.zeros_like(dv_sum)

    def block(i, carry):
        at = pl.ds(pl.multiple_of(i * shard_len, shard_len), shard_len)
        queries, grad = q_ref[at, :], grad_all[at, :]
        product = grad.astype(jnp.float32) * mixed_all[at, :].astype(jnp.float32)
        parts = []
        for h in range(width // HEAD):
            cols = slice(h * HEAD, (h + 1) * HEAD)
            head_q, head_grad = queries[:, cols], grad[:, cols]
            scores = dot_right_t(head_q * SCORE_SCALE, k_ref[:, cols]) + masked
            probs = jnp.exp(scores - lse_ref[at, h : h + 1])
            delta = jnp.sum(product[:, cols], axis=1, keepdims=True)
            grad_probs = dot_right_t(head_grad, v_ref[:, cols])
            grad_scores = (probs * (grad_probs - delta)).astype(jnp.bfloat16)
            parts.append(
                jnp.dot(grad_scores, k_ref[:, cols], preferred_element_type=jnp.float32)
                * SCORE_SCALE
            )
            dk_sum[cols, :] += jnp.dot(head_q.T, grad_scores, preferred_element_type=jnp.float32)
            dv_sum[cols, :] += jnp.dot(
                head_grad.T, probs.astype(jnp.bfloat16), preferred_element_type=jnp.float32
            )
        all_ref[at, :width] = jnp.concatenate(parts, axis=1).astype(jnp.bfloat16)
        return carry

    lax.fori_loop(0, count, block, 0)
    all_ref[:, width : 2 * width] = (dk_sum[...].T * SCORE_SCALE).astype(jnp.bfloat16)
    all_ref[:, 2 * width :] = dv_sum[...].T.astype(jnp.bfloat16)
    sums_ref[...] = jnp.zeros_like(sums_ref)
    sums_ref[:1, :] = jnp.sum(all_ref[...].astype(jnp.float32), axis=0, keepdims=True)

    def part_of(at):
        part = dot_right_t(all_ref[at, :width], weight_refs[0][...])
        part = part + dot_right_t(all_ref[at, width : 2 * width], weight_refs[1][...])
        return part + dot_right_t(all_ref[at, 2 * width :], weight_refs[2][...])

    def other(i, carry):
        at = pl.ds(pl.multiple_of(i * shard_len, shard_len), shard_len)
        part_all[at, :] = part_of(at).astype(jnp.bfloat16)
        return carry

    part_refs[0][...] = part_of(slice(0, shard_len))
    lax.fori_loop(1, count, other, 0)
    for i in range(1, count):
        part_refs[i][...] = part_all[i * shard_len : (i + 1) * shard_len, :]


def attend_back(
    place, length, queries, keys_all, values_all, lse, mixed_pieces, grad_pieces, weights
):
    rows, width = queries.shape
    shard_len, model_width = mixed_pieces[0].shape[0], weights[0].shape[0]
    smem, vmem = pl.BlockSpec(memory_space=pltpu.SMEM), pl.BlockSpec(memory_space=pltpu.VMEM)
    arrays = (queries, keys_all, values_all, lse, *mixed_pieces, *grad_pieces, *weights)
    parts = [jax.ShapeDtypeStruct((shard_len, model_width), jnp.float32)] + [
        jax.ShapeDtypeStruct((shard_len, model_width), jnp.bfloat16)
    ] * (len(mixed_pieces) - 1)
    return pl.pallas_call(
        attend_back_kernel,
        out_shape=(
            jax.ShapeDtypeStruct((rows, 3 * width), jnp.bfloat16),
            jax.ShapeDtypeStruct((16, 3 * width), jnp.float32),
            *parts,
        ),
        in_specs=[smem, smem] + [vmem] * len(arrays),
        out_specs=(vmem,) * (2 + len(parts)),
        scratch_shapes=[pltpu.VMEM((width, rows), jnp.float32)] * 2
        + [pltpu.VMEM((rows, width), jnp.bfloat16)] * 2
        + [pltpu.VMEM((rows, model_width), jnp.bfloat16)],
        compiler_params=pltpu.CompilerParams(vmem_limit_bytes=48 << 20),
        cost_estimate=pl.CostEstimate(
            flops=20 * rows * width * rows,
            bytes_accessed=8 << 20,
            transcendentals=rows * rows * (width // HEAD),
        ),
        name="attend_back",
    )(place.reshape(1), length.reshape(1), *arrays)


def vector_kernel(
    place_ref, one_ref, two_ref, resid_ref, normed_one_ref, normed_two_ref, cot_ref, pre_ref, out_ref
):
    seq_count, _, head_width = out_ref.shape
    model_width = one_ref.shape[1]
    resid = resid_ref[...]
    cot = cot_ref[...].astype(jnp.float32)
    rows = [
        one_ref[...],
        two_ref[...],
        resid * normed_one_ref[...],
        resid,
        cot * normed_two_ref[...],
        cot,
    ]
    out_ref[...] = jnp.zeros_like(out_ref)
    for k, values in enumerate(rows):
        total = jnp.sum(values, axis=0, keepdims=True)
        for j in range(seq_count):
            out_ref[j, 2 + k : 3 + k, :] = total[:, j * head_width : (j + 1) * head_width]
    pre = pre_ref[...].astype(jnp.float32)
    per_place = pre.shape[1] // seq_count // model_width
    totals = [
        jnp.sum(pre[:, k * model_width : (k + 1) * model_width], axis=0, keepdims=True)
        for k in range(seq_count * per_place)
    ]
    for k in range(seq_count):
        owner = (place_ref[0] + seq_count - k) % seq_count
        for i in range(per_place):
            row = 8 + owner * per_place + i
            total = totals[k * per_place + i]
            for j in range(seq_count):
                out_ref[j, pl.ds(row, 1), :] = total[:, j * head_width : (j + 1) * head_width]


def vector_sums(place, seq_count, head_width, *arrays):
    return pl.pallas_call(
        vector_kernel,
        out_shape=jax.ShapeDtypeStruct((seq_count, 16, head_width), jnp.float32),
        in_specs=[pl.BlockSpec(memory_space=pltpu.SMEM)]
        + [pl.BlockSpec(memory_space=pltpu.VMEM)] * len(arrays),
        out_specs=pl.BlockSpec(memory_space=pltpu.VMEM),
        compiler_params=pltpu.CompilerParams(vmem_limit_bytes=32 << 20),
        name="vector_sums",
    )(place.reshape(1), *arrays)


def layer(
    tokens,
    cotangent,
    lengths,
    w_attn,
    attn_first,
    attn_second,
    w_ffn,
    ffn_first,
    ffn_second,
    vectors,
    vec_first,
    vec_second,
):
    bf16, f32 = jnp.bfloat16, jnp.float32
    _, shard_len, model_width = tokens.shape
    seq_count, fsdp_count = lax.axis_size("seq"), lax.axis_size("fsdp")
    place, member = lax.axis_index("seq"), lax.axis_index("fsdp")
    _, row_shard, head_width = w_attn.shape
    hidden_shard = w_ffn.shape[2]
    vec_rows, vec_shard = vectors.shape
    token_rows = tokens.reshape(shard_len, model_width)
    cot_half = cotangent.reshape(shard_len, model_width)
    cot_rows = cot_half.astype(f32)
    bits = list(range(fsdp_count.bit_length() - 1))

    own_shard = jnp.concatenate([w_ffn[0], w_ffn[1], w_attn[3]], axis=1).astype(bf16)
    vec_placed = lax.dynamic_update_slice(
        jnp.zeros((16, head_width), bf16), vectors.astype(bf16), (0, member * vec_shard)
    )
    qkv_shard = jnp.concatenate(
        [w_attn[:3].astype(bf16).reshape(3 * row_shard, head_width), vec_placed], axis=0
    )
    own_all = lax.all_gather(own_shard, "fsdp", axis=0, tiled=True)
    weight_pieces = gather_behind(own_shard)[1:]
    token_pieces = gather_behind(token_rows)
    qkv_all = lax.all_gather(qkv_shard, "fsdp", axis=0, tiled=False)
    w_qkv = [
        qkv_all[:, i * row_shard : (i + 1) * row_shard].reshape(model_width, head_width)
        for i in range(3)
    ]
    vec_own = jnp.sum(qkv_all[:, 3 * row_shard :].astype(f32), axis=0)[:vec_rows]
    vec_half = vec_own.astype(bf16)
    weight_pieces = after(weight_pieces, w_qkv, vec_half)
    cuts = (0, hidden_shard, 2 * hidden_shard, 2 * hidden_shard + head_width)
    rest_cat = jnp.concatenate(
        [
            piece[:, low:high]
            for low, high in zip(cuts[:-1], cuts[1:], strict=True)
            for piece in weight_pieces
        ],
        axis=1,
    )
    rest_all = lax.all_gather(rest_cat, "fsdp", axis=0, tiled=True)
    up_parts, down_parts, out_parts = (
        [own_all[:, low:high], rest_all[:, low * (seq_count - 1) : high * (seq_count - 1)]]
        for low, high in zip(cuts[:-1], cuts[1:], strict=True)
    )

    def times(left, parts):
        return jnp.concatenate(
            [jnp.dot(left, part, preferred_element_type=f32) for part in parts], axis=1
        )

    def times_t(left, parts):
        width = parts[0].shape[1]
        return dot_right_t(left[:, :width], parts[0]) + dot_right_t(left[:, width:], parts[1])

    vec_near = [piece.astype(f32) for piece in gather_behind(vec_half)]

    def near(order):
        return sum(jnp.where(order == r, piece, 0.0) for r, piece in enumerate(vec_near))

    vec_wide = jnp.concatenate(
        [near((place - j) % seq_count) for j in range(seq_count)], axis=1
    )
    up_bias = turn_blocks(vec_wide[8:12].reshape(seq_count, hidden_shard)).reshape(-1)

    valid_len = lengths[0]
    queries, keys_all, values_all, lse, *mixed_pieces = attend(
        place, valid_len, vec_own[:2], after(token_pieces, vec_wide, up_bias), w_qkv
    )
    mixed_rows = jnp.concatenate(swap_behind(mixed_pieces), axis=1)

    hidden_one = token_rows.astype(f32) + times_t(mixed_rows, out_parts) + vec_wide[2]
    normed_one, inv_one = layer_norm(hidden_one)
    resid_one = normed_one * vec_wide[4] + vec_wide[5]
    resid_half = resid_one.astype(bf16)
    preact = times(resid_half, up_parts) + up_bias
    activation, gelu_slope = gelu_pair(preact)
    act_half = activation.astype(bf16)
    hidden_two = resid_one + times_t(act_half, down_parts) + vec_wide[3]
    normed_two, inv_two = layer_norm(hidden_two)
    block_out = (normed_two * vec_wide[6] + vec_wide[7]).astype(bf16)
    grad_two = norm_back(cot_rows * vec_wide[6], normed_two, inv_two)
    grad_two_half = grad_two.astype(bf16)

    def outer(left, right):
        return lax.dot_general(
            left, right, (((0,), (0,)), ((), ())), preferred_element_type=f32
        ).astype(bf16)

    def total_of(pieces):
        total = pieces[0].astype(f32)
        for piece in pieces[1:]:
            total = total + piece.astype(f32)
        return total

    def halves_of(pieces):
        return [piece.astype(bf16) for piece in pieces]

    down_local, grad_two_half = lax.optimization_barrier(
        (outer(grad_two_half, act_half), grad_two_half)
    )
    down_part = lax.psum_scatter(down_local, "fsdp", scatter_dimension=0, tiled=True)
    grad_pre_half = (times(grad_two_half, down_parts) * gelu_slope).astype(bf16)
    up_kept, up_sent = halving(
        outer(resid_half, grad_pre_half).reshape(fsdp_count, row_shard, -1), bits[0], True
    )
    up_sent, up_kept, grad_pre_half = lax.optimization_barrier((up_sent, up_kept, grad_pre_half))
    up_received = swapped(up_sent, bits[0])
    grad_resid = grad_two + times_t(grad_pre_half, up_parts)
    grad_one = norm_back(grad_resid * vec_wide[4], normed_one, inv_one)
    grad_one_half = grad_one.astype(bf16)
    grad_mixed = times(grad_one_half, out_parts).astype(bf16)
    grad_pieces = swap_behind(jnp.split(grad_mixed, seq_count, axis=1))

    out_kept, out_sent = halving(
        outer(after(grad_one_half, grad_mixed), mixed_rows).reshape(fsdp_count, row_shard, -1),
        bits[0],
        True,
    )
    out_received = swapped(out_sent, bits[0])
    vec_blocks = vector_sums(
        place,
        seq_count,
        head_width,
        grad_one,
        grad_two,
        grad_resid,
        normed_one,
        normed_two,
        cot_half,
        grad_pre_half,
    )
    vec_order = turn_blocks(vec_blocks)
    vec_moved = swap_behind([vec_order[r] for r in range(seq_count)])
    up_wide = joined(up_kept, up_received)
    out_wide = joined(out_kept, out_received)
    near_places = seq_count // 2
    up_cut, out_cut = near_places * hidden_shard, near_places * head_width
    wide = [
        jnp.concatenate([up_wide[..., :up_cut], out_wide[..., :out_cut]], axis=-1),
        jnp.concatenate([up_wide[..., up_cut:], out_wide[..., out_cut:]], axis=-1),
    ]
    routes = [list(bits[1:]), list(reversed(bits[1:]))]
    wide_moving = []
    for half, route, low in zip(wide, routes, (True, False), strict=True):
        kept, sent = halving(half, route[0], low)
        wide_moving.append((kept, swapped(sent, route[0])))
        grad_pieces = after(grad_pieces, sent)

    grad_qkv, head_sums, input_own, *input_parts = attend_back(
        place,
        valid_len,
        queries,
        keys_all,
        values_all,
        lse,
        mixed_pieces,
        grad_pieces,
        w_qkv,
    )
    input_moved = swap_behind([input_own, *input_parts])
    vec_part = sum(after(vec_moved, input_own))
    vec_lines = jnp.concatenate(
        [head_sums[:1, :head_width], head_sums[:1, 2 * head_width :], vec_part[2:]], axis=0
    )
    vec_lines = jnp.pad(vec_lines, ((0, 0), (0, 2 * head_width)))
    token_all = jnp.concatenate(token_pieces, axis=0)
    qkv_local = lax.dot_general(
        token_all, grad_qkv, (((0,), (0,)), ((), ())), preferred_element_type=f32
    ).astype(bf16)
    qkv_blocks = jnp.concatenate(
        [
            qkv_local.reshape(fsdp_count, row_shard, 3 * head_width),
            jnp.broadcast_to(
                vec_lines.astype(bf16)[None], (fsdp_count, 16, 3 * head_width)
            ),
        ],
        axis=1,
    )

    def place_pieces(half, count):
        ups, outs = half[:, : count * hidden_shard], half[:, count * hidden_shard :]
        return [
            jnp.concatenate(
                [
                    ups[:, r * hidden_shard : (r + 1) * hidden_shard],
                    outs[:, r * head_width : (r + 1) * head_width],
                ],
                axis=1,
            )
            for r in range(count)
        ]

    qkv_kept, qkv_sent = halving(qkv_blocks, bits[0], True)
    qkv_received = swapped(qkv_sent, bits[0])
    step = qkv_sent
    down_moved = None
    for at in range(1, len(bits)):
        moving = []
        for (kept, received), route, low in zip(wide_moving, routes, (True, False), strict=True):
            half = joined(kept, after(received, step))
            if at < len(bits) - 1:
                kept, sent = halving(half, route[at], low)
                moving.append((kept, swapped(sent, route[at])))
                step = sent
            else:
                moving.append(half[0])
        wide_moving = moving
        if down_moved is None:
            down_pieces = jnp.split(after(down_part, step), seq_count, axis=1)
            down_moved = swap_behind(down_pieces)
            step = down_pieces
    wide_pieces = place_pieces(wide_moving[0], near_places) + place_pieces(
        wide_moving[1], seq_count - near_places
    )
    wide_sent = halves_of(wide_pieces[1:])
    wide_moved = swap_behind([wide_pieces[0]] + wide_sent)
    step = wide_sent
    for bit in bits[1:]:
        qkv_half = joined(qkv_kept, after(qkv_received, step))
        qkv_kept, qkv_sent = halving(qkv_half, bit, True)
        qkv_received = swapped(qkv_sent, bit)
        step = qkv_sent
    qkv_sum = joined(qkv_kept, qkv_received)[0]
    input_grad = grad_one + total_of([input_moved[0]] + after(input_moved[1:], qkv_sum))
    down_sum = total_of([down_moved[0]] + after(down_moved[1:], input_grad))
    up_out_sum = total_of([wide_moved[0]] + after(wide_moved[1:], down_sum))

    token_total = shard_len * seq_count * fsdp_count
    grad_scale = float(token_total) ** (-0.5)
    attn_grad = grad_scale * with_layout_constraint(
        jnp.stack(
            [
                qkv_sum[:row_shard, i * head_width : (i + 1) * head_width]
                for i in range(3)
            ]
            + [up_out_sum[:, hidden_shard:]]
        ),
        Layout(major_to_minor=(0, 1, 2)),
    )
    ffn_grad = grad_scale * jnp.stack([up_out_sum[:, :hidden_shard], down_sum])
    vec_grad = grad_scale * lax.dynamic_slice(
        qkv_sum[row_shard:], (0, member * vec_shard), (vec_rows, vec_shard)
    )
    attn_new, attn_one, attn_two = adam_step(
        w_attn, attn_grad, attn_first, attn_second, WEIGHT_DECAY
    )
    ffn_new, ffn_one, ffn_two = adam_step(w_ffn, ffn_grad, ffn_first, ffn_second, WEIGHT_DECAY)
    vec_new, vec_one, vec_two = adam_step(vectors, vec_grad, vec_first, vec_second, 0.0)
    return (
        block_out.reshape(tokens.shape),
        input_grad.reshape(tokens.shape),
        attn_grad,
        ffn_grad,
        vec_grad,
        attn_new,
        attn_one,
        attn_two,
        ffn_new,
        ffn_one,
        ffn_two,
        vec_new,
        vec_one,
        vec_two,
    )


def solution(mesh):
    placed = (
        P("fsdp", "seq", None),
        P("fsdp", "seq", None),
        P("fsdp"),
        P(None, "fsdp", "seq"),
        P(None, "fsdp", "seq"),
        P(None, "fsdp", "seq"),
        P(None, "fsdp", "seq"),
        P(None, "fsdp", "seq"),
        P(None, "fsdp", "seq"),
        P(None, ("seq", "fsdp")),
        P(None, ("seq", "fsdp")),
        P(None, ("seq", "fsdp")),
    )
    return jax.shard_map(
        layer,
        mesh=mesh,
        in_specs=placed,
        out_specs=(
            P("fsdp", "seq", None),
            P("fsdp", "seq", None),
            P(None, "fsdp", "seq"),
            P(None, "fsdp", "seq"),
            P(None, ("seq", "fsdp")),
            P(None, "fsdp", "seq"),
            P(None, "fsdp", "seq"),
            P(None, "fsdp", "seq"),
            P(None, "fsdp", "seq"),
            P(None, "fsdp", "seq"),
            P(None, "fsdp", "seq"),
            P(None, ("seq", "fsdp")),
            P(None, ("seq", "fsdp")),
            P(None, ("seq", "fsdp")),
        ),
        check_vma=False,
    )
```

```python
import math

import jax
import jax.numpy as jnp
from jax import lax
from jax.experimental import pallas as pl
from jax.experimental.layout import Layout, with_layout_constraint
from jax.experimental.pallas import tpu as pltpu
from jax.sharding import PartitionSpec as P


HEAD = 64
STEP = 3
SCORE_SCALE = 1.0 / math.sqrt(HEAD)


EPS_NORM = 1e-12
ADAM_RATE = 0.005
BETA_ONE = 0.9
BETA_TWO = 0.999
ADAM_EPS = 1e-08
WEIGHT_DECAY = 0.01


def layer_norm(values):
    center = values - jnp.mean(values, axis=-1, keepdims=True)
    inv_scale = lax.rsqrt(jnp.mean(center * center, axis=-1, keepdims=True) + EPS_NORM)
    return (center * inv_scale, inv_scale)


def norm_back(grad_normed, normed, inv_scale):
    return inv_scale * (
        grad_normed
        - jnp.mean(grad_normed, axis=-1, keepdims=True)
        - normed * jnp.mean(grad_normed * normed, axis=-1, keepdims=True)
    )


def gelu_pair(preact):
    normal_cdf = 0.5 * (1.0 + jax.scipy.special.erf(preact * (1.0 / math.sqrt(2.0))))
    density = jnp.exp(-0.5 * preact * preact) * (1.0 / math.sqrt(2.0 * math.pi))
    return (preact * normal_cdf, normal_cdf + preact * density)


def dot_right_t(left, right):
    return lax.dot_general(
        left, right, (((1,), (1,)), ((), ())), preferred_element_type=jnp.float32
    )


def from_behind(piece, distance):
    count = lax.axis_size("seq")
    if distance % count == 0:
        return piece
    return lax.ppermute(piece, "seq", [(i, (i + distance) % count) for i in range(count)])


def gather_behind(piece):
    return [from_behind(piece, r) for r in range(lax.axis_size("seq"))]


def swap_behind(pieces):
    count = len(pieces)
    return [from_behind(pieces[(-r) % count], r) for r in range(count)]


def turn_blocks(blocks):
    count = blocks.shape[0]
    place = lax.axis_index("seq")
    order = (place - jnp.arange(count, dtype=jnp.int32)) % count
    mask = order[:, None] == jnp.arange(count, dtype=jnp.int32)[None, :]
    mask = mask.reshape((count, count) + (1,) * (blocks.ndim - 1))
    return jnp.sum(jnp.where(mask, blocks[None], jnp.zeros((), blocks.dtype)), axis=1)


def adam_step(parameter, gradient, moment_one, moment_two, decay_rate):
    one_new = BETA_ONE * moment_one + (1.0 - BETA_ONE) * gradient
    two_new = BETA_TWO * moment_two + (1.0 - BETA_TWO) * gradient * gradient
    one_hat = one_new / (1.0 - BETA_ONE**STEP)
    two_hat = two_new / (1.0 - BETA_TWO**STEP)
    update = one_hat / (jnp.sqrt(two_hat) + ADAM_EPS)
    return (parameter - ADAM_RATE * (update + decay_rate * parameter), one_new, two_new)


def after(values, *earlier):
    return lax.optimization_barrier((values, earlier))[0]


def halving(blocks, bit, from_low):
    count = blocks.shape[0]
    own = (lax.axis_index("fsdp") >> bit) & 1
    split = (count // 2, 2) if from_low else (2, count // 2)
    axis = 1 if from_low else 0
    view = blocks.reshape(split + blocks.shape[1:])
    kept = lax.dynamic_index_in_dim(view, own, axis, keepdims=False)
    sent = lax.dynamic_index_in_dim(view, 1 - own, axis, keepdims=False)
    return kept, sent.astype(jnp.bfloat16)


def swapped(sent, bit):
    pairs = [(i, i ^ (1 << bit)) for i in range(lax.axis_size("fsdp"))]
    return lax.ppermute(sent, "fsdp", pairs)


def joined(kept, received):
    return kept.astype(jnp.float32) + received.astype(jnp.float32)


def attend_kernel(
    place_ref, length_ref, bias_ref, *refs
):
    count = (len(refs) - 3 - 4 - 2) // 2
    token_refs, weight_refs = refs[:count], refs[count : count + 3]
    q_ref, k_ref, v_ref, lse_ref, mixed_all = refs[count + 3 : count + 8]
    mixed_refs, token_all = refs[count + 8 : -1], refs[-1]
    shard_len = token_refs[0].shape[0]
    _, width = q_ref.shape
    for r, token_ref in enumerate(token_refs):
        token_all[r * shard_len : (r + 1) * shard_len, :] = token_ref[...]

    def project(i, carry):
        at = pl.ds(pl.multiple_of(i * shard_len, shard_len), shard_len)
        piece = token_all[at, :]
        for k, (weight_ref, out_ref) in enumerate(
            zip(weight_refs, (q_ref, k_ref, v_ref), strict=True)
        ):
            out = jnp.dot(piece, weight_ref[...], preferred_element_type=jnp.float32)
            if k != 1:
                out = out + bias_ref[k // 2 : k // 2 + 1, :]
            out_ref[at, :] = out.astype(jnp.bfloat16)
        return carry

    lax.fori_loop(0, count, project, 0)
    masked = key_mask(place_ref[0], length_ref[0], count, shard_len)


    def block(i, carry):
        at = pl.ds(pl.multiple_of(i * shard_len, shard_len), shard_len)
        queries = q_ref[at, :]
        mixed = []
        for h in range(width // HEAD):
            cols = slice(h * HEAD, (h + 1) * HEAD)
            scores = dot_right_t(queries[:, cols] * SCORE_SCALE, k_ref[:, cols]) + masked
            top = jnp.max(scores, axis=1, keepdims=True)
            raised = jnp.exp(scores - top)
            total = jnp.sum(raised, axis=1, keepdims=True)
            probs = (raised * (1.0 / total)).astype(jnp.bfloat16)
            mixed.append(jnp.dot(probs, v_ref[:, cols], preferred_element_type=jnp.float32))
            lse_ref[at, h : h + 1] = top + jnp.log(total)
        mixed_all[at, :] = jnp.concatenate(mixed, axis=1).astype(jnp.bfloat16)
        return carry

    lax.fori_loop(0, count, block, 0)
    for i, mixed_ref in enumerate(mixed_refs):
        mixed_ref[...] = mixed_all[i * shard_len : (i + 1) * shard_len, :]


def key_mask(place, length, count, shard_len):
    column = lax.broadcasted_iota(jnp.int32, (1, shard_len), 1)
    pieces = []
    for r in range(count):
        start = lax.rem(place + count - r, count) * shard_len
        pieces.append(jnp.where(column + start < length, 0.0, -jnp.inf))
    return jnp.concatenate(pieces, axis=1)


def attend(place, length, bias, token_pieces, weights):
    shard_len = token_pieces[0].shape[0]
    rows, width = shard_len * len(token_pieces), weights[0].shape[1]
    half = jax.ShapeDtypeStruct((rows, width), jnp.bfloat16)
    smem, vmem = pl.BlockSpec(memory_space=pltpu.SMEM), pl.BlockSpec(memory_space=pltpu.VMEM)
    arrays = (bias, *token_pieces, *weights)
    return pl.pallas_call(
        attend_kernel,
        out_shape=(half, half, half, jax.ShapeDtypeStruct((rows, 8), jnp.float32), half)
        + (jax.ShapeDtypeStruct((shard_len, width), jnp.bfloat16),) * len(token_pieces),
        in_specs=[smem, smem] + [vmem] * len(arrays),
        out_specs=(vmem,) * (5 + len(token_pieces)),
        scratch_shapes=[pltpu.VMEM((rows, weights[0].shape[0]), jnp.bfloat16)],
        compiler_params=pltpu.CompilerParams(vmem_limit_bytes=40 << 20),
        cost_estimate=pl.CostEstimate(
            flops=2 * rows * width * (3 * weights[0].shape[0] + 8 * rows),
            bytes_accessed=8 << 20,
            transcendentals=rows * rows * (width // HEAD),
        ),
        name="attend",
    )(place.reshape(1), length.reshape(1), *arrays)


def attend_back_kernel(
    place_ref,
    length_ref,
    q_ref,
    k_ref,
    v_ref,
    lse_ref,
    mixed_all,
    *refs,
):
    count = (len(refs) - 3 - 2 - 4) // 2
    grad_refs = refs[:count]
    weight_refs, refs = refs[count : count + 3], refs[count + 3 :]
    all_ref, sums_ref = refs[:2]
    part_refs = refs[2 : 2 + count]
    dk_sum, dv_sum, grad_all, part_all = refs[2 + count :]
    shard_len = grad_refs[0].shape[0]
    _, width = q_ref.shape
    masked = key_mask(place_ref[0], length_ref[0], count, shard_len)
    for i in range(count):
        at = slice(i * shard_len, (i + 1) * shard_len)
        grad_all[at, :] = grad_refs[i][...]
    dk_sum[...] = jnp.zeros_like(dk_sum)
    dv_sum[...] = jnp.zeros_like(dv_sum)

    def block(i, carry):
        at = pl.ds(pl.multiple_of(i * shard_len, shard_len), shard_len)
        queries, grad = q_ref[at, :], grad_all[at, :]
        product = grad.astype(jnp.float32) * mixed_all[at, :].astype(jnp.float32)
        parts = []
        for h in range(width // HEAD):
            cols = slice(h * HEAD, (h + 1) * HEAD)
            head_q, head_grad = queries[:, cols], grad[:, cols]
            scores = dot_right_t(head_q * SCORE_SCALE, k_ref[:, cols]) + masked
            probs = jnp.exp(scores - lse_ref[at, h : h + 1])
            delta = jnp.sum(product[:, cols], axis=1, keepdims=True)
            grad_probs = dot_right_t(head_grad, v_ref[:, cols])
            grad_scores = (probs * (grad_probs - delta)).astype(jnp.bfloat16)
            parts.append(
                jnp.dot(grad_scores, k_ref[:, cols], preferred_element_type=jnp.float32)
                * SCORE_SCALE
            )
            dk_sum[cols, :] += jnp.dot(head_q.T, grad_scores, preferred_element_type=jnp.float32)
            dv_sum[cols, :] += jnp.dot(
                head_grad.T, probs.astype(jnp.bfloat16), preferred_element_type=jnp.float32
            )
        all_ref[at, :width] = jnp.concatenate(parts, axis=1).astype(jnp.bfloat16)
        return carry

    lax.fori_loop(0, count, block, 0)
    all_ref[:, width : 2 * width] = (dk_sum[...].T * SCORE_SCALE).astype(jnp.bfloat16)
    all_ref[:, 2 * width :] = dv_sum[...].T.astype(jnp.bfloat16)
    sums_ref[...] = jnp.zeros_like(sums_ref)
    sums_ref[:1, :] = jnp.sum(all_ref[...].astype(jnp.float32), axis=0, keepdims=True)

    def part_of(at):
        part = dot_right_t(all_ref[at, :width], weight_refs[0][...])
        part = part + dot_right_t(all_ref[at, width : 2 * width], weight_refs[1][...])
        return part + dot_right_t(all_ref[at, 2 * width :], weight_refs[2][...])

    def other(i, carry):
        at = pl.ds(pl.multiple_of(i * shard_len, shard_len), shard_len)
        part_all[at, :] = part_of(at).astype(jnp.bfloat16)
        return carry

    part_refs[0][...] = part_of(slice(0, shard_len))
    lax.fori_loop(1, count, other, 0)
    for i in range(1, count):
        part_refs[i][...] = part_all[i * shard_len : (i + 1) * shard_len, :]


def attend_back(
    place, length, queries, keys_all, values_all, lse, mixed, grad_pieces, weights
):
    rows, width = queries.shape
    shard_len, model_width = grad_pieces[0].shape[0], weights[0].shape[0]
    smem, vmem = pl.BlockSpec(memory_space=pltpu.SMEM), pl.BlockSpec(memory_space=pltpu.VMEM)
    arrays = (queries, keys_all, values_all, lse, mixed, *grad_pieces, *weights)
    parts = [jax.ShapeDtypeStruct((shard_len, model_width), jnp.float32)] + [
        jax.ShapeDtypeStruct((shard_len, model_width), jnp.bfloat16)
    ] * (len(grad_pieces) - 1)
    return pl.pallas_call(
        attend_back_kernel,
        out_shape=(
            jax.ShapeDtypeStruct((rows, 3 * width), jnp.bfloat16),
            jax.ShapeDtypeStruct((16, 3 * width), jnp.float32),
            *parts,
        ),
        in_specs=[smem, smem] + [vmem] * len(arrays),
        out_specs=(vmem,) * (2 + len(parts)),
        scratch_shapes=[pltpu.VMEM((width, rows), jnp.float32)] * 2
        + [pltpu.VMEM((rows, width), jnp.bfloat16)]
        + [pltpu.VMEM((rows, model_width), jnp.bfloat16)],
        compiler_params=pltpu.CompilerParams(vmem_limit_bytes=48 << 20),
        cost_estimate=pl.CostEstimate(
            flops=20 * rows * width * rows,
            bytes_accessed=8 << 20,
            transcendentals=rows * rows * (width // HEAD),
        ),
        name="attend_back",
    )(place.reshape(1), length.reshape(1), *arrays)


VECTOR_CHUNK = 32


def vector_kernel(
    place_ref,
    one_ref,
    two_ref,
    resid_ref,
    normed_one_ref,
    normed_two_ref,
    cot_ref,
    pre_ref,
    out_ref,
    row_sum,
    pre_sum,
):
    seq_count, _, head_width = out_ref.shape
    row_total, model_width = one_ref.shape
    row_sum[...] = jnp.zeros_like(row_sum)
    pre_sum[...] = jnp.zeros_like(pre_sum)

    def fold(values):
        return jnp.sum(values.reshape(VECTOR_CHUNK // 8, 8, values.shape[1]), axis=0)

    def add_rows(i, carry):
        at = pl.ds(pl.multiple_of(i * VECTOR_CHUNK, VECTOR_CHUNK), VECTOR_CHUNK)
        resid = resid_ref[at, :]
        cot = cot_ref[at, :].astype(jnp.float32)
        lines = [
            one_ref[at, :],
            two_ref[at, :],
            resid * normed_one_ref[at, :],
            resid,
            cot * normed_two_ref[at, :],
            cot,
        ]
        for k, values in enumerate(lines):
            row_sum[8 * k : 8 * k + 8, :] += fold(values)
        pre_sum[...] += fold(pre_ref[at, :].astype(jnp.float32))
        return carry

    lax.fori_loop(0, row_total // VECTOR_CHUNK, add_rows, 0)
    out_ref[...] = jnp.zeros_like(out_ref)
    for k in range(6):
        total = jnp.sum(row_sum[8 * k : 8 * k + 8, :], axis=0, keepdims=True)
        for j in range(seq_count):
            out_ref[j, 2 + k : 3 + k, :] = total[:, j * head_width : (j + 1) * head_width]
    per_place = pre_ref.shape[1] // seq_count // model_width
    for k in range(seq_count):
        owner = lax.rem(place_ref[0] + seq_count - k, seq_count)
        for i in range(per_place):
            row = 8 + owner * per_place + i
            low = (k * per_place + i) * model_width
            total = jnp.sum(pre_sum[:, low : low + model_width], axis=0, keepdims=True)
            for j in range(seq_count):
                out_ref[j, pl.ds(row, 1), :] = total[:, j * head_width : (j + 1) * head_width]


def vector_sums(place, seq_count, head_width, *arrays):
    return pl.pallas_call(
        vector_kernel,
        out_shape=jax.ShapeDtypeStruct((seq_count, 16, head_width), jnp.float32),
        in_specs=[pl.BlockSpec(memory_space=pltpu.SMEM)]
        + [pl.BlockSpec(memory_space=pltpu.VMEM)] * len(arrays),
        out_specs=pl.BlockSpec(memory_space=pltpu.VMEM),
        scratch_shapes=[
            pltpu.VMEM((48, arrays[0].shape[1]), jnp.float32),
            pltpu.VMEM((8, arrays[-1].shape[1]), jnp.float32),
        ],
        compiler_params=pltpu.CompilerParams(vmem_limit_bytes=32 << 20),
        name="vector_sums",
    )(place.reshape(1), *arrays)


def layer(
    tokens,
    cotangent,
    lengths,
    w_attn,
    attn_first,
    attn_second,
    w_ffn,
    ffn_first,
    ffn_second,
    vectors,
    vec_first,
    vec_second,
):
    bf16, f32 = jnp.bfloat16, jnp.float32
    _, shard_len, model_width = tokens.shape
    seq_count, fsdp_count = lax.axis_size("seq"), lax.axis_size("fsdp")
    place, member = lax.axis_index("seq"), lax.axis_index("fsdp")
    _, row_shard, head_width = w_attn.shape
    hidden_shard = w_ffn.shape[2]
    vec_rows, vec_shard = vectors.shape
    token_rows = tokens.reshape(shard_len, model_width)
    cot_half = cotangent.reshape(shard_len, model_width)
    cot_rows = cot_half.astype(f32)
    bits = list(range(fsdp_count.bit_length() - 1))

    own_shard = jnp.concatenate([w_ffn[0], w_ffn[1], w_attn[3]], axis=1).astype(bf16)
    vec_placed = lax.dynamic_update_slice(
        jnp.zeros((16, head_width), bf16), vectors.astype(bf16), (0, member * vec_shard)
    )
    qkv_shard = jnp.concatenate(
        [w_attn[:3].astype(bf16).reshape(3 * row_shard, head_width), vec_placed], axis=0
    )
    own_all = lax.all_gather(own_shard, "fsdp", axis=0, tiled=True)
    weight_pieces = gather_behind(own_shard)[1:]
    token_pieces = gather_behind(token_rows)
    qkv_all = lax.all_gather(qkv_shard, "fsdp", axis=0, tiled=False)
    w_qkv = [
        qkv_all[:, i * row_shard : (i + 1) * row_shard].reshape(model_width, head_width)
        for i in range(3)
    ]
    vec_own = jnp.sum(qkv_all[:, 3 * row_shard :].astype(f32), axis=0)[:vec_rows]
    vec_half = vec_own.astype(bf16)
    weight_pieces = after(weight_pieces, w_qkv, vec_half)
    cuts = (0, hidden_shard, 2 * hidden_shard, 2 * hidden_shard + head_width)
    rest_cat = jnp.concatenate(
        [
            piece[:, low:high]
            for low, high in zip(cuts[:-1], cuts[1:], strict=True)
            for piece in weight_pieces
        ],
        axis=1,
    )
    rest_all = lax.all_gather(rest_cat, "fsdp", axis=0, tiled=True)
    up_parts, down_parts, out_parts = (
        [own_all[:, low:high], rest_all[:, low * (seq_count - 1) : high * (seq_count - 1)]]
        for low, high in zip(cuts[:-1], cuts[1:], strict=True)
    )

    def times(left, parts):
        return jnp.concatenate(
            [jnp.dot(left, part, preferred_element_type=f32) for part in parts], axis=1
        )

    def times_t(left, parts):
        width = parts[0].shape[1]
        return dot_right_t(left[:, :width], parts[0]) + dot_right_t(left[:, width:], parts[1])

    vec_near = [piece.astype(f32) for piece in gather_behind(vec_half)]

    def near(order):
        return sum(jnp.where(order == r, piece, 0.0) for r, piece in enumerate(vec_near))

    vec_wide = jnp.concatenate(
        [near((place - j) % seq_count) for j in range(seq_count)], axis=1
    )
    up_bias = turn_blocks(vec_wide[8:12].reshape(seq_count, hidden_shard)).reshape(-1)

    valid_len = lengths[0]
    queries, keys_all, values_all, lse, mixed_all, *mixed_pieces = attend(
        place, valid_len, vec_own[:2], after(token_pieces, vec_wide, up_bias), w_qkv
    )
    mixed_rows = jnp.concatenate(swap_behind(mixed_pieces), axis=1)

    hidden_one = token_rows.astype(f32) + times_t(mixed_rows, out_parts) + vec_wide[2]
    normed_one, inv_one = layer_norm(hidden_one)
    resid_one = normed_one * vec_wide[4] + vec_wide[5]
    resid_half = resid_one.astype(bf16)
    preact = times(resid_half, up_parts) + up_bias
    activation, gelu_slope = gelu_pair(preact)
    act_half = activation.astype(bf16)
    hidden_two = resid_one + times_t(act_half, down_parts) + vec_wide[3]
    normed_two, inv_two = layer_norm(hidden_two)
    block_out = (normed_two * vec_wide[6] + vec_wide[7]).astype(bf16)
    grad_two = norm_back(cot_rows * vec_wide[6], normed_two, inv_two)
    grad_two_half = grad_two.astype(bf16)

    def outer(left, right):
        return lax.dot_general(
            left, right, (((0,), (0,)), ((), ())), preferred_element_type=f32
        ).astype(bf16)

    def total_of(pieces):
        total = pieces[0].astype(f32)
        for piece in pieces[1:]:
            total = total + piece.astype(f32)
        return total

    def halves_of(pieces):
        return [piece.astype(bf16) for piece in pieces]

    down_local, grad_two_half = lax.optimization_barrier(
        (outer(grad_two_half, act_half), grad_two_half)
    )
    down_part = lax.psum_scatter(down_local, "fsdp", scatter_dimension=0, tiled=True)
    grad_pre_half = (times(grad_two_half, down_parts) * gelu_slope).astype(bf16)
    up_kept, up_sent = halving(
        outer(resid_half, grad_pre_half).reshape(fsdp_count, row_shard, -1), bits[0], True
    )
    up_sent, up_kept, grad_pre_half = lax.optimization_barrier((up_sent, up_kept, grad_pre_half))
    up_received = swapped(up_sent, bits[0])
    grad_resid = grad_two + times_t(grad_pre_half, up_parts)
    grad_one = norm_back(grad_resid * vec_wide[4], normed_one, inv_one)
    grad_one_half = grad_one.astype(bf16)
    grad_mixed = times(grad_one_half, out_parts).astype(bf16)
    grad_pieces = swap_behind(jnp.split(grad_mixed, seq_count, axis=1))

    out_kept, out_sent = halving(
        outer(after(grad_one_half, grad_mixed), mixed_rows).reshape(fsdp_count, row_shard, -1),
        bits[0],
        True,
    )
    out_received = swapped(out_sent, bits[0])
    up_wide = joined(up_kept, up_received)
    out_wide = joined(out_kept, out_received)
    near_places = seq_count // 2
    up_cut, out_cut = near_places * hidden_shard, near_places * head_width
    wide = [
        jnp.concatenate([up_wide[..., :up_cut], out_wide[..., :out_cut]], axis=-1),
        jnp.concatenate([up_wide[..., up_cut:], out_wide[..., out_cut:]], axis=-1),
    ]
    routes = [list(bits[1:]), list(reversed(bits[1:]))]
    wide_moving = []
    for half, route, low in zip(wide, routes, (True, False), strict=True):
        kept, sent = halving(half, route[0], low)
        wide_moving.append((kept, swapped(sent, route[0])))
        grad_pieces = after(grad_pieces, sent)

    grad_qkv, head_sums, input_own, *input_parts = attend_back(
        place,
        valid_len,
        queries,
        keys_all,
        values_all,
        lse,
        mixed_all,
        grad_pieces,
        w_qkv,
    )
    input_moved = swap_behind([input_own, *input_parts])
    vec_blocks = vector_sums(
        place,
        seq_count,
        head_width,
        after(grad_one, input_own),
        grad_two,
        grad_resid,
        normed_one,
        normed_two,
        cot_half,
        grad_pre_half,
    )
    vec_order = turn_blocks(vec_blocks)
    vec_moved = swap_behind([vec_order[r] for r in range(seq_count)])
    vec_part = sum(vec_moved)
    vec_lines = jnp.concatenate(
        [head_sums[:1, :head_width], head_sums[:1, 2 * head_width :], vec_part[2:]], axis=0
    )
    vec_lines = jnp.pad(vec_lines, ((0, 0), (0, 2 * head_width)))
    token_all = jnp.concatenate(token_pieces, axis=0)
    qkv_local = lax.dot_general(
        token_all, grad_qkv, (((0,), (0,)), ((), ())), preferred_element_type=f32
    ).astype(bf16)
    qkv_blocks = jnp.concatenate(
        [
            qkv_local.reshape(fsdp_count, row_shard, 3 * head_width),
            jnp.broadcast_to(
                vec_lines.astype(bf16)[None], (fsdp_count, 16, 3 * head_width)
            ),
        ],
        axis=1,
    )

    def place_pieces(half, count):
        ups, outs = half[:, : count * hidden_shard], half[:, count * hidden_shard :]
        return [
            jnp.concatenate(
                [
                    ups[:, r * hidden_shard : (r + 1) * hidden_shard],
                    outs[:, r * head_width : (r + 1) * head_width],
                ],
                axis=1,
            )
            for r in range(count)
        ]

    qkv_kept, qkv_sent = halving(qkv_blocks, bits[0], True)
    qkv_received = swapped(qkv_sent, bits[0])
    step = qkv_sent
    down_moved = None
    for at in range(1, len(bits)):
        moving = []
        for (kept, received), route, low in zip(wide_moving, routes, (True, False), strict=True):
            half = joined(kept, after(received, step))
            if at < len(bits) - 1:
                kept, sent = halving(half, route[at], low)
                moving.append((kept, swapped(sent, route[at])))
                step = sent
            else:
                moving.append(half[0])
        wide_moving = moving
        if down_moved is None:
            down_pieces = jnp.split(after(down_part, step), seq_count, axis=1)
            down_moved = swap_behind(down_pieces)
            step = down_pieces
    wide_pieces = place_pieces(wide_moving[0], near_places) + place_pieces(
        wide_moving[1], seq_count - near_places
    )
    wide_sent = halves_of(wide_pieces[1:])
    wide_moved = swap_behind([wide_pieces[0]] + wide_sent)
    step = wide_sent
    for bit in bits[1:]:
        qkv_half = joined(qkv_kept, after(qkv_received, step))
        qkv_kept, qkv_sent = halving(qkv_half, bit, True)
        qkv_received = swapped(qkv_sent, bit)
        step = qkv_sent
    qkv_sum = joined(qkv_kept, qkv_received)[0]
    input_grad = grad_one + total_of([input_moved[0]] + after(input_moved[1:], qkv_sum))
    down_sum = total_of([down_moved[0]] + after(down_moved[1:], input_grad))
    up_out_sum = total_of([wide_moved[0]] + after(wide_moved[1:], down_sum))

    token_total = shard_len * seq_count * fsdp_count
    grad_scale = float(token_total) ** (-0.5)
    attn_grad = grad_scale * with_layout_constraint(
        jnp.stack(
            [
                qkv_sum[:row_shard, i * head_width : (i + 1) * head_width]
                for i in range(3)
            ]
            + [up_out_sum[:, hidden_shard:]]
        ),
        Layout(major_to_minor=(0, 1, 2)),
    )
    ffn_grad = grad_scale * jnp.stack([up_out_sum[:, :hidden_shard], down_sum])
    vec_grad = grad_scale * lax.dynamic_slice(
        qkv_sum[row_shard:], (0, member * vec_shard), (vec_rows, vec_shard)
    )
    attn_new, attn_one, attn_two = adam_step(
        w_attn, attn_grad, attn_first, attn_second, WEIGHT_DECAY
    )
    ffn_new, ffn_one, ffn_two = adam_step(w_ffn, ffn_grad, ffn_first, ffn_second, WEIGHT_DECAY)
    vec_new, vec_one, vec_two = adam_step(vectors, vec_grad, vec_first, vec_second, 0.0)
    return (
        block_out.reshape(tokens.shape),
        input_grad.reshape(tokens.shape),
        attn_grad,
        ffn_grad,
        vec_grad,
        attn_new,
        attn_one,
        attn_two,
        ffn_new,
        ffn_one,
        ffn_two,
        vec_new,
        vec_one,
        vec_two,
    )


def solution(mesh):
    placed = (
        P("fsdp", "seq", None),
        P("fsdp", "seq", None),
        P("fsdp"),
        P(None, "fsdp", "seq"),
        P(None, "fsdp", "seq"),
        P(None, "fsdp", "seq"),
        P(None, "fsdp", "seq"),
        P(None, "fsdp", "seq"),
        P(None, "fsdp", "seq"),
        P(None, ("seq", "fsdp")),
        P(None, ("seq", "fsdp")),
        P(None, ("seq", "fsdp")),
    )
    return jax.shard_map(
        layer,
        mesh=mesh,
        in_specs=placed,
        out_specs=(
            P("fsdp", "seq", None),
            P("fsdp", "seq", None),
            P(None, "fsdp", "seq"),
            P(None, "fsdp", "seq"),
            P(None, ("seq", "fsdp")),
            P(None, "fsdp", "seq"),
            P(None, "fsdp", "seq"),
            P(None, "fsdp", "seq"),
            P(None, "fsdp", "seq"),
            P(None, "fsdp", "seq"),
            P(None, "fsdp", "seq"),
            P(None, ("seq", "fsdp")),
            P(None, ("seq", "fsdp")),
            P(None, ("seq", "fsdp")),
        ),
        check_vma=False,
    )
```

```python
import math

import jax
import jax.numpy as jnp
from jax import lax
from jax.experimental import pallas as pl
from jax.experimental.layout import Layout, with_layout_constraint
from jax.experimental.pallas import tpu as pltpu
from jax.sharding import PartitionSpec as P


HEAD = 64
STEP = 3
SCORE_SCALE = 1.0 / math.sqrt(HEAD)


EPS_NORM = 1e-12
ADAM_RATE = 0.005
BETA_ONE = 0.9
BETA_TWO = 0.999
ADAM_EPS = 1e-08
WEIGHT_DECAY = 0.01


def layer_norm(values):
    center = values - jnp.mean(values, axis=-1, keepdims=True)
    inv_scale = lax.rsqrt(jnp.mean(center * center, axis=-1, keepdims=True) + EPS_NORM)
    return (center * inv_scale, inv_scale)


def norm_back(grad_normed, normed, inv_scale):
    return inv_scale * (
        grad_normed
        - jnp.mean(grad_normed, axis=-1, keepdims=True)
        - normed * jnp.mean(grad_normed * normed, axis=-1, keepdims=True)
    )


def gelu_pair(preact):
    normal_cdf = 0.5 * (1.0 + jax.scipy.special.erf(preact * (1.0 / math.sqrt(2.0))))
    density = jnp.exp(-0.5 * preact * preact) * (1.0 / math.sqrt(2.0 * math.pi))
    return (preact * normal_cdf, normal_cdf + preact * density)


def dot_right_t(left, right):
    return lax.dot_general(
        left, right, (((1,), (1,)), ((), ())), preferred_element_type=jnp.float32
    )


def across(piece, bits):
    count = lax.axis_size("seq")
    return lax.ppermute(piece, "seq", [(i, i ^ bits) for i in range(count)])


def seq_bits():
    return range(lax.axis_size("seq").bit_length() - 1)


def gather_across(piece):
    pieces = {0: piece}
    for bit in reversed(seq_bits()):
        for r in sorted(pieces, reverse=True):
            pieces[r | 1 << bit] = across(pieces[r], 1 << bit)
    return [pieces[r] for r in sorted(pieces)]


def swap_across(pieces):
    return pieces[:1] + [across(piece, r) for r, piece in enumerate(pieces) if r]


def sum_across(pieces):
    count = len(pieces)
    totals = {r: [piece] for r, piece in enumerate(pieces)}
    for bit in seq_bits():
        step = 1 << bit
        for r in reversed(range(step, count, 2 * step)):
            terms = totals.pop(r)
            sent = terms[0].astype(jnp.bfloat16) if len(terms) == 1 else total_of(terms)
            totals[r - step].append(across(sent.astype(jnp.bfloat16), step))
    return totals[0]


def total_of(pieces):
    total = pieces[0].astype(jnp.float32)
    for piece in pieces[1:]:
        total = total + piece.astype(jnp.float32)
    return total


def turn_blocks(blocks):
    count = blocks.shape[0]
    place = lax.axis_index("seq")
    order = place ^ jnp.arange(count, dtype=jnp.int32)
    mask = order[:, None] == jnp.arange(count, dtype=jnp.int32)[None, :]
    mask = mask.reshape((count, count) + (1,) * (blocks.ndim - 1))
    return jnp.sum(jnp.where(mask, blocks[None], jnp.zeros((), blocks.dtype)), axis=1)


def adam_step(parameter, gradient, moment_one, moment_two, decay_rate):
    one_new = BETA_ONE * moment_one + (1.0 - BETA_ONE) * gradient
    two_new = BETA_TWO * moment_two + (1.0 - BETA_TWO) * gradient * gradient
    one_hat = one_new / (1.0 - BETA_ONE**STEP)
    two_hat = two_new / (1.0 - BETA_TWO**STEP)
    update = one_hat / (jnp.sqrt(two_hat) + ADAM_EPS)
    return (parameter - ADAM_RATE * (update + decay_rate * parameter), one_new, two_new)


def after(values, *earlier):
    return lax.optimization_barrier((values, earlier))[0]


def halving(blocks, bit, from_low):
    count = blocks.shape[0]
    own = (lax.axis_index("fsdp") >> bit) & 1
    split = (count // 2, 2) if from_low else (2, count // 2)
    axis = 1 if from_low else 0
    view = blocks.reshape(split + blocks.shape[1:])
    kept = lax.dynamic_index_in_dim(view, own, axis, keepdims=False)
    sent = lax.dynamic_index_in_dim(view, 1 - own, axis, keepdims=False)
    return kept, sent.astype(jnp.bfloat16)


def swapped(sent, bit):
    pairs = [(i, i ^ (1 << bit)) for i in range(lax.axis_size("fsdp"))]
    return lax.ppermute(sent, "fsdp", pairs)


def joined(kept, received):
    return kept.astype(jnp.float32) + received.astype(jnp.float32)


def attend_kernel(
    place_ref, length_ref, bias_ref, *refs
):
    count = (len(refs) - 3 - 4 - 2) // 2
    token_refs, weight_refs = refs[:count], refs[count : count + 3]
    q_ref, k_ref, v_ref, lse_ref = refs[count + 3 : count + 7]
    mixed_refs, (mixed_all, token_all) = refs[count + 7 : -2], refs[-2:]
    shard_len = token_refs[0].shape[0]
    _, width = q_ref.shape
    for r, token_ref in enumerate(token_refs):
        token_all[r * shard_len : (r + 1) * shard_len, :] = token_ref[...]

    def project(i, carry):
        at = pl.ds(pl.multiple_of(i * shard_len, shard_len), shard_len)
        piece = token_all[at, :]
        for k, (weight_ref, out_ref) in enumerate(
            zip(weight_refs, (q_ref, k_ref, v_ref), strict=True)
        ):
            out = jnp.dot(piece, weight_ref[...], preferred_element_type=jnp.float32)
            if k != 1:
                out = out + bias_ref[k // 2 : k // 2 + 1, :]
            out_ref[at, :] = out.astype(jnp.bfloat16)
        return carry

    lax.fori_loop(0, count, project, 0)
    masked = key_mask(place_ref[0], length_ref[0], count, shard_len)


    def block(i, carry):
        at = pl.ds(pl.multiple_of(i * shard_len, shard_len), shard_len)
        queries = q_ref[at, :]
        mixed = []
        for h in range(width // HEAD):
            cols = slice(h * HEAD, (h + 1) * HEAD)
            scores = dot_right_t(queries[:, cols] * SCORE_SCALE, k_ref[:, cols]) + masked
            top = jnp.max(scores, axis=1, keepdims=True)
            raised = jnp.exp(scores - top)
            total = jnp.sum(raised, axis=1, keepdims=True)
            probs = (raised * (1.0 / total)).astype(jnp.bfloat16)
            mixed.append(jnp.dot(probs, v_ref[:, cols], preferred_element_type=jnp.float32))
            lse_ref[at, h : h + 1] = top + jnp.log(total)
        mixed_all[at, :] = jnp.concatenate(mixed, axis=1).astype(jnp.bfloat16)
        return carry

    lax.fori_loop(0, count, block, 0)
    for i, mixed_ref in enumerate(mixed_refs):
        mixed_ref[...] = mixed_all[i * shard_len : (i + 1) * shard_len, :]


def key_mask(place, length, count, shard_len):
    column = lax.broadcasted_iota(jnp.int32, (1, shard_len), 1)
    pieces = []
    for r in range(count):
        start = (place ^ r) * shard_len
        pieces.append(jnp.where(column + start < length, 0.0, -jnp.inf))
    return jnp.concatenate(pieces, axis=1)


def attend(place, length, bias, token_pieces, weights):
    shard_len = token_pieces[0].shape[0]
    rows, width = shard_len * len(token_pieces), weights[0].shape[1]
    half = jax.ShapeDtypeStruct((rows, width), jnp.bfloat16)
    smem, vmem = pl.BlockSpec(memory_space=pltpu.SMEM), pl.BlockSpec(memory_space=pltpu.VMEM)
    arrays = (bias, *token_pieces, *weights)
    return pl.pallas_call(
        attend_kernel,
        out_shape=(half, half, half, jax.ShapeDtypeStruct((rows, 8), jnp.float32))
        + (jax.ShapeDtypeStruct((shard_len, width), jnp.bfloat16),) * len(token_pieces),
        in_specs=[smem, smem] + [vmem] * len(arrays),
        out_specs=(vmem,) * (4 + len(token_pieces)),
        scratch_shapes=[
            pltpu.VMEM((rows, width), jnp.bfloat16),
            pltpu.VMEM((rows, weights[0].shape[0]), jnp.bfloat16),
        ],
        compiler_params=pltpu.CompilerParams(vmem_limit_bytes=40 << 20),
        cost_estimate=pl.CostEstimate(
            flops=2 * rows * width * (3 * weights[0].shape[0] + 8 * rows),
            bytes_accessed=8 << 20,
            transcendentals=rows * rows * (width // HEAD),
        ),
        name="attend",
    )(place.reshape(1), length.reshape(1), *arrays)


def attend_back_kernel(
    place_ref,
    length_ref,
    q_ref,
    k_ref,
    v_ref,
    lse_ref,
    *refs,
):
    count = (len(refs) - 3 - 2 - 5) // 3
    mixed_refs, grad_refs = refs[:count], refs[count : 2 * count]
    weight_refs, refs = refs[2 * count : 2 * count + 3], refs[2 * count + 3 :]
    all_ref, sums_ref = refs[:2]
    part_refs = refs[2 : 2 + count]
    dk_sum, dv_sum, mixed_all, grad_all, part_all = refs[2 + count :]
    shard_len = grad_refs[0].shape[0]
    _, width = q_ref.shape
    masked = key_mask(place_ref[0], length_ref[0], count, shard_len)
    for i in range(count):
        at = slice(i * shard_len, (i + 1) * shard_len)
        mixed_all[at, :] = mixed_refs[i][...]
        grad_all[at, :] = grad_refs[i][...]
    dk_sum[...] = jnp.zeros_like(dk_sum)
    dv_sum[...] = jnp.zeros_like(dv_sum)

    def block(i, carry):
        at = pl.ds(pl.multiple_of(i * shard_len, shard_len), shard_len)
        queries, grad = q_ref[at, :], grad_all[at, :]
        product = grad.astype(jnp.float32) * mixed_all[at, :].astype(jnp.float32)
        parts = []
        for h in range(width // HEAD):
            cols = slice(h * HEAD, (h + 1) * HEAD)
            head_q, head_grad = queries[:, cols], grad[:, cols]
            scores = dot_right_t(head_q * SCORE_SCALE, k_ref[:, cols]) + masked
            probs = jnp.exp(scores - lse_ref[at, h : h + 1])
            delta = jnp.sum(product[:, cols], axis=1, keepdims=True)
            grad_probs = dot_right_t(head_grad, v_ref[:, cols])
            grad_scores = (probs * (grad_probs - delta)).astype(jnp.bfloat16)
            parts.append(
                jnp.dot(grad_scores, k_ref[:, cols], preferred_element_type=jnp.float32)
                * SCORE_SCALE
            )
            dk_sum[cols, :] += jnp.dot(head_q.T, grad_scores, preferred_element_type=jnp.float32)
            dv_sum[cols, :] += jnp.dot(
                head_grad.T, probs.astype(jnp.bfloat16), preferred_element_type=jnp.float32
            )
        all_ref[at, :width] = jnp.concatenate(parts, axis=1).astype(jnp.bfloat16)
        return carry

    lax.fori_loop(0, count, block, 0)
    all_ref[:, width : 2 * width] = (dk_sum[...].T * SCORE_SCALE).astype(jnp.bfloat16)
    all_ref[:, 2 * width :] = dv_sum[...].T.astype(jnp.bfloat16)
    sums_ref[...] = jnp.zeros_like(sums_ref)
    sums_ref[:1, :] = jnp.sum(all_ref[...].astype(jnp.float32), axis=0, keepdims=True)

    def part_of(at):
        part = dot_right_t(all_ref[at, :width], weight_refs[0][...])
        part = part + dot_right_t(all_ref[at, width : 2 * width], weight_refs[1][...])
        return part + dot_right_t(all_ref[at, 2 * width :], weight_refs[2][...])

    def other(i, carry):
        at = pl.ds(pl.multiple_of(i * shard_len, shard_len), shard_len)
        part_all[at, :] = part_of(at).astype(jnp.bfloat16)
        return carry

    part_refs[0][...] = part_of(slice(0, shard_len))
    lax.fori_loop(1, count, other, 0)
    for i in range(1, count):
        part_refs[i][...] = part_all[i * shard_len : (i + 1) * shard_len, :]


def attend_back(
    place, length, queries, keys_all, values_all, lse, mixed_pieces, grad_pieces, weights
):
    rows, width = queries.shape
    shard_len, model_width = mixed_pieces[0].shape[0], weights[0].shape[0]
    smem, vmem = pl.BlockSpec(memory_space=pltpu.SMEM), pl.BlockSpec(memory_space=pltpu.VMEM)
    arrays = (queries, keys_all, values_all, lse, *mixed_pieces, *grad_pieces, *weights)
    parts = [jax.ShapeDtypeStruct((shard_len, model_width), jnp.float32)] + [
        jax.ShapeDtypeStruct((shard_len, model_width), jnp.bfloat16)
    ] * (len(mixed_pieces) - 1)
    return pl.pallas_call(
        attend_back_kernel,
        out_shape=(
            jax.ShapeDtypeStruct((rows, 3 * width), jnp.bfloat16),
            jax.ShapeDtypeStruct((16, 3 * width), jnp.float32),
            *parts,
        ),
        in_specs=[smem, smem] + [vmem] * len(arrays),
        out_specs=(vmem,) * (2 + len(parts)),
        scratch_shapes=[pltpu.VMEM((width, rows), jnp.float32)] * 2
        + [pltpu.VMEM((rows, width), jnp.bfloat16)] * 2
        + [pltpu.VMEM((rows, model_width), jnp.bfloat16)],
        compiler_params=pltpu.CompilerParams(vmem_limit_bytes=48 << 20),
        cost_estimate=pl.CostEstimate(
            flops=20 * rows * width * rows,
            bytes_accessed=8 << 20,
            transcendentals=rows * rows * (width // HEAD),
        ),
        name="attend_back",
    )(place.reshape(1), length.reshape(1), *arrays)


def vector_kernel(
    place_ref, one_ref, two_ref, resid_ref, normed_one_ref, normed_two_ref, cot_ref, pre_ref, out_ref
):
    seq_count, _, head_width = out_ref.shape
    model_width = one_ref.shape[1]
    resid = resid_ref[...]
    cot = cot_ref[...].astype(jnp.float32)
    rows = [
        one_ref[...],
        two_ref[...],
        resid * normed_one_ref[...],
        resid,
        cot * normed_two_ref[...],
        cot,
    ]
    out_ref[...] = jnp.zeros_like(out_ref)
    for k, values in enumerate(rows):
        total = jnp.sum(values, axis=0, keepdims=True)
        for j in range(seq_count):
            out_ref[j, 2 + k : 3 + k, :] = total[:, j * head_width : (j + 1) * head_width]
    pre = pre_ref[...].astype(jnp.float32)
    per_place = pre.shape[1] // seq_count // model_width
    totals = [
        jnp.sum(pre[:, k * model_width : (k + 1) * model_width], axis=0, keepdims=True)
        for k in range(seq_count * per_place)
    ]
    for k in range(seq_count):
        owner = place_ref[0] ^ k
        for i in range(per_place):
            row = 8 + owner * per_place + i
            total = totals[k * per_place + i]
            for j in range(seq_count):
                out_ref[j, pl.ds(row, 1), :] = total[:, j * head_width : (j + 1) * head_width]


def vector_sums(place, seq_count, head_width, *arrays):
    return pl.pallas_call(
        vector_kernel,
        out_shape=jax.ShapeDtypeStruct((seq_count, 16, head_width), jnp.float32),
        in_specs=[pl.BlockSpec(memory_space=pltpu.SMEM)]
        + [pl.BlockSpec(memory_space=pltpu.VMEM)] * len(arrays),
        out_specs=pl.BlockSpec(memory_space=pltpu.VMEM),
        compiler_params=pltpu.CompilerParams(vmem_limit_bytes=32 << 20),
        name="vector_sums",
    )(place.reshape(1), *arrays)


def layer(
    tokens,
    cotangent,
    lengths,
    w_attn,
    attn_first,
    attn_second,
    w_ffn,
    ffn_first,
    ffn_second,
    vectors,
    vec_first,
    vec_second,
):
    bf16, f32 = jnp.bfloat16, jnp.float32
    _, shard_len, model_width = tokens.shape
    seq_count, fsdp_count = lax.axis_size("seq"), lax.axis_size("fsdp")
    place, member = lax.axis_index("seq"), lax.axis_index("fsdp")
    _, row_shard, head_width = w_attn.shape
    hidden_shard = w_ffn.shape[2]
    vec_rows, vec_shard = vectors.shape
    token_rows = tokens.reshape(shard_len, model_width)
    cot_half = cotangent.reshape(shard_len, model_width)
    cot_rows = cot_half.astype(f32)
    bits = list(range(fsdp_count.bit_length() - 1))

    own_shard = jnp.concatenate([w_ffn[0], w_ffn[1], w_attn[3]], axis=1).astype(bf16)
    vec_placed = lax.dynamic_update_slice(
        jnp.zeros((16, head_width), bf16), vectors.astype(bf16), (0, member * vec_shard)
    )
    qkv_shard = jnp.concatenate(
        [w_attn[:3].astype(bf16).reshape(3 * row_shard, head_width), vec_placed], axis=0
    )
    own_all = lax.all_gather(own_shard, "fsdp", axis=0, tiled=True)
    weight_pieces = gather_across(own_shard)[1:]
    token_pieces = gather_across(token_rows)
    qkv_all = lax.all_gather(qkv_shard, "fsdp", axis=0, tiled=False)
    w_qkv = [
        qkv_all[:, i * row_shard : (i + 1) * row_shard].reshape(model_width, head_width)
        for i in range(3)
    ]
    vec_own = jnp.sum(qkv_all[:, 3 * row_shard :].astype(f32), axis=0)[:vec_rows]
    vec_half = vec_own.astype(bf16)
    cuts = (0, hidden_shard, 2 * hidden_shard, 2 * hidden_shard + head_width)
    rest_cat = jnp.concatenate(
        [
            piece[:, low:high]
            for low, high in zip(cuts[:-1], cuts[1:], strict=True)
            for piece in weight_pieces
        ],
        axis=1,
    )
    rest_all = lax.all_gather(rest_cat, "fsdp", axis=0, tiled=True)
    up_parts, down_parts, out_parts = (
        [own_all[:, low:high], rest_all[:, low * (seq_count - 1) : high * (seq_count - 1)]]
        for low, high in zip(cuts[:-1], cuts[1:], strict=True)
    )

    def times(left, parts):
        return jnp.concatenate(
            [jnp.dot(left, part, preferred_element_type=f32) for part in parts], axis=1
        )

    def times_t(left, parts):
        width = parts[0].shape[1]
        return dot_right_t(left[:, :width], parts[0]) + dot_right_t(left[:, width:], parts[1])

    vec_near = [piece.astype(f32) for piece in gather_across(vec_half)]

    def near(order):
        return sum(jnp.where(order == r, piece, 0.0) for r, piece in enumerate(vec_near))

    vec_wide = jnp.concatenate(
        [near(place ^ j) for j in range(seq_count)], axis=1
    )
    up_bias = turn_blocks(vec_wide[8:12].reshape(seq_count, hidden_shard)).reshape(-1)

    valid_len = lengths[0]
    queries, keys_all, values_all, lse, *mixed_pieces = attend(
        place, valid_len, vec_own[:2], after(token_pieces, vec_wide, up_bias), w_qkv
    )
    mixed_rows = jnp.concatenate(swap_across(mixed_pieces), axis=1)

    hidden_one = token_rows.astype(f32) + times_t(mixed_rows, out_parts) + vec_wide[2]
    normed_one, inv_one = layer_norm(hidden_one)
    resid_one = normed_one * vec_wide[4] + vec_wide[5]
    resid_half = resid_one.astype(bf16)
    preact = times(resid_half, up_parts) + up_bias
    activation, gelu_slope = gelu_pair(preact)
    act_half = activation.astype(bf16)
    hidden_two = resid_one + times_t(act_half, down_parts) + vec_wide[3]
    normed_two, inv_two = layer_norm(hidden_two)
    block_out = (normed_two * vec_wide[6] + vec_wide[7]).astype(bf16)
    grad_two = norm_back(cot_rows * vec_wide[6], normed_two, inv_two)
    grad_two_half = grad_two.astype(bf16)

    def outer(left, right):
        return lax.dot_general(
            left, right, (((0,), (0,)), ((), ())), preferred_element_type=f32
        ).astype(bf16)

    down_local, grad_two_half = lax.optimization_barrier(
        (outer(grad_two_half, act_half), grad_two_half)
    )
    down_part = lax.psum_scatter(down_local, "fsdp", scatter_dimension=0, tiled=True)
    grad_pre_half = (times(grad_two_half, down_parts) * gelu_slope).astype(bf16)
    up_kept, up_sent = halving(
        outer(resid_half, grad_pre_half).reshape(fsdp_count, row_shard, -1), bits[0], True
    )
    up_sent, up_kept, grad_pre_half = lax.optimization_barrier((up_sent, up_kept, grad_pre_half))
    up_received = swapped(up_sent, bits[0])
    grad_resid = grad_two + times_t(grad_pre_half, up_parts)
    grad_one = norm_back(grad_resid * vec_wide[4], normed_one, inv_one)
    grad_one_half = grad_one.astype(bf16)
    grad_mixed = times(grad_one_half, out_parts).astype(bf16)
    grad_pieces = swap_across(jnp.split(grad_mixed, seq_count, axis=1))

    out_kept, out_sent = halving(
        outer(after(grad_one_half, grad_mixed), mixed_rows).reshape(fsdp_count, row_shard, -1),
        bits[0],
        True,
    )
    out_received = swapped(out_sent, bits[0])
    vec_blocks = vector_sums(
        place,
        seq_count,
        head_width,
        grad_one,
        grad_two,
        grad_resid,
        normed_one,
        normed_two,
        cot_half,
        grad_pre_half,
    )
    vec_order = turn_blocks(vec_blocks)
    vec_moved = swap_across([vec_order[r] for r in range(seq_count)])
    up_wide = joined(up_kept, up_received)
    out_wide = joined(out_kept, out_received)
    near_places = seq_count // 2
    up_cut, out_cut = near_places * hidden_shard, near_places * head_width
    wide = [
        jnp.concatenate([up_wide[..., :up_cut], out_wide[..., :out_cut]], axis=-1),
        jnp.concatenate([up_wide[..., up_cut:], out_wide[..., out_cut:]], axis=-1),
    ]
    routes = [list(bits[1:]), list(reversed(bits[1:]))]
    wide_moving = []
    for half, route, low in zip(wide, routes, (True, False), strict=True):
        kept, sent = halving(half, route[0], low)
        wide_moving.append((kept, swapped(sent, route[0])))
        grad_pieces = after(grad_pieces, sent)

    grad_qkv, head_sums, input_own, *input_parts = attend_back(
        place,
        valid_len,
        queries,
        keys_all,
        values_all,
        lse,
        mixed_pieces,
        grad_pieces,
        w_qkv,
    )
    input_terms = sum_across([input_own, *input_parts])
    vec_part = sum(after(vec_moved, input_own))
    vec_lines = jnp.concatenate(
        [head_sums[:1, :head_width], head_sums[:1, 2 * head_width :], vec_part[2:]], axis=0
    )
    vec_lines = jnp.pad(vec_lines, ((0, 0), (0, 2 * head_width)))
    token_all = jnp.concatenate(token_pieces, axis=0)
    qkv_local = lax.dot_general(
        token_all, grad_qkv, (((0,), (0,)), ((), ())), preferred_element_type=f32
    ).astype(bf16)
    qkv_blocks = jnp.concatenate(
        [
            qkv_local.reshape(fsdp_count, row_shard, 3 * head_width),
            jnp.broadcast_to(
                vec_lines.astype(bf16)[None], (fsdp_count, 16, 3 * head_width)
            ),
        ],
        axis=1,
    )

    def place_pieces(half, count):
        ups, outs = half[:, : count * hidden_shard], half[:, count * hidden_shard :]
        return [
            jnp.concatenate(
                [
                    ups[:, r * hidden_shard : (r + 1) * hidden_shard],
                    outs[:, r * head_width : (r + 1) * head_width],
                ],
                axis=1,
            )
            for r in range(count)
        ]

    qkv_kept, qkv_sent = halving(qkv_blocks, bits[0], True)
    qkv_received = swapped(qkv_sent, bits[0])
    step = qkv_sent
    down_moved = None
    for at in range(1, len(bits)):
        moving = []
        for (kept, received), route, low in zip(wide_moving, routes, (True, False), strict=True):
            half = joined(kept, after(received, step))
            if at < len(bits) - 1:
                kept, sent = halving(half, route[at], low)
                moving.append((kept, swapped(sent, route[at])))
                step = sent
            else:
                moving.append(half[0])
        wide_moving = moving
        if down_moved is None:
            down_pieces = jnp.split(after(down_part, step), seq_count, axis=1)
            down_moved = sum_across(down_pieces)
            step = down_pieces
    wide_pieces = place_pieces(wide_moving[0], near_places) + place_pieces(
        wide_moving[1], seq_count - near_places
    )
    wide_sent = [piece.astype(bf16) for piece in wide_pieces[1:]]
    wide_moved = sum_across([wide_pieces[0]] + wide_sent)
    step = wide_sent
    for bit in bits[1:]:
        qkv_half = joined(qkv_kept, after(qkv_received, step))
        qkv_kept, qkv_sent = halving(qkv_half, bit, True)
        qkv_received = swapped(qkv_sent, bit)
        step = qkv_sent
    qkv_sum = joined(qkv_kept, qkv_received)[0]
    input_grad = grad_one + total_of(input_terms[:1] + after(input_terms[1:], qkv_sum))
    down_sum = total_of(down_moved[:1] + after(down_moved[1:], input_grad))
    up_out_sum = total_of(wide_moved[:1] + after(wide_moved[1:], down_sum))

    token_total = shard_len * seq_count * fsdp_count
    grad_scale = float(token_total) ** (-0.5)
    attn_grad = grad_scale * with_layout_constraint(
        jnp.stack(
            [
                qkv_sum[:row_shard, i * head_width : (i + 1) * head_width]
                for i in range(3)
            ]
            + [up_out_sum[:, hidden_shard:]]
        ),
        Layout(major_to_minor=(0, 1, 2)),
    )
    ffn_grad = grad_scale * jnp.stack([up_out_sum[:, :hidden_shard], down_sum])
    vec_grad = grad_scale * lax.dynamic_slice(
        qkv_sum[row_shard:], (0, member * vec_shard), (vec_rows, vec_shard)
    )
    attn_new, attn_one, attn_two = adam_step(
        w_attn, attn_grad, attn_first, attn_second, WEIGHT_DECAY
    )
    ffn_new, ffn_one, ffn_two = adam_step(w_ffn, ffn_grad, ffn_first, ffn_second, WEIGHT_DECAY)
    vec_new, vec_one, vec_two = adam_step(vectors, vec_grad, vec_first, vec_second, 0.0)
    return (
        block_out.reshape(tokens.shape),
        input_grad.reshape(tokens.shape),
        attn_grad,
        ffn_grad,
        vec_grad,
        attn_new,
        attn_one,
        attn_two,
        ffn_new,
        ffn_one,
        ffn_two,
        vec_new,
        vec_one,
        vec_two,
    )


def solution(mesh):
    placed = (
        P("fsdp", "seq", None),
        P("fsdp", "seq", None),
        P("fsdp"),
        P(None, "fsdp", "seq"),
        P(None, "fsdp", "seq"),
        P(None, "fsdp", "seq"),
        P(None, "fsdp", "seq"),
        P(None, "fsdp", "seq"),
        P(None, "fsdp", "seq"),
        P(None, ("seq", "fsdp")),
        P(None, ("seq", "fsdp")),
        P(None, ("seq", "fsdp")),
    )
    return jax.shard_map(
        layer,
        mesh=mesh,
        in_specs=placed,
        out_specs=(
            P("fsdp", "seq", None),
            P("fsdp", "seq", None),
            P(None, "fsdp", "seq"),
            P(None, "fsdp", "seq"),
            P(None, ("seq", "fsdp")),
            P(None, "fsdp", "seq"),
            P(None, "fsdp", "seq"),
            P(None, "fsdp", "seq"),
            P(None, "fsdp", "seq"),
            P(None, "fsdp", "seq"),
            P(None, "fsdp", "seq"),
            P(None, ("seq", "fsdp")),
            P(None, ("seq", "fsdp")),
            P(None, ("seq", "fsdp")),
        ),
        check_vma=False,
    )
```

```python
import math

import jax
import jax.numpy as jnp
from jax import lax
from jax.experimental import pallas as pl
from jax.experimental.layout import Layout, with_layout_constraint
from jax.experimental.pallas import tpu as pltpu
from jax.sharding import PartitionSpec as P


HEAD = 64
STEP = 3
SCORE_SCALE = 1.0 / math.sqrt(HEAD)


EPS_NORM = 1e-12
ADAM_RATE = 0.005
BETA_ONE = 0.9
BETA_TWO = 0.999
ADAM_EPS = 1e-08
WEIGHT_DECAY = 0.01


def layer_norm(values):
    center = values - jnp.mean(values, axis=-1, keepdims=True)
    inv_scale = lax.rsqrt(jnp.mean(center * center, axis=-1, keepdims=True) + EPS_NORM)
    return (center * inv_scale, inv_scale)


def norm_back(grad_normed, normed, inv_scale):
    return inv_scale * (
        grad_normed
        - jnp.mean(grad_normed, axis=-1, keepdims=True)
        - normed * jnp.mean(grad_normed * normed, axis=-1, keepdims=True)
    )


def gelu_pair(preact):
    normal_cdf = 0.5 * (1.0 + jax.scipy.special.erf(preact * (1.0 / math.sqrt(2.0))))
    density = jnp.exp(-0.5 * preact * preact) * (1.0 / math.sqrt(2.0 * math.pi))
    return (preact * normal_cdf, normal_cdf + preact * density)


def dot_right_t(left, right):
    return lax.dot_general(
        left, right, (((1,), (1,)), ((), ())), preferred_element_type=jnp.float32
    )


def across(piece, bits):
    count = lax.axis_size("seq")
    return lax.ppermute(piece, "seq", [(i, i ^ bits) for i in range(count)])


def seq_bits():
    return range(lax.axis_size("seq").bit_length() - 1)


def gather_across(piece):
    pieces = {0: piece}
    for bit in reversed(seq_bits()):
        for r in sorted(pieces, reverse=True):
            pieces[r | 1 << bit] = across(pieces[r], 1 << bit)
    return [pieces[r] for r in sorted(pieces)]


def swap_across(pieces):
    return pieces[:1] + [across(piece, r) for r, piece in enumerate(pieces) if r]


def sum_first(pieces):
    totals = {r: [piece] for r, piece in enumerate(pieces)}
    return sum_bit(totals, 0, len(pieces)) if len(pieces) > 1 else totals


def sum_rest(totals, count):
    for bit in seq_bits()[1:]:
        totals = sum_bit(totals, bit, count)
    return totals[0]


def sum_bit(totals, bit, count):
    step = 1 << bit
    for r in reversed(range(step, count, 2 * step)):
        terms = totals.pop(r)
        sent = terms[0] if len(terms) == 1 else total_of(terms)
        totals[r - step].append(across(sent.astype(jnp.bfloat16), step))
    return totals


def sum_across(pieces):
    return sum_rest(sum_first(pieces), len(pieces))


def total_of(pieces):
    total = pieces[0].astype(jnp.float32)
    for piece in pieces[1:]:
        total = total + piece.astype(jnp.float32)
    return total


def turn_blocks(blocks):
    count = blocks.shape[0]
    place = lax.axis_index("seq")
    order = place ^ jnp.arange(count, dtype=jnp.int32)
    mask = order[:, None] == jnp.arange(count, dtype=jnp.int32)[None, :]
    mask = mask.reshape((count, count) + (1,) * (blocks.ndim - 1))
    return jnp.sum(jnp.where(mask, blocks[None], jnp.zeros((), blocks.dtype)), axis=1)


def adam_step(parameter, gradient, moment_one, moment_two, decay_rate):
    one_new = BETA_ONE * moment_one + (1.0 - BETA_ONE) * gradient
    two_new = BETA_TWO * moment_two + (1.0 - BETA_TWO) * gradient * gradient
    one_hat = one_new / (1.0 - BETA_ONE**STEP)
    two_hat = two_new / (1.0 - BETA_TWO**STEP)
    update = one_hat / (jnp.sqrt(two_hat) + ADAM_EPS)
    return (parameter - ADAM_RATE * (update + decay_rate * parameter), one_new, two_new)


def after(values, *earlier):
    return lax.optimization_barrier((values, earlier))[0]


def halving(blocks, bit, from_low):
    count = blocks.shape[0]
    own = (lax.axis_index("fsdp") >> bit) & 1
    split = (count // 2, 2) if from_low else (2, count // 2)
    axis = 1 if from_low else 0
    view = blocks.reshape(split + blocks.shape[1:])
    kept = lax.dynamic_index_in_dim(view, own, axis, keepdims=False)
    sent = lax.dynamic_index_in_dim(view, 1 - own, axis, keepdims=False)
    return kept, sent.astype(jnp.bfloat16)


def swapped(sent, bit):
    pairs = [(i, i ^ (1 << bit)) for i in range(lax.axis_size("fsdp"))]
    return lax.ppermute(sent, "fsdp", pairs)


def joined(kept, received):
    return kept.astype(jnp.float32) + received.astype(jnp.float32)


def attend_kernel(
    place_ref, length_ref, bias_ref, *refs
):
    count = (len(refs) - 3 - 4 - 2) // 2
    token_refs, weight_refs = refs[:count], refs[count : count + 3]
    q_ref, k_ref, v_ref, lse_ref = refs[count + 3 : count + 7]
    mixed_refs, (mixed_all, token_all) = refs[count + 7 : -2], refs[-2:]
    shard_len = token_refs[0].shape[0]
    _, width = q_ref.shape
    for r, token_ref in enumerate(token_refs):
        token_all[r * shard_len : (r + 1) * shard_len, :] = token_ref[...]

    def project(i, carry):
        at = pl.ds(pl.multiple_of(i * shard_len, shard_len), shard_len)
        piece = token_all[at, :]
        for k, (weight_ref, out_ref) in enumerate(
            zip(weight_refs, (q_ref, k_ref, v_ref), strict=True)
        ):
            out = jnp.dot(piece, weight_ref[...], preferred_element_type=jnp.float32)
            if k != 1:
                out = out + bias_ref[k // 2 : k // 2 + 1, :]
            out_ref[at, :] = out.astype(jnp.bfloat16)
        return carry

    lax.fori_loop(0, count, project, 0)
    masked = key_mask(place_ref[0], length_ref[0], count, shard_len)


    def block(i, carry):
        at = pl.ds(pl.multiple_of(i * shard_len, shard_len), shard_len)
        queries = q_ref[at, :]
        mixed = []
        for h in range(width // HEAD):
            cols = slice(h * HEAD, (h + 1) * HEAD)
            scores = dot_right_t(queries[:, cols] * SCORE_SCALE, k_ref[:, cols]) + masked
            top = jnp.max(scores, axis=1, keepdims=True)
            raised = jnp.exp(scores - top)
            total = jnp.sum(raised, axis=1, keepdims=True)
            probs = (raised * (1.0 / total)).astype(jnp.bfloat16)
            mixed.append(jnp.dot(probs, v_ref[:, cols], preferred_element_type=jnp.float32))
            lse_ref[at, h : h + 1] = top + jnp.log(total)
        mixed_all[at, :] = jnp.concatenate(mixed, axis=1).astype(jnp.bfloat16)
        return carry

    lax.fori_loop(0, count, block, 0)
    for i, mixed_ref in enumerate(mixed_refs):
        mixed_ref[...] = mixed_all[i * shard_len : (i + 1) * shard_len, :]


def key_mask(place, length, count, shard_len):
    column = lax.broadcasted_iota(jnp.int32, (1, shard_len), 1)
    pieces = []
    for r in range(count):
        start = (place ^ r) * shard_len
        pieces.append(jnp.where(column + start < length, 0.0, -jnp.inf))
    return jnp.concatenate(pieces, axis=1)


def attend(place, length, bias, token_pieces, weights):
    shard_len = token_pieces[0].shape[0]
    rows, width = shard_len * len(token_pieces), weights[0].shape[1]
    half = jax.ShapeDtypeStruct((rows, width), jnp.bfloat16)
    smem, vmem = pl.BlockSpec(memory_space=pltpu.SMEM), pl.BlockSpec(memory_space=pltpu.VMEM)
    arrays = (bias, *token_pieces, *weights)
    return pl.pallas_call(
        attend_kernel,
        out_shape=(half, half, half, jax.ShapeDtypeStruct((rows, 8), jnp.float32))
        + (jax.ShapeDtypeStruct((shard_len, width), jnp.bfloat16),) * len(token_pieces),
        in_specs=[smem, smem] + [vmem] * len(arrays),
        out_specs=(vmem,) * (4 + len(token_pieces)),
        scratch_shapes=[
            pltpu.VMEM((rows, width), jnp.bfloat16),
            pltpu.VMEM((rows, weights[0].shape[0]), jnp.bfloat16),
        ],
        compiler_params=pltpu.CompilerParams(vmem_limit_bytes=40 << 20),
        cost_estimate=pl.CostEstimate(
            flops=2 * rows * width * (3 * weights[0].shape[0] + 8 * rows),
            bytes_accessed=8 << 20,
            transcendentals=rows * rows * (width // HEAD),
        ),
        name="attend",
    )(place.reshape(1), length.reshape(1), *arrays)


def attend_back_kernel(
    place_ref,
    length_ref,
    q_ref,
    k_ref,
    v_ref,
    lse_ref,
    *refs,
):
    count = (len(refs) - 3 - 2 - 5) // 3
    mixed_refs, grad_refs = refs[:count], refs[count : 2 * count]
    weight_refs, refs = refs[2 * count : 2 * count + 3], refs[2 * count + 3 :]
    all_ref, sums_ref = refs[:2]
    part_refs = refs[2 : 2 + count]
    dk_sum, dv_sum, mixed_all, grad_all, part_all = refs[2 + count :]
    shard_len = grad_refs[0].shape[0]
    _, width = q_ref.shape
    masked = key_mask(place_ref[0], length_ref[0], count, shard_len)
    for i in range(count):
        at = slice(i * shard_len, (i + 1) * shard_len)
        mixed_all[at, :] = mixed_refs[i][...]
        grad_all[at, :] = grad_refs[i][...]
    dk_sum[...] = jnp.zeros_like(dk_sum)
    dv_sum[...] = jnp.zeros_like(dv_sum)

    def block(i, carry):
        at = pl.ds(pl.multiple_of(i * shard_len, shard_len), shard_len)
        queries, grad = q_ref[at, :], grad_all[at, :]
        product = grad.astype(jnp.float32) * mixed_all[at, :].astype(jnp.float32)
        parts = []
        for h in range(width // HEAD):
            cols = slice(h * HEAD, (h + 1) * HEAD)
            head_q, head_grad = queries[:, cols], grad[:, cols]
            scores = dot_right_t(head_q * SCORE_SCALE, k_ref[:, cols]) + masked
            probs = jnp.exp(scores - lse_ref[at, h : h + 1])
            delta = jnp.sum(product[:, cols], axis=1, keepdims=True)
            grad_probs = dot_right_t(head_grad, v_ref[:, cols])
            grad_scores = (probs * (grad_probs - delta)).astype(jnp.bfloat16)
            parts.append(
                jnp.dot(grad_scores, k_ref[:, cols], preferred_element_type=jnp.float32)
                * SCORE_SCALE
            )
            dk_sum[cols, :] += jnp.dot(head_q.T, grad_scores, preferred_element_type=jnp.float32)
            dv_sum[cols, :] += jnp.dot(
                head_grad.T, probs.astype(jnp.bfloat16), preferred_element_type=jnp.float32
            )
        all_ref[at, :width] = jnp.concatenate(parts, axis=1).astype(jnp.bfloat16)
        return carry

    lax.fori_loop(0, count, block, 0)
    all_ref[:, width : 2 * width] = (dk_sum[...].T * SCORE_SCALE).astype(jnp.bfloat16)
    all_ref[:, 2 * width :] = dv_sum[...].T.astype(jnp.bfloat16)
    sums_ref[...] = jnp.zeros_like(sums_ref)
    sums_ref[:1, :] = jnp.sum(all_ref[...].astype(jnp.float32), axis=0, keepdims=True)

    def part_of(at):
        part = dot_right_t(all_ref[at, :width], weight_refs[0][...])
        part = part + dot_right_t(all_ref[at, width : 2 * width], weight_refs[1][...])
        return part + dot_right_t(all_ref[at, 2 * width :], weight_refs[2][...])

    def other(i, carry):
        at = pl.ds(pl.multiple_of(i * shard_len, shard_len), shard_len)
        part_all[at, :] = part_of(at).astype(jnp.bfloat16)
        return carry

    part_refs[0][...] = part_of(slice(0, shard_len))
    lax.fori_loop(1, count, other, 0)
    for i in range(1, count):
        part_refs[i][...] = part_all[i * shard_len : (i + 1) * shard_len, :]


def attend_back(
    place, length, queries, keys_all, values_all, lse, mixed_pieces, grad_pieces, weights
):
    rows, width = queries.shape
    shard_len, model_width = mixed_pieces[0].shape[0], weights[0].shape[0]
    smem, vmem = pl.BlockSpec(memory_space=pltpu.SMEM), pl.BlockSpec(memory_space=pltpu.VMEM)
    arrays = (queries, keys_all, values_all, lse, *mixed_pieces, *grad_pieces, *weights)
    parts = [jax.ShapeDtypeStruct((shard_len, model_width), jnp.float32)] + [
        jax.ShapeDtypeStruct((shard_len, model_width), jnp.bfloat16)
    ] * (len(mixed_pieces) - 1)
    return pl.pallas_call(
        attend_back_kernel,
        out_shape=(
            jax.ShapeDtypeStruct((rows, 3 * width), jnp.bfloat16),
            jax.ShapeDtypeStruct((16, 3 * width), jnp.float32),
            *parts,
        ),
        in_specs=[smem, smem] + [vmem] * len(arrays),
        out_specs=(vmem,) * (2 + len(parts)),
        scratch_shapes=[pltpu.VMEM((width, rows), jnp.float32)] * 2
        + [pltpu.VMEM((rows, width), jnp.bfloat16)] * 2
        + [pltpu.VMEM((rows, model_width), jnp.bfloat16)],
        compiler_params=pltpu.CompilerParams(vmem_limit_bytes=48 << 20),
        cost_estimate=pl.CostEstimate(
            flops=20 * rows * width * rows,
            bytes_accessed=8 << 20,
            transcendentals=rows * rows * (width // HEAD),
        ),
        name="attend_back",
    )(place.reshape(1), length.reshape(1), *arrays)


def vector_kernel(
    place_ref, one_ref, two_ref, resid_ref, normed_one_ref, normed_two_ref, cot_ref, pre_ref, out_ref
):
    seq_count, _, head_width = out_ref.shape
    model_width = one_ref.shape[1]
    resid = resid_ref[...]
    cot = cot_ref[...].astype(jnp.float32)
    rows = [
        one_ref[...],
        two_ref[...],
        resid * normed_one_ref[...],
        resid,
        cot * normed_two_ref[...],
        cot,
    ]
    out_ref[...] = jnp.zeros_like(out_ref)
    for k, values in enumerate(rows):
        total = jnp.sum(values, axis=0, keepdims=True)
        for j in range(seq_count):
            out_ref[j, 2 + k : 3 + k, :] = total[:, j * head_width : (j + 1) * head_width]
    pre = pre_ref[...].astype(jnp.float32)
    per_place = pre.shape[1] // seq_count // model_width
    totals = [
        jnp.sum(pre[:, k * model_width : (k + 1) * model_width], axis=0, keepdims=True)
        for k in range(seq_count * per_place)
    ]
    for k in range(seq_count):
        owner = place_ref[0] ^ k
        for i in range(per_place):
            row = 8 + owner * per_place + i
            total = totals[k * per_place + i]
            for j in range(seq_count):
                out_ref[j, pl.ds(row, 1), :] = total[:, j * head_width : (j + 1) * head_width]


def vector_sums(place, seq_count, head_width, *arrays):
    return pl.pallas_call(
        vector_kernel,
        out_shape=jax.ShapeDtypeStruct((seq_count, 16, head_width), jnp.float32),
        in_specs=[pl.BlockSpec(memory_space=pltpu.SMEM)]
        + [pl.BlockSpec(memory_space=pltpu.VMEM)] * len(arrays),
        out_specs=pl.BlockSpec(memory_space=pltpu.VMEM),
        compiler_params=pltpu.CompilerParams(vmem_limit_bytes=32 << 20),
        name="vector_sums",
    )(place.reshape(1), *arrays)


def layer(
    tokens,
    cotangent,
    lengths,
    w_attn,
    attn_first,
    attn_second,
    w_ffn,
    ffn_first,
    ffn_second,
    vectors,
    vec_first,
    vec_second,
):
    bf16, f32 = jnp.bfloat16, jnp.float32
    _, shard_len, model_width = tokens.shape
    seq_count, fsdp_count = lax.axis_size("seq"), lax.axis_size("fsdp")
    place, member = lax.axis_index("seq"), lax.axis_index("fsdp")
    _, row_shard, head_width = w_attn.shape
    hidden_shard = w_ffn.shape[2]
    vec_rows, vec_shard = vectors.shape
    token_rows = tokens.reshape(shard_len, model_width)
    cot_half = cotangent.reshape(shard_len, model_width)
    cot_rows = cot_half.astype(f32)
    bits = list(range(fsdp_count.bit_length() - 1))

    own_shard = jnp.concatenate([w_ffn[0], w_ffn[1], w_attn[3]], axis=1).astype(bf16)
    vec_placed = lax.dynamic_update_slice(
        jnp.zeros((16, head_width), bf16), vectors.astype(bf16), (0, member * vec_shard)
    )
    qkv_shard = jnp.concatenate(
        [w_attn[:3].astype(bf16).reshape(3 * row_shard, head_width), vec_placed], axis=0
    )
    own_all = lax.all_gather(own_shard, "fsdp", axis=0, tiled=True)
    weight_pieces = gather_across(own_shard)[1:]
    token_pieces = gather_across(token_rows)
    qkv_all = lax.all_gather(qkv_shard, "fsdp", axis=0, tiled=False)
    w_qkv = [
        qkv_all[:, i * row_shard : (i + 1) * row_shard].reshape(model_width, head_width)
        for i in range(3)
    ]
    vec_own = jnp.sum(qkv_all[:, 3 * row_shard :].astype(f32), axis=0)[:vec_rows]
    vec_half = vec_own.astype(bf16)
    weight_pieces[-1] = after(weight_pieces[-1], qkv_all)
    cuts = (0, hidden_shard, 2 * hidden_shard, 2 * hidden_shard + head_width)
    rest_cat = jnp.concatenate(
        [
            piece[:, low:high]
            for low, high in zip(cuts[:-1], cuts[1:], strict=True)
            for piece in weight_pieces
        ],
        axis=1,
    )
    rest_all = lax.all_gather(rest_cat, "fsdp", axis=0, tiled=True)
    up_parts, down_parts, out_parts = (
        [own_all[:, low:high], rest_all[:, low * (seq_count - 1) : high * (seq_count - 1)]]
        for low, high in zip(cuts[:-1], cuts[1:], strict=True)
    )

    def times(left, parts):
        return jnp.concatenate(
            [jnp.dot(left, part, preferred_element_type=f32) for part in parts], axis=1
        )

    def times_t(left, parts):
        width = parts[0].shape[1]
        return dot_right_t(left[:, :width], parts[0]) + dot_right_t(left[:, width:], parts[1])

    vec_near = [piece.astype(f32) for piece in swap_across([vec_half] * seq_count)]

    def near(order):
        return sum(jnp.where(order == r, piece, 0.0) for r, piece in enumerate(vec_near))

    vec_wide = jnp.concatenate(
        [near(place ^ j) for j in range(seq_count)], axis=1
    )
    up_bias = turn_blocks(vec_wide[8:12].reshape(seq_count, hidden_shard)).reshape(-1)

    valid_len = lengths[0]
    queries, keys_all, values_all, lse, *mixed_pieces = attend(
        place, valid_len, vec_own[:2], token_pieces, w_qkv
    )
    mixed_rows = jnp.concatenate(swap_across(mixed_pieces), axis=1)

    hidden_one = token_rows.astype(f32) + times_t(mixed_rows, out_parts) + vec_wide[2]
    normed_one, inv_one = layer_norm(hidden_one)
    resid_one = normed_one * vec_wide[4] + vec_wide[5]
    resid_half = resid_one.astype(bf16)
    preact = times(resid_half, up_parts) + up_bias
    activation, gelu_slope = gelu_pair(preact)
    act_half = activation.astype(bf16)
    hidden_two = resid_one + times_t(act_half, down_parts) + vec_wide[3]
    normed_two, inv_two = layer_norm(hidden_two)
    block_out = (normed_two * vec_wide[6] + vec_wide[7]).astype(bf16)
    grad_two = norm_back(cot_rows * vec_wide[6], normed_two, inv_two)
    grad_two_half = grad_two.astype(bf16)

    def outer(left, right):
        return lax.dot_general(
            left, right, (((0,), (0,)), ((), ())), preferred_element_type=f32
        ).astype(bf16)

    down_local, grad_two_half = lax.optimization_barrier(
        (outer(grad_two_half, act_half), grad_two_half)
    )
    down_part = lax.psum_scatter(down_local, "fsdp", scatter_dimension=0, tiled=True)
    grad_pre_half = (times(grad_two_half, down_parts) * gelu_slope).astype(bf16)
    up_kept, up_sent = halving(
        outer(resid_half, grad_pre_half).reshape(fsdp_count, row_shard, -1), bits[0], True
    )
    up_sent, up_kept, grad_pre_half = lax.optimization_barrier((up_sent, up_kept, grad_pre_half))
    up_received = swapped(up_sent, bits[0])
    grad_resid = grad_two + times_t(grad_pre_half, up_parts)
    grad_one = norm_back(grad_resid * vec_wide[4], normed_one, inv_one)
    grad_one_half = grad_one.astype(bf16)
    grad_mixed = times(grad_one_half, out_parts).astype(bf16)
    grad_pieces = swap_across(jnp.split(grad_mixed, seq_count, axis=1))

    out_kept, out_sent = halving(
        outer(after(grad_one_half, grad_mixed), mixed_rows).reshape(fsdp_count, row_shard, -1),
        bits[0],
        True,
    )
    out_received = swapped(out_sent, bits[0])
    vec_blocks = vector_sums(
        place,
        seq_count,
        head_width,
        grad_one,
        grad_two,
        grad_resid,
        normed_one,
        normed_two,
        cot_half,
        grad_pre_half,
    )
    vec_order = turn_blocks(vec_blocks)
    vec_moved = swap_across([vec_order[r] for r in range(seq_count)])
    up_wide = joined(up_kept, up_received)
    out_wide = joined(out_kept, out_received)
    near_places = seq_count // 2
    up_cut, out_cut = near_places * hidden_shard, near_places * head_width
    wide = [
        jnp.concatenate([up_wide[..., :up_cut], out_wide[..., :out_cut]], axis=-1),
        jnp.concatenate([up_wide[..., up_cut:], out_wide[..., out_cut:]], axis=-1),
    ]
    routes = [list(bits[1:]), list(reversed(bits[1:]))]
    wide_moving = []
    for half, route, low in zip(wide, routes, (True, False), strict=True):
        kept, sent = halving(half, route[0], low)
        wide_moving.append((kept, swapped(sent, route[0])))
        grad_pieces = after(grad_pieces, sent)

    grad_qkv, head_sums, input_own, *input_parts = attend_back(
        place,
        valid_len,
        queries,
        keys_all,
        values_all,
        lse,
        mixed_pieces,
        grad_pieces,
        w_qkv,
    )
    input_totals = sum_first([input_own, *input_parts])
    input_terms = None
    vec_part = sum(after(vec_moved, input_own))
    vec_lines = jnp.concatenate(
        [head_sums[:1, :head_width], head_sums[:1, 2 * head_width :], vec_part[2:]], axis=0
    )
    vec_lines = jnp.pad(vec_lines, ((0, 0), (0, 2 * head_width)))
    token_all = jnp.concatenate(token_pieces, axis=0)
    qkv_local = lax.dot_general(
        token_all, grad_qkv, (((0,), (0,)), ((), ())), preferred_element_type=f32
    ).astype(bf16)
    qkv_blocks = jnp.concatenate(
        [
            qkv_local.reshape(fsdp_count, row_shard, 3 * head_width),
            jnp.broadcast_to(
                vec_lines.astype(bf16)[None], (fsdp_count, 16, 3 * head_width)
            ),
        ],
        axis=1,
    )

    def place_pieces(half, count):
        ups, outs = half[:, : count * hidden_shard], half[:, count * hidden_shard :]
        return [
            jnp.concatenate(
                [
                    ups[:, r * hidden_shard : (r + 1) * hidden_shard],
                    outs[:, r * head_width : (r + 1) * head_width],
                ],
                axis=1,
            )
            for r in range(count)
        ]

    qkv_kept, qkv_sent = halving(qkv_blocks, bits[0], True)
    qkv_received = swapped(qkv_sent, bits[0])
    step = qkv_sent
    down_moved = None
    for at in range(1, len(bits)):
        moving = []
        for (kept, received), route, low in zip(wide_moving, routes, (True, False), strict=True):
            half = joined(kept, after(received, step))
            if at < len(bits) - 1:
                kept, sent = halving(half, route[at], low)
                moving.append((kept, swapped(sent, route[at])))
                step = sent
            else:
                moving.append(half[0])
        wide_moving = moving
        if input_terms is None:
            input_totals = {
                r: terms[:1] + after(terms[1:], step) for r, terms in input_totals.items()
            }
            input_terms = sum_rest(input_totals, seq_count)
        if down_moved is None:
            down_pieces = jnp.split(after(down_part, step), seq_count, axis=1)
            down_moved = sum_across(down_pieces)
            step = down_pieces
    wide_pieces = place_pieces(wide_moving[0], near_places) + place_pieces(
        wide_moving[1], seq_count - near_places
    )
    wide_sent = [piece.astype(bf16) for piece in wide_pieces[1:]]
    wide_moved = sum_across([wide_pieces[0]] + wide_sent)
    step = wide_sent
    for bit in bits[1:]:
        qkv_half = joined(qkv_kept, after(qkv_received, step))
        qkv_kept, qkv_sent = halving(qkv_half, bit, True)
        qkv_received = swapped(qkv_sent, bit)
        step = qkv_sent
    qkv_sum = joined(qkv_kept, qkv_received)[0]
    input_grad = grad_one + total_of(input_terms[:1] + after(input_terms[1:], qkv_sum))
    down_sum = total_of(down_moved[:1] + after(down_moved[1:], input_grad))
    up_out_sum = total_of(wide_moved[:1] + after(wide_moved[1:], down_sum))

    token_total = shard_len * seq_count * fsdp_count
    grad_scale = float(token_total) ** (-0.5)
    attn_grad = grad_scale * with_layout_constraint(
        jnp.stack(
            [
                qkv_sum[:row_shard, i * head_width : (i + 1) * head_width]
                for i in range(3)
            ]
            + [up_out_sum[:, hidden_shard:]]
        ),
        Layout(major_to_minor=(0, 1, 2)),
    )
    ffn_grad = grad_scale * jnp.stack([up_out_sum[:, :hidden_shard], down_sum])
    vec_grad = grad_scale * lax.dynamic_slice(
        qkv_sum[row_shard:], (0, member * vec_shard), (vec_rows, vec_shard)
    )
    attn_new, attn_one, attn_two = adam_step(
        w_attn, attn_grad, attn_first, attn_second, WEIGHT_DECAY
    )
    ffn_new, ffn_one, ffn_two = adam_step(w_ffn, ffn_grad, ffn_first, ffn_second, WEIGHT_DECAY)
    vec_new, vec_one, vec_two = adam_step(vectors, vec_grad, vec_first, vec_second, 0.0)
    return (
        block_out.reshape(tokens.shape),
        input_grad.reshape(tokens.shape),
        attn_grad,
        ffn_grad,
        vec_grad,
        attn_new,
        attn_one,
        attn_two,
        ffn_new,
        ffn_one,
        ffn_two,
        vec_new,
        vec_one,
        vec_two,
    )


def solution(mesh):
    placed = (
        P("fsdp", "seq", None),
        P("fsdp", "seq", None),
        P("fsdp"),
        P(None, "fsdp", "seq"),
        P(None, "fsdp", "seq"),
        P(None, "fsdp", "seq"),
        P(None, "fsdp", "seq"),
        P(None, "fsdp", "seq"),
        P(None, "fsdp", "seq"),
        P(None, ("seq", "fsdp")),
        P(None, ("seq", "fsdp")),
        P(None, ("seq", "fsdp")),
    )
    return jax.shard_map(
        layer,
        mesh=mesh,
        in_specs=placed,
        out_specs=(
            P("fsdp", "seq", None),
            P("fsdp", "seq", None),
            P(None, "fsdp", "seq"),
            P(None, "fsdp", "seq"),
            P(None, ("seq", "fsdp")),
            P(None, "fsdp", "seq"),
            P(None, "fsdp", "seq"),
            P(None, "fsdp", "seq"),
            P(None, "fsdp", "seq"),
            P(None, "fsdp", "seq"),
            P(None, "fsdp", "seq"),
            P(None, ("seq", "fsdp")),
            P(None, ("seq", "fsdp")),
            P(None, ("seq", "fsdp")),
        ),
        check_vma=False,
    )
```
